32 devices in a mesh: groups: 2 (over y), samples: 8 (over z, x), genome: 2 (over core).
Axes of the slice: x: 2, y: 2, z: 4, core: 2. Of those that a mesh axis runs over, the one named last changes fastest.
Arguments:
- genotypes: bfloat16 [16384, 1536], P(('groups', 'samples'), 'genome'), parts along dimension 0, may hold values from 0 to 2
- chromosome: int32 [3072], P('groups'), parts along dimension 0, may hold values from 1 to 3, as said below
- blocks: int32 [3072], P('groups'), parts along dimension 0, may hold values from 0 to 199, never falling along the last dimension, each value on 1 to 16 neighbouring positions
- annotation: int32 [97, 3072], P(None, 'groups'), parts along dimension 1, may hold values 0 or 1
- reach: int32 [3072], P('groups'), parts along dimension 0, may hold values from 384 to 768
Outputs:
- ld_scores: float32 [97, 3072], P(None, ('groups', 'genome')), parts along dimension 1
- block_sums: float32 [97, 400], P(None, 'groups'), parts along dimension 1
The draws below stay inside these ranges and needn't reach their ends.
There are 2 independent parts, one for each index of `groups`. The reference program is written for one: setup_inputs(seed, part) draws one part's arguments, and reference() takes and returns one part's arrays. A program takes and returns all parts, laid end to end along the dimension named above; each array names one. Nothing has to cross between parts.
Inputs may be any that keep to these rules, and one draw needn't show every extreme that they name: chromosome ids never fall along the window and rise by one at each of 2 boundaries.
All inputs are finite; a program needn't handle non-finite values.
Results may differ from the reference program's by a relative error of at most 0.0015.
Values may be sent and summed in bfloat16 or wider, within the bound.
No kernel may reach another device: no remote copies, remote signals or barrier semaphores. Data moves between devices by JAX's collectives and lax.ppermute only.
A program may use at most 64 MiB of HBM per device.

```python
import math
import jax
import jax.numpy as jnp
import numpy as np
from jax import lax

BAND = 768
ANNOT = 97
MS = 768
NBLK = 200
SAMPLES = 8192
SNPS = 1536
N_GENOME = 2


founder_count = 16


def linkage_map(key):
    subkeys = jax.random.split(key, 5)
    position = jnp.arange(SNPS, dtype=jnp.int32)
    region_len = MS // 4
    region_count = (SNPS + region_len - 1) // region_len
    decay_len = jax.random.randint(subkeys[0], (region_count,), BAND // 4, BAND + 1)
    base_rate = 65536 // jnp.take(decay_len, position // region_len)
    hot_count = max(2, SNPS // 64)
    hot_place = jax.random.randint(subkeys[1], (hot_count,), 0, SNPS)
    hot_rate = jax.random.randint(subkeys[2], (hot_count,), 13107, 32769)
    hot_hit = jnp.max(jnp.where(position[:, None] == hot_place[None, :], hot_rate[None, :], 0), axis=1)
    switch_rate = jnp.maximum(base_rate, hot_hit).astype(jnp.int32)
    freq_cut = jax.random.randint(subkeys[3], (SNPS,), 200, 501)
    alleles = (jax.random.randint(subkeys[4], (founder_count, SNPS), 0, 1000) < freq_cut[None, :]).astype(jnp.int32)
    founder_row = jnp.arange(founder_count, dtype=jnp.int32)[:, None]
    alleles = jnp.where(founder_row == position[None, :] % founder_count, 1, alleles)
    alleles = jnp.where(founder_row == (position[None, :] + 5) % founder_count, 0, alleles)
    return (switch_rate, alleles)


def haplotype_alleles(key, alleles, switch_rate):
    subkeys = jax.random.split(key, 3)
    position = jnp.arange(SNPS, dtype=jnp.int32)
    sample_pos = jnp.arange(SAMPLES, dtype=jnp.int32)
    group_cut = 205 + 614 * sample_pos // SAMPLES
    switched = jax.random.randint(subkeys[0], (SAMPLES, SNPS), 0, 65536) < switch_rate[None, :]
    switched = jnp.logical_or(switched, position[None, :] == 0)
    segment_start = lax.cummax(jnp.where(switched, position[None, :], 0), axis=1)
    group_pick = (jax.random.randint(subkeys[1], (SAMPLES, SNPS), 0, 1024) < group_cut[:, None]).astype(jnp.int32)
    member = jax.random.randint(subkeys[2], (SAMPLES, SNPS), 0, founder_count // 2)
    founder_table = group_pick * (founder_count // 2) + member
    founder = jnp.take_along_axis(founder_table, segment_start, axis=1)
    return alleles[founder, position[None, :]]


def draw_genotypes(key, part):
    switch_rate, alleles = linkage_map(jax.random.fold_in(key, 11))
    first_bits = haplotype_alleles(jax.random.fold_in(key, 12), alleles, switch_rate)
    second_bits = haplotype_alleles(jax.random.fold_in(key, 13), alleles, switch_rate)
    noise_keys = jax.random.split(jax.random.fold_in(key, 14), 2)
    fraction = jnp.arange(SAMPLES).astype(jnp.float32) / SAMPLES
    first_miss = (0.04 + 0.2 * fraction[:, None]) * jax.nn.sigmoid(jax.random.normal(noise_keys[0], (SAMPLES, SNPS), jnp.float32) - 1.0)
    second_miss = (0.04 + 0.2 * fraction[:, None]) * jax.nn.sigmoid(jax.random.normal(noise_keys[1], (SAMPLES, SNPS), jnp.float32) - 1.0)
    first_prob = jnp.where(first_bits == 1, 1.0 - first_miss, first_miss)
    second_prob = jnp.where(second_bits == 1, 1.0 - second_miss, second_miss)
    return (first_prob + second_prob).astype(jnp.bfloat16)


def draw_chromosome(key, part):
    offsets = jax.random.randint(key, (N_GENOME,), MS // 4, MS // 2)
    boundary = jnp.arange(N_GENOME) * MS + offsets
    position = jnp.arange(SNPS)
    return (1 + jnp.sum((position[:, None] >= boundary[None, :]).astype(jnp.int32), axis=1)).astype(jnp.int32)


def draw_reach(key, part):
    values_r = jax.random.randint(key, (SNPS,), BAND // 2, BAND + 1)
    return values_r.at[0].set(BAND).at[1].set(BAND // 2).astype(jnp.int32)


def touch_ends(entries, stream_key, least, high):
    longest = entries.shape.index(max(entries.shape))
    spots = []
    for shift in (0, 1):
        where = [jax.random.randint(jax.random.fold_in(stream_key, axis), (), 0, length) for axis, length in enumerate(entries.shape)]
        where[longest] = (where[longest] + shift) % entries.shape[longest]
        spots.append(tuple(where))
    return entries.at[spots[0]].set(least).at[spots[1]].set(high)


def length_profile(amount, total, most, slope):
    loads = [(1 << 20) // math.isqrt(rank ** slope) + 1 for rank in range(2, amount + 1)]
    rest, counts = total - most - (amount - 1), [1] * (amount - 1)
    while rest > 0:
        free = [i for i in range(amount - 1) if counts[i] < most]
        pool, budget = sum([loads[i] for i in free]), rest
        for i in free:
            extra = min(most - counts[i], max(1, budget * loads[i] // pool), rest)
            counts[i] = counts[i] + extra
            rest = rest - extra
    return np.array([most] + counts)


def uneven(rng, amount, total, most, skew):
    if amount == 2:
        one = jax.random.randint(rng, (), max(1, total - most), min(most, total - 1) + 1)
        return jnp.stack([one, total - one])
    lengths = jnp.asarray(length_profile(amount, total, most, skew), jnp.int32)
    couples = (amount - 1) // 2
    giver, taker = lengths[1:1 + 2 * couples:2], lengths[2:2 + 2 * couples:2]
    room = jnp.minimum(giver - 1, most - taker)
    passed = jax.random.randint(jax.random.fold_in(rng, 1), (couples,), 0, 1 << 20) % (room + 1)
    lengths = lengths.at[1:1 + 2 * couples:2].set(giver - passed).at[2:2 + 2 * couples:2].set(taker + passed)
    return lengths[jax.random.permutation(jax.random.fold_in(rng, 2), amount)]


def setup_inputs(seed: int = 0, part: int = 0) -> dict:
    seeds = jax.random.split(jax.random.key(seed), 6)
    part_splits = jax.random.split(jax.random.fold_in(seeds[5], part), 6)
    return {
        "genotypes": draw_genotypes(jax.random.fold_in(jax.random.fold_in(seeds[5], part), 71), part),
        "chromosome": draw_chromosome(jax.random.fold_in(jax.random.fold_in(seeds[5], part), 71), part),
        "blocks": jnp.searchsorted(jnp.cumsum(uneven(part_splits[2], NBLK, SNPS, 2 * SNPS // NBLK + 1, 1)), jnp.arange(SNPS), side="right").astype(jnp.int32),
        "annotation": touch_ends((jax.random.randint(part_splits[3], (ANNOT, SNPS), 0, 3) < 1).astype(jnp.int32), jax.random.fold_in(part_splits[3], 1), 0, 1),
        "reach": draw_reach(jax.random.fold_in(jax.random.fold_in(seeds[5], part), 71), part),
    }


VAR_EPS = 1e-06

def reference(genotypes, chromosome, blocks, annotation, reach):
    samples_all = float(SAMPLES)
    snp_total = SNPS
    band_len = BAND
    values_f = genotypes.astype(jnp.float32)
    col_means = lax.optimization_barrier(jnp.sum(values_f, 0)) / samples_all
    variance = lax.optimization_barrier(jnp.sum(values_f * values_f, 0)) / samples_all - col_means * col_means + VAR_EPS
    scales = jnp.sqrt(variance)
    padded_geno = jnp.pad(genotypes, ((0, 0), (0, band_len)))
    means_pad = jnp.pad(col_means, (0, band_len))
    scales_pad = jnp.pad(scales, (0, band_len), constant_values=1.0)
    chrom_pad = jnp.pad(chromosome, (0, band_len), constant_values=-1)
    annot = annotation.astype(jnp.float32)
    annot_pad = jnp.pad(annot, ((0, 0), (0, band_len)))
    block_rows = 256 if snp_total % 256 == 0 else snp_total
    col_span = block_rows + band_len
    scores = jnp.zeros((ANNOT, snp_total + band_len), jnp.float32)
    for row_start in range(0, snp_total, block_rows):
        left_cols = padded_geno[:, row_start:row_start + block_rows]
        right_cols = padded_geno[:, row_start:row_start + col_span]
        product = lax.dot_general(left_cols, right_cols, (((0,), (0,)), ((), ())), preferred_element_type=jnp.float32)
        mean_rows = col_means[row_start:row_start + block_rows]
        mean_cols = means_pad[row_start:row_start + col_span]
        scale_rows = scales[row_start:row_start + block_rows]
        scale_cols = scales_pad[row_start:row_start + col_span]
        correl = (product / samples_all - mean_rows[:, None] * mean_cols[None, :]) / (scale_rows[:, None] * scale_cols[None, :])
        squared = correl * correl
        unbiased = squared - (1.0 - squared) / (samples_all - 2.0)
        offsets = jnp.arange(col_span)[None, :] - jnp.arange(block_rows)[:, None]
        col_index = row_start + jnp.arange(col_span)
        reach_rows = reach[row_start:row_start + block_rows]
        chrom_rows = chromosome[row_start:row_start + block_rows]
        chrom_cols = chrom_pad[row_start:row_start + col_span]
        allowed = (offsets >= 1) & (offsets <= reach_rows[:, None]) & (col_index[None, :] < snp_total) & (chrom_rows[:, None] == chrom_cols[None, :])
        weights = jnp.where(allowed, unbiased, 0.0)
        annot_rows = annot_pad[:, row_start:row_start + block_rows]
        annot_cols = annot_pad[:, row_start:row_start + col_span]
        forward = lax.dot_general(annot_cols, weights, (((1,), (1,)), ((), ())), precision=lax.Precision.HIGHEST)
        backward = jnp.dot(annot_rows, weights, precision=lax.Precision.HIGHEST)
        scores = scores.at[:, row_start:row_start + col_span].add(backward)
        scores = scores.at[:, row_start:row_start + block_rows].add(forward)
    ld_scores = annot + scores[:, :snp_total]
    onehot = (blocks[None, :] == jnp.arange(NBLK)[:, None]).astype(jnp.float32)
    block_sums = lax.dot_general(ld_scores, onehot, (((1,), (1,)), ((), ())), precision=lax.Precision.HIGHEST)
    return (ld_scores, block_sums)
```

```python
import functools
import math

import jax
import jax.numpy as jnp
from jax import lax
from jax.experimental import pallas as pl
from jax.experimental.pallas import tpu as pltpu
from jax.sharding import PartitionSpec as P

NBLK = 200
VAR_EPS = 1e-06
F32 = jnp.float32
BF16 = jnp.bfloat16
STAT_ROWS = 8
VMEM_LIMIT = 48 * 1024 * 1024


def pick(first, one, other):
    return jnp.where(first, one, other)


def col_parts(vec, first, half):
    left, right, there = vec[:, :half], vec[:, half : 2 * half], vec[:, 2 * half :]
    a_cols = pick(first, left, there)
    b_cols = pick(first, there, right)
    a_rolled = pltpu.roll(a_cols, half // 2, 1)
    b3_cols = pick(first, pltpu.roll(there, half // 2, 1), left)
    return left, right, b_cols, a_rolled, b3_cols


def row_parts(ref, core, start, count, half):
    def at(offset):
        rows = ref[pl.ds(pl.multiple_of(offset + start, 16), count), :]
        return jnp.concatenate([rows] * (half // 128), axis=1)

    left, right = at(0), at(half)
    a_rows = at(2 * half * core)
    a2_rows = at(half + half * core)
    b_rows = at(2 * half + half // 2 - half * core)
    return left, right, a_rows, a2_rows, b_rows


def index_parts(start, count, half):
    row = lax.broadcasted_iota(jnp.int32, (count, half), 0) + start
    col = lax.broadcasted_iota(jnp.int32, (count, half), 1)
    return row, col


def pair_products(rows, cols, row, col, half):
    left, right, a_rows, a2_rows, b_rows = rows
    c_left, c_right, c_b, c_a, c_b3 = cols
    fold = col < half // 2
    one = left * c_right
    two = jnp.where(row < col, left * c_left, jnp.where(row > col, right * c_right, a_rows * c_b))
    three = jnp.where(fold, jnp.where(row > col, a_rows * c_b, b_rows * c_a), a2_rows * c_b3)
    return one, two, three


def to_column(vec_row, ref, width):
    tall = jnp.broadcast_to(vec_row, (128, width))
    for k in range(width // 128):
        ref[k * 128 : (k + 1) * 128, :] = tall[:, k * 128 : (k + 1) * 128].T
    rest = ref.shape[0] - width
    ref[width:, :] = jnp.zeros((rest, 128), F32)


def coded(stats):
    high = stats.astype(BF16)
    left = stats - high.astype(F32)
    middle = left.astype(BF16)
    low = (left - middle.astype(F32)).astype(BF16)
    return jnp.concatenate([high[:2], middle[:2], low[:2], high[:2]], axis=0)


def decoded(rows):
    parts = rows.astype(F32)
    return parts[0:2] + parts[2:4] + parts[4:6]


def dot_tt(left, right):
    return lax.dot_general(left, right, (((0,), (0,)), ((), ())), preferred_element_type=F32)


def gram_kernel(pos_ref, own_ref, there_ref, keep_ref, send_ref, stats_ref, full_ref, col_ref):
    half = own_ref.shape[1] // 2
    count = own_ref.shape[0]
    width = 3 * half
    core = pos_ref[0]
    first = core == 0
    left, right, there = own_ref[:, :half], own_ref[:, half:], there_ref[...]
    ones = jnp.ones((8, count), BF16)
    sums = jnp.concatenate(
        [
            lax.dot_general(ones, x, (((1,), (0,)), ((), ())), preferred_element_type=F32)[:1]
            for x in (left, right, there)
        ],
        axis=1,
    )
    squares = []
    for ref, lo in ((own_ref, 0), (own_ref, half), (there_ref, 0)):
        total = jnp.zeros((8, half), F32)
        for k in range(0, count, 64):
            part = ref[k : k + 64, lo : lo + half].astype(F32)
            total = total + jnp.sum((part * part).reshape(8, 8, half), axis=0)
        squares.append(jnp.sum(total, axis=0, keepdims=True))
    squares = jnp.concatenate(squares, axis=1)
    shift = sums * (1.0 / math.sqrt(count))
    stats = jnp.concatenate([sums, squares - shift * shift], axis=0)
    stats_ref[...] = jnp.concatenate([stats] * 4, axis=0)
    to_column(shift, col_ref, width)
    full_ref[:, :half] = dot_tt(left, right)
    row, col = index_parts(0, half, half)
    full_ref[:, half : 2 * half] = jnp.where(row < col, dot_tt(left, left), dot_tt(right, right))

    def cross(a_cols, b_cols, a2_cols, b3_cols, turn):
        straight = dot_tt(a_cols, b_cols)
        full_ref[:, half : 2 * half] = jnp.where(row == col, straight, full_ref[:, half : 2 * half])
        folded = pltpu.roll(dot_tt(b_cols[:, half // 2 :], a_cols), half // 2, 1)
        folded = jnp.concatenate([folded, folded], axis=0)
        apart = dot_tt(a2_cols, b3_cols)
        if turn:
            apart = pltpu.roll(apart, half // 2, 1)
        full_ref[:, 2 * half :] = jnp.where(
            col < half // 2, jnp.where(row > col, straight, folded), apart
        )

    @pl.when(first)
    def _():
        cross(left, there, right, there, True)

    @pl.when(jnp.logical_not(first))
    def _():
        cross(there, right, there, left, False)

    cols = col_parts(jnp.broadcast_to(shift, (8, width)), first, half)
    cols = tuple(x[:1] for x in cols)
    step = 48
    bit = pos_ref[1]

    def centred(start):
        rows = row_parts(col_ref, core, start, step, half)
        products = pair_products(rows, cols, *index_parts(start, step, half), half)
        return full_ref[pl.ds(start, step), :] - jnp.concatenate(products, axis=1)

    part = keep_ref.shape[0]
    for k in range(0, part, step):
        keep_ref[k : k + step, :] = centred(pl.multiple_of(bit * part + k, 16))
        send_ref[k : k + step, :] = centred(pl.multiple_of((1 - bit) * part + k, 16)).astype(BF16)
    send_ref[part:, :] = coded(stats)


def merged_stats(msg_ref, stats_ref, rows, samples):
    theirs = decoded(msg_ref[rows:, :])
    mine = stats_ref[:2, :]
    shift = (mine[:1] - theirs[:1]) * (1.0 / math.sqrt(2.0 * samples))
    total = mine + theirs
    total = jnp.concatenate([total[:1], total[1:] + shift * shift], axis=0)
    return shift, total


def merge_kernel(pos_ref, kept_ref, msg_ref, stats_ref, keep_ref, send_ref, out_ref, col_ref, *, samples, split):
    rows, width = kept_ref.shape
    half = width // 3
    core = pos_ref[0]
    shift, total = merged_stats(msg_ref, stats_ref, rows, samples)
    out_ref[...] = jnp.concatenate([total] * 4, axis=0)
    to_column(shift, col_ref, width)
    cols = col_parts(jnp.broadcast_to(shift, (8, width)), core == 0, half)
    cols = tuple(x[:1] for x in cols)
    base, bit = pos_ref[2], pos_ref[1]
    step = 48

    def added(offset):
        start = base + offset
        part = row_parts(col_ref, core, start, step, half)
        products = pair_products(part, cols, *index_parts(start, step, half), half)
        here = pl.ds(offset, step)
        return kept_ref[here, :] + msg_ref[here, :].astype(F32) + jnp.concatenate(products, axis=1)

    out_rows = keep_ref.shape[0]
    for k in range(0, out_rows, step):
        if split:
            keep_ref[k : k + step, :] = added(pl.multiple_of(bit * out_rows + k, 16))
            send_ref[k : k + step, :] = added(pl.multiple_of((1 - bit) * out_rows + k, 16)).astype(BF16)
        else:
            rounded = added(k).astype(BF16)
            keep_ref[k : k + step, :] = rounded.astype(F32)
            send_ref[k : k + step, :] = rounded
    send_ref[out_rows:, :] = coded(total)


def weight_kernel(pos_ref, kept_ref, msg_ref, stats_ref, limit_ref, out_ref, col_ref, scale_ref, lim_ref, *, samples):
    rows, width = kept_ref.shape
    half = width // 3
    core = pos_ref[0]
    first = core == 0
    everyone = 2.0 * samples
    shift, total = merged_stats(msg_ref, stats_ref, rows, samples)
    scale = 1.0 / jnp.sqrt(total[1:] * (1.0 / everyone) + VAR_EPS)
    limit = limit_ref[:1, :]
    to_column(shift, col_ref, width)
    to_column(scale * (1.0 / everyone), scale_ref, width)
    to_column(limit, lim_ref, width)

    def cols_of(vec):
        return tuple(x[:1] for x in col_parts(jnp.broadcast_to(vec, (8, width)), first, half))

    cols, scales, limits = cols_of(shift), cols_of(scale), cols_of(limit)
    base = pos_ref[2]
    step = 48
    for k in range(0, rows, step):
        start = base + k
        row, col = index_parts(start, step, half)
        fold = col < half // 2
        products = pair_products(row_parts(col_ref, core, start, step, half), cols, row, col, half)
        norms = pair_products(row_parts(scale_ref, core, start, step, half), scales, row, col, half)
        l_left, _, l_a, l_a2, _ = row_parts(lim_ref, core, start, step, half)
        apart = jnp.abs(row - col)
        two_lim = jnp.where(row < col, l_left, jnp.where(row > col, limits[1], l_a))
        three_lim = jnp.where(fold, jnp.where(row > col, l_a, limits[3]), l_a2)
        two_gap = jnp.where(row == col, 2 * half, apart)
        three_gap = jnp.where(
            fold,
            jnp.where(row == col, 4 * half, 2 * half - apart),
            half - half // 2 + (half // 2) * core + col - row,
        )
        gaps = (half + col - row, two_gap, three_gap)
        lims = (l_left, two_lim, three_lim)
        for s in range(3):
            here = slice(s * half, (s + 1) * half)
            value = kept_ref[k : k + step, here] + msg_ref[k : k + step, here].astype(F32) + products[s]
            correl = value * norms[s]
            squared = correl * correl
            unbiased = squared - (1.0 - squared) * (1.0 / (everyone - 2.0))
            out_ref[k : k + step, here] = jnp.where(gaps[s].astype(F32) <= lims[s], unbiased, 0.0).astype(BF16)


def dot_n(left, right):
    return lax.dot_general(left, right, (((1,), (0,)), ((), ())), preferred_element_type=F32)


def dot_t(left, right):
    return lax.dot_general(left, right, (((1,), (1,)), ((), ())), preferred_element_type=F32)


def onehot_sums(scores, onehot):
    high = scores.astype(BF16)
    left = scores - high.astype(F32)
    middle = left.astype(BF16)
    low = (left - middle.astype(F32)).astype(BF16)
    return dot_n(high, onehot) + dot_n(middle, onehot) + dot_n(low, onehot)


def score_kernel(pos_ref, mine_ref, theirs_ref, annot_ref, hot_ref, own_ref, msg_ref, w_ref):
    part, width = mine_ref.shape
    half = width // 3
    quarter = half // 2
    core = pos_ref[0]
    bit = pos_ref[1]
    w_ref[pl.ds(pl.multiple_of(bit * part, 16), part), :] = mine_ref[...]
    w_ref[pl.ds(pl.multiple_of((1 - bit) * part, 16), part), :] = theirs_ref[...]
    row, col = index_parts(0, half, half)
    zero = jnp.zeros((half, half), BF16)
    one = w_ref[:, :half]
    two = w_ref[:, half : 2 * half]
    three = w_ref[:, 2 * half :]
    a_left, a_right, a_there = annot_ref[:, :half], annot_ref[:, half : 2 * half], annot_ref[:, 2 * half :]
    upper = jnp.where(row < col, two, zero)
    lower = jnp.where(row > col, two, zero)
    diag = jnp.sum(jnp.where(row == col, two, zero).astype(F32), axis=0, keepdims=True)
    fold = col < quarter
    straight = jnp.where(fold & (row > col), three, zero)
    folded = jnp.where(fold & (row < col), three, zero)[:quarter]
    apart = jnp.where(fold, zero, three)
    out_left = dot_t(a_right, one) + dot_n(a_left, upper) + dot_t(a_left, upper) + a_left.astype(F32)
    out_right = dot_n(a_left, one) + dot_n(a_right, lower) + dot_t(a_right, lower) + a_right.astype(F32)
    wide = jnp.zeros((annot_ref.shape[0], half), BF16)
    lane = lax.broadcasted_iota(jnp.int32, wide.shape, 1)

    def turned(x):
        return pltpu.roll(x, quarter, 1)

    def cross(a_cols, b_cols, a2_cols, b3_cols):
        late_b = turned(b_cols.astype(F32)).astype(BF16)[:, :quarter]
        late_a = turned(jnp.where(lane < quarter, 0.0, a_cols.astype(F32))).astype(BF16)
        out_a = dot_t(b_cols, straight) + turned(dot_n(late_b, folded)) + b_cols.astype(F32) * diag
        back = jnp.concatenate([dot_t(late_a, folded), jnp.zeros((wide.shape[0], quarter), F32)], axis=1)
        out_b = dot_n(a_cols, straight) + turned(back) + a_cols.astype(F32) * diag
        out_a2 = dot_t(b3_cols, apart)
        out_b3 = dot_n(a2_cols, apart)
        return out_a, out_b, out_a2, out_b3

    def finish(own_left, own_right, other):
        own_ref[:, :half] = own_left
        own_ref[:, half:] = own_right
        msg_ref[:, :half] = other
        msg_ref[:, half:] = (
            onehot_sums(own_left, hot_ref[:half, :])
            + onehot_sums(own_right, hot_ref[half : 2 * half, :])
            + onehot_sums(other, hot_ref[2 * half :, :])
        )

    @pl.when(core == 0)
    def _():
        b3_cols = turned(a_there.astype(F32)).astype(BF16)
        out_a, out_b, out_a2, out_b3 = cross(a_left, a_there, a_right, b3_cols)
        finish(out_left + out_a, out_right + out_a2, out_b + turned(out_b3))

    @pl.when(core != 0)
    def _():
        out_a, out_b, out_a2, out_b3 = cross(a_there, a_right, a_there, a_left)
        finish(out_left + out_b3, out_right + out_b, out_a + out_a2)


def call(kernel, inputs, outputs, scratch, flops, moved):
    vmem = pl.BlockSpec(memory_space=pltpu.VMEM)
    smem = pl.BlockSpec(memory_space=pltpu.SMEM)
    return pl.pallas_call(
        kernel,
        out_shape=outputs,
        in_specs=[smem] + [vmem] * (len(inputs) - 1),
        out_specs=jax.tree.map(lambda _: vmem, outputs),
        scratch_shapes=scratch,
        compiler_params=pltpu.CompilerParams(vmem_limit_bytes=VMEM_LIMIT),
        cost_estimate=pl.CostEstimate(flops=flops, bytes_accessed=moved, transcendentals=0),
    )(*inputs)


def body(genotypes, chromosome, blocks, annotation, reach):
    count, slab = genotypes.shape
    half = slab // 2
    width = 3 * half
    snps = chromosome.shape[0]
    parts = lax.axis_size("samples")
    bits = parts.bit_length() - 1
    core = lax.axis_index("genome")
    place = lax.axis_index("samples")
    order = [list(range(bits)) for _ in range(2)]
    if bits > 1:
        order[1][0], order[1][1] = 1, 0
    splits = min(bits, 3)
    bit_at = [(place >> jnp.where(core == 0, order[0][t], order[1][t])) & 1 for t in range(bits)]

    def exchange(x, t):
        route = []
        for s in range(parts):
            for g in range(2):
                route.append((s * 2 + g, (s ^ (1 << order[g][t])) * 2 + g))
        return lax.ppermute(x, ("samples", "genome"), route)

    def across(x):
        return lax.ppermute(x, "genome", [(0, 1), (1, 0)])

    def scalars(*values):
        return jnp.stack([jnp.asarray(v, jnp.int32) for v in values])

    def shape(rows, cols, dtype):
        return jax.ShapeDtypeStruct((rows, cols), dtype)

    there = across(lax.dynamic_slice_in_dim(genotypes, (1 - core) * half, half, 1))

    first_col = core * slab
    there_col = (1 - core) * slab + core * half

    def local(x):
        axis = x.ndim - 1
        return jnp.concatenate(
            [
                lax.dynamic_slice_in_dim(x, first_col, slab, axis),
                lax.dynamic_slice_in_dim(x, there_col, half, axis),
            ],
            axis=axis,
        )

    ends = jnp.sum((chromosome[None, :] <= jnp.arange(1, 4)[:, None]).astype(jnp.int32), axis=1)
    last = jnp.where(chromosome == 1, ends[0], jnp.where(chromosome == 2, ends[1], ends[2]))
    limit = local(jnp.minimum(reach, last - 1 - jnp.arange(snps))).astype(F32)
    limit = jnp.broadcast_to(limit[None, :], (8, width))
    annot = annotation.shape[0]
    annot_rows = -(-annot // 16) * 16
    flags = jnp.pad(local(annotation).astype(BF16), ((0, annot_rows - annot), (0, 0)))
    hot_cols = -(-NBLK // 128) * 128
    hot = (local(blocks)[:, None] == jnp.arange(hot_cols)[None, :]).astype(BF16)

    columns = pltpu.VMEM((width + half // 2, 128), F32)
    rows = half // 2
    keep, send, stats = call(
        gram_kernel,
        (scalars(core, bit_at[0]), genotypes, there),
        (shape(rows, width, F32), shape(rows + STAT_ROWS, width, BF16), shape(8, width, F32)),
        [pltpu.VMEM((half, width), F32), columns],
        2 * count * half * half * 6,
        count * width * 2,
    )
    base = bit_at[0] * rows
    samples = count
    for t in range(1, bits):
        msg = exchange(send, t - 1)
        split = t < splits
        new_rows = rows // 2 if split else rows
        keep, send, stats = call(
            functools.partial(merge_kernel, samples=float(samples), split=split),
            (scalars(core, bit_at[t], base), keep, msg, stats),
            (shape(new_rows, width, F32), shape(new_rows + STAT_ROWS, width, BF16), shape(8, width, F32)),
            [columns],
            rows * width * 8,
            rows * width * 12,
        )
        if split:
            base = base + bit_at[t] * new_rows
        rows = new_rows
        samples = 2 * samples
    msg = exchange(send, bits - 1)
    weights = call(
        functools.partial(weight_kernel, samples=float(samples)),
        (scalars(core, 0, base), keep, msg, stats, limit),
        shape(rows, width, BF16),
        [columns, columns, columns],
        rows * width * 30,
        rows * width * 8,
    )
    for t in range(splits - 1, 0, -1):
        other = exchange(weights, t)
        weights = jnp.where(
            bit_at[t] == 0,
            jnp.concatenate([weights, other], axis=0),
            jnp.concatenate([other, weights], axis=0),
        )
    other = exchange(weights, 0)
    own, msg = call(
        score_kernel,
        (scalars(core, bit_at[0]), weights, other, flags, hot),
        (shape(annot_rows, slab, F32), shape(annot_rows, half + hot_cols, F32)),
        [pltpu.VMEM((half, width), BF16)],
        2 * annot_rows * half * half * 12,
        half * width * 2,
    )
    carried = across(msg)
    arrived = carried[:annot, :half]
    nothing = jnp.zeros_like(arrived)
    ld_scores = own[:annot] + jnp.where(
        core == 0,
        jnp.concatenate([nothing, arrived], axis=1),
        jnp.concatenate([arrived, nothing], axis=1),
    )
    block_sums = msg[:annot, half : half + NBLK] + carried[:annot, half : half + NBLK]
    return (ld_scores, block_sums)


def solution(mesh):
    placed = (
        P(("groups", "samples"), "genome"),
        P("groups"),
        P("groups"),
        P(None, "groups"),
        P("groups"),
    )
    return jax.shard_map(
        body,
        mesh=mesh,
        in_specs=placed,
        out_specs=(P(None, ("groups", "genome")), P(None, "groups")),
        check_vma=False,
    )
```

```python
import functools
import math

import jax
import jax.numpy as jnp
from jax import lax
from jax.experimental import pallas as pl
from jax.experimental.pallas import tpu as pltpu
from jax.sharding import PartitionSpec as P

NBLK = 200
VAR_EPS = 1e-06
F32 = jnp.float32
BF16 = jnp.bfloat16
CORE_ONE_ORDER = [1, 2, 0]
VMEM_LIMIT = 48 * 1024 * 1024


STEP = 48


def pick(first, one, other):
    return jnp.where(first, one, other)


def wide_rows(ref, offset, count, half):
    rows = ref[pl.ds(pl.multiple_of(offset, 16), count), :]
    return jnp.concatenate([rows] * (half // 128), axis=1)


def index_parts(start, count, half):
    row = lax.broadcasted_iota(jnp.int32, (count, half), 0) + start
    col = lax.broadcasted_iota(jnp.int32, (count, half), 1)
    return row, col


def to_column(vec_row, ref):
    width = vec_row.shape[1]
    tall = jnp.broadcast_to(vec_row, (128, width))
    for k in range(width // 128):
        ref[k * 128 : (k + 1) * 128, :] = tall[:, k * 128 : (k + 1) * 128].T
    rest = ref.shape[0] - width
    if rest:
        ref[width:, :] = jnp.zeros((rest, 128), F32)


def coded(stats):
    high = stats.astype(BF16)
    left = stats - high.astype(F32)
    middle = left.astype(BF16)
    low = (left - middle.astype(F32)).astype(BF16)
    blank = jnp.zeros((stats.shape[0] * 8 // 2 - 3 * stats.shape[0], stats.shape[1]), BF16)
    return jnp.concatenate([high, middle, low, blank], axis=0)


def decoded(rows, count):
    parts = rows.astype(F32)
    return parts[:count] + parts[count : 2 * count] + parts[2 * count : 3 * count]


def own_cols(vec, half):
    return vec[:, :half], vec[:, half : 2 * half]


def own_products(ref, cols, start, row, col):
    count, half = row.shape
    left, right = cols
    l_rows = wide_rows(ref, start, count, half)
    r_rows = wide_rows(ref, start + half, count, half)
    return l_rows * right, jnp.where(row < col, l_rows * left, r_rows * right)


def cross_halves(vec, first, half):
    left, right, there = vec[:, :half], vec[:, half : 2 * half], vec[:, 2 * half :]
    return pick(first, left, there), pick(first, there, right)


def cross_cols(vec, first, half):
    vec = jnp.broadcast_to(vec, (8, vec.shape[1]))
    a_cols, b_cols = cross_halves(vec, first, half)
    a_turned = pltpu.roll(a_cols, half // 2, 1)
    b3_cols = pick(first, pltpu.roll(vec[:, 2 * half :], half // 2, 1), vec[:, :half])
    return b_cols[:1], a_turned[:1], b3_cols[:1]


def cross_products(ref, cols, core, start, row, col):
    count, half = row.shape
    c_b, c_a, c_b3 = cols
    a_rows = wide_rows(ref, start + 2 * half * core, count, half)
    a2_rows = wide_rows(ref, start + half + half * core, count, half)
    b_rows = wide_rows(ref, start + 2 * half + half // 2 - half * core, count, half)
    return jnp.where(
        col < half // 2, jnp.where(row > col, a_rows * c_b, b_rows * c_a), a2_rows * c_b3
    )


def dot_tt(left, right):
    return lax.dot_general(left, right, (((0,), (0,)), ((), ())), preferred_element_type=F32)


def dot_n(left, right):
    return lax.dot_general(left, right, (((1,), (0,)), ((), ())), preferred_element_type=F32)


def dot_t(left, right):
    return lax.dot_general(left, right, (((1,), (1,)), ((), ())), preferred_element_type=F32)


def moments(ref):
    count, width = ref.shape
    sums = dot_n(jnp.ones((8, count), BF16), ref[...])[:1]
    total = jnp.zeros((8, width), F32)
    for k in range(0, count, 64):
        part = ref[k : k + 64, :].astype(F32)
        total = total + jnp.sum((part * part).reshape(8, 8, width), axis=0)
    shift = sums * (1.0 / math.sqrt(count))
    return sums, jnp.sum(total, axis=0, keepdims=True) - shift * shift, shift


def eight(*rows):
    return jnp.concatenate(list(rows) + [rows[-1]] * (8 - len(rows)), axis=0)


def halved(pos_ref, keep_ref, send_ref, value):
    part = keep_ref.shape[0]
    bit = pos_ref[1]
    for k in range(0, part, STEP):
        send_ref[k : k + STEP, :] = value(pl.multiple_of((1 - bit) * part + k, 16)).astype(BF16)
        keep_ref[k : k + STEP, :] = value(pl.multiple_of(bit * part + k, 16))


def own_gram_kernel(pos_ref, own_ref, keep_ref, send_ref, stats_ref, full_ref, col_ref):
    half = own_ref.shape[1] // 2
    left, right = own_ref[:, :half], own_ref[:, half:]
    sums, squares, shift = moments(own_ref)
    stats_ref[...] = eight(sums, squares, shift)
    to_column(shift, col_ref)
    full_ref[:, :half] = dot_tt(left, right)
    row, col = index_parts(0, half, half)
    full_ref[:, half:] = jnp.where(row < col, dot_tt(left, left), dot_tt(right, right))
    cols = own_cols(shift, half)

    def value(start):
        products = own_products(col_ref, cols, start, *index_parts(start, STEP, half))
        return full_ref[pl.ds(start, STEP), :] - jnp.concatenate(products, axis=1)

    halved(pos_ref, keep_ref, send_ref, value)
    send_ref[keep_ref.shape[0] :, :] = coded(jnp.concatenate([sums, squares], axis=0))


def cross_gram_kernel(pos_ref, own_ref, there_ref, own_stats_ref, keep_ref, send_ref, stats_ref, full_ref, col_ref):
    half = there_ref.shape[1]
    core = pos_ref[0]
    first = core == 0
    left, right, there = own_ref[:, :half], own_ref[:, half:], there_ref[...]
    sums, squares, shift = moments(there_ref)
    shift = jnp.concatenate([own_stats_ref[2:3, :], shift], axis=1)
    to_column(shift, col_ref)
    row, col = index_parts(0, half, half)
    a_shift, b_shift = cross_halves(shift, first, half)

    def cross(a_cols, b_cols, a2_cols, b3_cols, turn):
        straight = dot_tt(a_cols, b_cols)
        level = jnp.sum(jnp.where(row == col, straight, 0.0), axis=0, keepdims=True)
        stats = jnp.concatenate([sums, squares, level - a_shift * b_shift], axis=0)
        stats_ref[...] = eight(stats[0:1], stats[1:2], stats[2:3])
        send_ref[keep_ref.shape[0] :, :] = coded(jnp.concatenate([stats, stats[2:3]], axis=0))
        folded = pltpu.roll(dot_tt(b_cols[:, half // 2 :], a_cols), half // 2, 1)
        folded = jnp.concatenate([folded, folded], axis=0)
        apart = dot_tt(a2_cols, b3_cols)
        if turn:
            apart = pltpu.roll(apart, half // 2, 1)
        full_ref[...] = jnp.where(col < half // 2, jnp.where(row > col, straight, folded), apart)

    @pl.when(first)
    def _():
        cross(left, there, right, there, True)

    @pl.when(jnp.logical_not(first))
    def _():
        cross(there, right, there, left, False)

    cols = cross_cols(shift, first, half)

    def value(start):
        products = cross_products(col_ref, cols, core, start, *index_parts(start, STEP, half))
        return full_ref[pl.ds(start, STEP), :] - products

    halved(pos_ref, keep_ref, send_ref, value)


def own_merged(msg_ref, stats_ref, rows, samples):
    theirs = decoded(msg_ref[rows:, :], 2)
    sums, squares = stats_ref[:1, :], stats_ref[1:2, :]
    shift = (sums - theirs[:1]) * (1.0 / math.sqrt(2.0 * samples))
    return sums + theirs[:1], squares + theirs[1:2] + shift * shift, shift


def cross_merged(msg_ref, stats_ref, own_shift, rows, samples, first):
    half = stats_ref.shape[1]
    theirs = decoded(msg_ref[rows:, :], 4)
    sums, squares, level = stats_ref[:1, :], stats_ref[1:2, :], stats_ref[2:3, :]
    shift = (sums - theirs[:1]) * (1.0 / math.sqrt(2.0 * samples))
    both = jnp.concatenate([own_shift, shift], axis=1)
    a_shift, b_shift = cross_halves(both, first, half)
    return (
        sums + theirs[:1],
        squares + theirs[1:2] + shift * shift,
        (level + theirs[2:3]) + a_shift * b_shift,
        both,
    )


def passed_on(pos_ref, keep_ref, send_ref, value, split):
    if split:
        halved(pos_ref, keep_ref, send_ref, value)
        return keep_ref.shape[0]
    rows = send_ref.shape[0] // STEP * STEP
    for k in range(0, rows, STEP):
        send_ref[k : k + STEP, :] = value(k).astype(BF16)
    return rows


def own_merge_kernel(pos_ref, kept_ref, msg_ref, stats_ref, *refs, samples, split):
    keep_ref = refs[0] if split else None
    send_ref, out_ref, col_ref = refs[-3:]
    rows = kept_ref.shape[0] // STEP * STEP
    half = kept_ref.shape[1] // 2
    sums, squares, shift = own_merged(msg_ref, stats_ref, rows, samples)
    out_ref[...] = eight(sums, squares, shift)
    to_column(shift, col_ref)
    cols = own_cols(shift, half)
    base = pos_ref[2]

    def value(offset):
        start = base + offset
        products = own_products(col_ref, cols, start, *index_parts(start, STEP, half))
        here = pl.ds(offset, STEP)
        both = kept_ref[here, :].astype(F32) + msg_ref[here, :].astype(F32)
        return both + jnp.concatenate(products, axis=1)

    done = passed_on(pos_ref, keep_ref, send_ref, value, split)
    send_ref[done:, :] = coded(jnp.concatenate([sums, squares], axis=0))


def cross_merge_kernel(pos_ref, kept_ref, msg_ref, stats_ref, own_ref, *refs, samples, split):
    keep_ref = refs[0] if split else None
    send_ref, out_ref, col_ref = refs[-3:]
    rows = kept_ref.shape[0] // STEP * STEP
    half = kept_ref.shape[1]
    core = pos_ref[0]
    first = core == 0
    sums, squares, level, shift = cross_merged(msg_ref, stats_ref, own_ref[2:3, :], rows, samples, first)
    out_ref[...] = eight(sums, squares, level)
    to_column(shift, col_ref)
    cols = cross_cols(shift, first, half)
    base = pos_ref[2]

    def value(offset):
        start = base + offset
        products = cross_products(col_ref, cols, core, start, *index_parts(start, STEP, half))
        here = pl.ds(offset, STEP)
        return kept_ref[here, :].astype(F32) + msg_ref[here, :].astype(F32) + products

    done = passed_on(pos_ref, keep_ref, send_ref, value, split)
    send_ref[done:, :] = coded(jnp.concatenate([sums, squares, level, level], axis=0))


def unbiased(correl, everyone):
    squared = correl * correl
    return squared - (1.0 - squared) * (1.0 / (everyone - 2.0))


def placed_at(rows_part, offset, half):
    blank = jnp.zeros((rows_part.shape[0], half - rows_part.shape[1]), F32)
    return pltpu.roll(jnp.concatenate([rows_part, blank], axis=1), offset, 1)


def own_score_kernel(
    pos_ref, kept_ref, msg_ref, stats_ref, limit_ref, flag_ref, sub_ref,
    out_ref, vec_ref, col_ref, scale_ref, lim_ref, one_ref, two_ref, *, samples,
):
    rows = one_ref.shape[0]
    half = kept_ref.shape[1] // 2
    everyone = 2.0 * samples
    _, squares, shift = own_merged(msg_ref, stats_ref, rows, samples)
    scale = 1.0 / jnp.sqrt(squares * (1.0 / everyone) + VAR_EPS)
    vec_ref[...] = eight(shift, scale)
    to_column(shift, col_ref)
    to_column(scale * (1.0 / everyone), scale_ref)
    to_column(limit_ref[:1, : 2 * half], lim_ref)
    cols, scales = own_cols(shift, half), own_cols(scale, half)
    right_lim = limit_ref[:1, half : 2 * half]
    base = pos_ref[2]
    for k in range(0, rows, STEP):
        start = base + k
        row, col = index_parts(start, STEP, half)
        products = own_products(col_ref, cols, start, row, col)
        norms = own_products(scale_ref, scales, start, row, col)
        left_lim = wide_rows(lim_ref, start, STEP, half)
        gaps = (half + col - row, jnp.where(row == col, 8 * half, jnp.abs(row - col)))
        lims = (left_lim, jnp.where(row < col, left_lim, right_lim))
        for s, ref in ((0, one_ref), (1, two_ref)):
            here = slice(s * half, (s + 1) * half)
            value = kept_ref[k : k + STEP, here].astype(F32) + msg_ref[k : k + STEP, here].astype(F32)
            weight = unbiased((value + products[s]) * norms[s], everyone)
            ref[k : k + STEP, :] = jnp.where(gaps[s].astype(F32) <= lims[s], weight, 0.0).astype(BF16)
    row, col = index_parts(base, rows, half)
    one, two = one_ref[...], two_ref[...]
    zero = jnp.zeros_like(two)
    upper, lower = jnp.where(row < col, two, zero), jnp.where(row > col, two, zero)
    f_left, f_right = flag_ref[:, :half], flag_ref[:, half : 2 * half]
    s_left, s_right = sub_ref[:, :rows], sub_ref[:, 128 : 128 + rows]
    out_ref[:, :half] = dot_n(s_left, upper) + placed_at(dot_t(f_right, one) + dot_t(f_left, upper), base, half)
    out_ref[:, half:] = dot_n(s_left, one) + dot_n(s_right, lower) + placed_at(dot_t(f_right, lower), base, half)


def cross_score_kernel(
    pos_ref, kept_ref, msg_ref, stats_ref, vec_ref, limit_ref, flag_ref, sub_ref, own_ref,
    out_ref, col_ref, scale_ref, lim_ref, three_ref, *, samples,
):
    rows = three_ref.shape[0]
    half = kept_ref.shape[1]
    quarter = half // 2
    core = pos_ref[0]
    first = core == 0
    everyone = 2.0 * samples
    _, squares, level, shift = cross_merged(msg_ref, stats_ref, vec_ref[:1, :], rows, samples, first)
    scale = 1.0 / jnp.sqrt(squares * (1.0 / everyone) + VAR_EPS)
    scale = jnp.concatenate([vec_ref[1:2, :], scale], axis=1)
    limit = limit_ref[:1, :]
    to_column(shift, col_ref)
    to_column(scale * (1.0 / everyone), scale_ref)
    to_column(limit, lim_ref)
    cols, scales = cross_cols(shift, first, half), cross_cols(scale, first, half)
    _, late_lim, _ = cross_cols(limit, first, half)
    base = pos_ref[2]
    for k in range(0, rows, STEP):
        start = base + k
        row, col = index_parts(start, STEP, half)
        fold = col < quarter
        products = cross_products(col_ref, cols, core, start, row, col)
        norms = cross_products(scale_ref, scales, core, start, row, col)
        a_lim = wide_rows(lim_ref, start + 2 * half * core, STEP, half)
        a2_lim = wide_rows(lim_ref, start + half + half * core, STEP, half)
        lims = jnp.where(fold, jnp.where(row > col, a_lim, late_lim), a2_lim)
        near = jnp.where(row == col, 8 * half, 2 * half - jnp.abs(row - col))
        gaps = jnp.where(fold, near, quarter + quarter * core + col - row)
        value = kept_ref[k : k + STEP, :].astype(F32) + msg_ref[k : k + STEP, :].astype(F32)
        weight = unbiased((value + products) * norms, everyone)
        three_ref[k : k + STEP, :] = jnp.where(gaps.astype(F32) <= lims, weight, 0.0).astype(BF16)
    a_scale, b_scale = cross_halves(scale, first, half)
    a_limit, _ = cross_halves(limit, first, half)
    lane = lax.broadcasted_iota(jnp.int32, (1, half), 1)
    level = unbiased(level * (1.0 / everyone) * a_scale * b_scale, everyone)
    mine = (lane >= base) & (lane < base + rows) & (a_limit >= 2.0 * half)
    level = jnp.where(mine, level, 0.0)
    row, col = index_parts(base, rows, half)
    three = three_ref[...]
    zero = jnp.zeros_like(three)
    fold = col < quarter
    straight = jnp.where(fold & (row > col), three, zero)
    folded = jnp.where(fold & (row < col), three, zero)
    apart = jnp.where(fold, zero, three)
    f_a, f_b = flag_ref[:, :half], flag_ref[:, half : 2 * half]
    f_late, f_b3 = flag_ref[:, 2 * half : 3 * half], flag_ref[:, 3 * half :]
    s_a, s_a2, s_late = sub_ref[:, 256 : 256 + rows], sub_ref[:, 384 : 384 + rows], sub_ref[:, 512 : 512 + rows]
    out_a = placed_at(dot_t(f_b, straight), base, half) + pltpu.roll(dot_n(s_late, folded), quarter, 1)
    out_b = dot_n(s_a, straight) + placed_at(dot_t(f_late, folded), lax.rem(base + quarter, half), half)
    out_a = out_a + f_b.astype(F32) * level
    out_b = out_b + f_a.astype(F32) * level
    out_a2 = placed_at(dot_t(f_b3, apart), base, half)
    out_b3 = dot_n(s_a2, apart)
    out_ref[:, :half] = own_ref[:, :half] + pick(first, out_a, out_b3)
    out_ref[:, half : 2 * half] = own_ref[:, half:] + pick(first, out_a2, out_b)
    out_ref[:, 2 * half :] = pick(first, out_b + pltpu.roll(out_b3, quarter, 1), out_a + out_a2)


def block_kernel(pos_ref, score_ref, flag_ref, hot_ref, own_ref, msg_ref, sum_ref):
    slab = own_ref.shape[1]
    own = score_ref[:, :slab] + flag_ref[:, :slab].astype(F32)
    other = score_ref[:, slab:]
    own_ref[...] = own
    msg_ref[...] = other
    scores = jnp.concatenate([own, other], axis=1)
    high = scores.astype(BF16)
    left = scores - high.astype(F32)
    middle = left.astype(BF16)
    low = (left - middle.astype(F32)).astype(BF16)
    hot = hot_ref[...]
    sum_ref[...] = dot_t(hot, high) + dot_t(hot, middle) + dot_t(hot, low)


def call(kernel, inputs, outputs, scratch, flops, moved):
    vmem = pl.BlockSpec(memory_space=pltpu.VMEM)
    smem = pl.BlockSpec(memory_space=pltpu.SMEM)
    return pl.pallas_call(
        kernel,
        out_shape=outputs,
        in_specs=[smem] + [vmem] * (len(inputs) - 1),
        out_specs=jax.tree.map(lambda _: vmem, outputs),
        scratch_shapes=scratch,
        compiler_params=pltpu.CompilerParams(vmem_limit_bytes=VMEM_LIMIT),
        cost_estimate=pl.CostEstimate(flops=flops, bytes_accessed=moved, transcendentals=0),
    )(*inputs)


def body(genotypes, chromosome, blocks, annotation, reach):
    count, slab = genotypes.shape
    half = slab // 2
    quarter = half // 2
    width = 3 * half
    snps = chromosome.shape[0]
    parts = lax.axis_size("samples")
    bits = parts.bit_length() - 1
    core = lax.axis_index("genome")
    place = lax.axis_index("samples")
    order = [list(range(bits)), CORE_ONE_ORDER + list(range(3, bits))]
    bit_at = [(place >> jnp.where(core == 0, order[0][t], order[1][t])) & 1 for t in range(bits)]

    def exchange(x, t):
        route = []
        for s in range(parts):
            for g in range(2):
                route.append((s * 2 + g, (s ^ (1 << order[g][t])) * 2 + g))
        return lax.ppermute(x, ("samples", "genome"), route)

    def across(x):
        return lax.ppermute(x, "genome", [(0, 1), (1, 0)])

    def scalars(*values):
        return jnp.stack([jnp.asarray(v, jnp.int32) for v in values])

    def shape(rows, cols, dtype):
        return jax.ShapeDtypeStruct((rows, cols), dtype)

    there = across(lax.dynamic_slice_in_dim(genotypes, (1 - core) * half, half, 1))
    base = bit_at[0] * quarter + bit_at[1] * (quarter // 2)
    rows = quarter // 2

    own_at = core * slab
    there_at = (1 - core) * slab + core * half
    a_at, b_at = core * half, slab + core * half
    b3_at = slab + core * quarter

    def local(x):
        axis = x.ndim - 1
        parts_of = [(own_at, slab), (there_at, half)]
        return jnp.concatenate([lax.dynamic_slice_in_dim(x, at, n, axis) for at, n in parts_of], axis=axis)

    ends = jnp.sum((chromosome[None, :] <= jnp.arange(1, 4)[:, None]).astype(jnp.int32), axis=1)
    last = jnp.where(chromosome == 1, ends[0], jnp.where(chromosome == 2, ends[1], ends[2]))
    limit = local(jnp.minimum(reach, last - 1 - jnp.arange(snps))).astype(F32)
    limit = jnp.broadcast_to(limit[None, :], (8, width))
    annot = annotation.shape[0]
    annot_rows = -(-annot // 16) * 16
    flags_all = jnp.pad(annotation.astype(BF16), ((0, annot_rows - annot), (0, 0)))

    def columns_of(at, n):
        return lax.dynamic_slice_in_dim(flags_all, at, n, 1)

    none = jnp.zeros((annot_rows, quarter), BF16)
    flags = local(flags_all)
    flags_cross = jnp.concatenate(
        [columns_of(a_at, half), columns_of(b_at, half), columns_of(a_at + quarter, quarter), none, none, columns_of(b3_at, quarter)],
        axis=1,
    )
    padded = jnp.pad(flags_all, ((0, 0), (0, slab)))
    starts = (own_at, own_at + half, a_at, half, b_at + quarter)
    subs = jnp.concatenate([lax.dynamic_slice_in_dim(padded, at + base, 128, 1) for at in starts], axis=1)
    hot_rows = -(-NBLK // 8) * 8
    hot = (jnp.arange(hot_rows)[:, None] == local(blocks)[None, :]).astype(BF16)

    own_column = pltpu.VMEM((slab, 128), F32)
    column = pltpu.VMEM((width + quarter, 128), F32)

    def outputs(kept, sent, cols, stat_rows):
        kept_shape = (shape(kept, cols, F32),) if kept else ()
        return kept_shape + (shape(sent + stat_rows, cols, BF16), shape(8, cols, F32))

    where = scalars(core, bit_at[0], 0)
    keep_a, send_a, stats_a = call(
        own_gram_kernel,
        (where, genotypes),
        outputs(quarter, quarter, slab, 8),
        [pltpu.VMEM((half, slab), F32), own_column],
        2 * count * half * half * 3,
        count * slab * 2,
    )
    msg_a = exchange(send_a, 0)
    keep_b, send_b, stats_b = call(
        cross_gram_kernel,
        (where, genotypes, there, stats_a),
        outputs(quarter, quarter, half, 16),
        [pltpu.VMEM((half, half), F32), column],
        2 * count * half * half * 3,
        count * slab * 2,
    )
    msg_b = exchange(send_b, 0)
    samples = float(count)
    for t in range(1, bits):
        split = t == 1
        where = scalars(core, bit_at[t], bit_at[0] * quarter if split else base)
        *kept_a, send_a, stats_a = call(
            functools.partial(own_merge_kernel, samples=samples, split=split),
            (where, keep_a, msg_a, stats_a),
            outputs(rows if split else 0, rows, slab, 8),
            [own_column],
            rows * slab * 8,
            rows * slab * 20,
        )
        msg_a = exchange(send_a, t)
        *kept_b, send_b, stats_b = call(
            functools.partial(cross_merge_kernel, samples=samples, split=split),
            (where, keep_b, msg_b, stats_b, stats_a),
            outputs(rows if split else 0, rows, half, 16),
            [column],
            rows * half * 8,
            rows * half * 20,
        )
        msg_b = exchange(send_b, t)
        keep_a = kept_a[0] if split else send_a
        keep_b = kept_b[0] if split else send_b
        samples = 2 * samples
    where = scalars(core, 0, base)
    scores_a, vectors = call(
        functools.partial(own_score_kernel, samples=samples),
        (where, keep_a, msg_a, stats_a, limit, flags, subs),
        (shape(annot_rows, slab, F32), shape(8, slab, F32)),
        [own_column] * 3 + [pltpu.VMEM((rows, half), BF16)] * 2,
        2 * annot_rows * half * rows * 8,
        rows * slab * 20,
    )
    partial = call(
        functools.partial(cross_score_kernel, samples=samples),
        (where, keep_b, msg_b, stats_b, vectors, limit, flags_cross, subs, scores_a),
        shape(annot_rows, width, F32),
        [column] * 3 + [pltpu.VMEM((rows, half), BF16)],
        2 * annot_rows * half * rows * 8,
        rows * slab * 20,
    )
    partial = partial[:annot]
    for t in (1, 0):
        rounded = partial.astype(jnp.float16)
        partial = rounded.astype(F32) + exchange(rounded, t).astype(F32)
    own, other, sums = call(
        block_kernel,
        (where, partial, flags[:annot], hot),
        (shape(annot, slab, F32), shape(annot, half, F32), shape(hot_rows, annot, F32)),
        [],
        2 * annot * width * hot_rows * 3,
        annot * width * 8,
    )
    arrived, sums_there = across(other), across(sums)
    nothing = jnp.zeros_like(arrived)
    ld_scores = own + jnp.where(
        core == 0,
        jnp.concatenate([nothing, arrived], axis=1),
        jnp.concatenate([arrived, nothing], axis=1),
    )
    return (ld_scores, (sums + sums_there)[:NBLK].T)


def solution(mesh):
    placed = (
        P(("groups", "samples"), "genome"),
        P("groups"),
        P("groups"),
        P(None, "groups"),
        P("groups"),
    )
    return jax.shard_map(
        body,
        mesh=mesh,
        in_specs=placed,
        out_specs=(P(None, ("groups", "genome")), P(None, "groups")),
        check_vma=False,
    )
```

```python
import functools
import math

import jax
import jax.numpy as jnp
from jax import lax
from jax.experimental import pallas as pl
from jax.experimental.pallas import tpu as pltpu
from jax.sharding import PartitionSpec as P

NBLK = 200
VAR_EPS = 1e-06
F32 = jnp.float32
BF16 = jnp.bfloat16
CORE_ONE_ORDER = [1, 2, 0]
VMEM_LIMIT = 20 * 1024 * 1024


STEP = 48


def pick(first, one, other):
    return jnp.where(first, one, other)


def wide_rows(ref, offset, count, half):
    rows = ref[pl.ds(pl.multiple_of(offset, 16), count), :]
    return jnp.concatenate([rows] * (half // 128), axis=1)


def index_parts(start, count, half):
    row = lax.broadcasted_iota(jnp.int32, (count, half), 0) + start
    col = lax.broadcasted_iota(jnp.int32, (count, half), 1)
    return row, col


def to_column(vec_row, ref):
    width = vec_row.shape[1]
    tall = jnp.broadcast_to(vec_row, (128, width))
    for k in range(width // 128):
        ref[k * 128 : (k + 1) * 128, :] = tall[:, k * 128 : (k + 1) * 128].T
    rest = ref.shape[0] - width
    if rest:
        ref[width:, :] = jnp.zeros((rest, 128), F32)


def coded(stats):
    high = stats.astype(BF16)
    left = stats - high.astype(F32)
    middle = left.astype(BF16)
    low = (left - middle.astype(F32)).astype(BF16)
    blank = jnp.zeros((stats.shape[0] * 8 // 2 - 3 * stats.shape[0], stats.shape[1]), BF16)
    return jnp.concatenate([high, middle, low, blank], axis=0)


def decoded(rows, count):
    parts = rows.astype(F32)
    return parts[:count] + parts[count : 2 * count] + parts[2 * count : 3 * count]


def own_cols(vec, half):
    return vec[:, :half], vec[:, half : 2 * half]


def own_products(ref, cols, start, row, col):
    count, half = row.shape
    left, right = cols
    l_rows = wide_rows(ref, start, count, half)
    r_rows = wide_rows(ref, start + half, count, half)
    return l_rows * right, jnp.where(row < col, l_rows * left, r_rows * right)


def cross_halves(vec, first, half):
    left, right, there = vec[:, :half], vec[:, half : 2 * half], vec[:, 2 * half :]
    return pick(first, left, there), pick(first, there, right)


def cross_cols(vec, first, half):
    vec = jnp.broadcast_to(vec, (8, vec.shape[1]))
    a_cols, b_cols = cross_halves(vec, first, half)
    a_turned = pltpu.roll(a_cols, half // 2, 1)
    b3_cols = pick(first, pltpu.roll(vec[:, 2 * half :], half // 2, 1), vec[:, :half])
    return b_cols[:1], a_turned[:1], b3_cols[:1]


def cross_products(ref, cols, core, start, row, col):
    count, half = row.shape
    c_b, c_a, c_b3 = cols
    a_rows = wide_rows(ref, start + 2 * half * core, count, half)
    a2_rows = wide_rows(ref, start + half + half * core, count, half)
    b_rows = wide_rows(ref, start + 2 * half + half // 2 - half * core, count, half)
    return jnp.where(
        col < half // 2, jnp.where(row > col, a_rows * c_b, b_rows * c_a), a2_rows * c_b3
    )


def dot_n(left, right):
    return lax.dot_general(left, right, (((1,), (0,)), ((), ())), preferred_element_type=F32)


def dot_t(left, right):
    return lax.dot_general(left, right, (((1,), (1,)), ((), ())), preferred_element_type=F32)


def moments(ref):
    count, width = ref.shape
    sums = dot_n(jnp.ones((8, count), BF16), ref[...])[:1]
    total = jnp.zeros((8, width), F32)
    for k in range(0, count, 64):
        part = ref[k : k + 64, :].astype(F32)
        total = total + jnp.sum((part * part).reshape(8, 8, width), axis=0)
    shift = sums * (1.0 / math.sqrt(count))
    return sums, jnp.sum(total, axis=0, keepdims=True) - shift * shift, shift


def eight(*rows):
    return jnp.concatenate(list(rows) + [rows[-1]] * (8 - len(rows)), axis=0)


def halved(bit, keep_ref, send_ref, value):
    part = keep_ref.shape[0]
    for k in range(0, part, STEP):
        send_ref[k : k + STEP, :] = value(pl.multiple_of((1 - bit) * part + k, 16)).astype(BF16)
        keep_ref[k : k + STEP, :] = value(pl.multiple_of(bit * part + k, 16))


def own_gram_kernel(pos_ref, own_ref, keep_ref, send_ref, stats_ref, turned_ref, piece_ref, full_ref, col_ref):
    half = own_ref.shape[1] // 2

    @pl.when(pos_ref[0] == 0)
    def _():
        piece_ref[...] = own_ref[:, half:]

    @pl.when(pos_ref[0] != 0)
    def _():
        piece_ref[...] = own_ref[:, :half]

    turned_ref[...] = own_ref[...].T
    sums, squares, shift = moments(own_ref)
    stats_ref[...] = eight(sums, squares, shift)
    to_column(shift, col_ref)
    left, right = turned_ref[:half, :], turned_ref[half:, :]
    full_ref[:, :half] = dot_n(left, own_ref[:, half:])
    row, col = index_parts(0, half, half)
    full_ref[:, half:] = jnp.where(row < col, dot_n(left, own_ref[:, :half]), dot_n(right, own_ref[:, half:]))
    cols = own_cols(shift, half)

    def value(start):
        products = own_products(col_ref, cols, start, *index_parts(start, STEP, half))
        return full_ref[pl.ds(start, STEP), :] - jnp.concatenate(products, axis=1)

    halved(pos_ref[1], keep_ref, send_ref, value)
    send_ref[keep_ref.shape[0] :, :] = coded(jnp.concatenate([sums, squares], axis=0))


def cross_gram_kernel(pos_ref, turned_ref, there_ref, own_stats_ref, keep_ref, send_ref, stats_ref, full_ref, col_ref, side_ref):
    half = there_ref.shape[1]
    quarter = half // 2
    core = pos_ref[0]
    first = core == 0
    row, col = index_parts(0, half, half)

    @pl.when(first)
    def _():
        full_ref[:, :half] = dot_n(turned_ref[:half, :], there_ref[...])
        full_ref[:, half:] = pltpu.roll(dot_n(turned_ref[half:, :], there_ref[...]), quarter, 1)

    @pl.when(jnp.logical_not(first))
    def _():
        side_ref[...] = there_ref[...].T
        full_ref[:, :half] = dot_t(side_ref[...], turned_ref[half:, :])
        full_ref[:, half:] = dot_t(side_ref[...], turned_ref[:half, :])

    sums, squares, shift = moments(there_ref)
    shift = jnp.concatenate([own_stats_ref[2:3, :], shift], axis=1)
    to_column(shift, col_ref)
    a_shift, b_shift = cross_halves(shift, first, half)
    straight = full_ref[:, :half]
    level = jnp.sum(jnp.where(row == col, straight, 0.0), axis=0, keepdims=True) - a_shift * b_shift
    stats_ref[...] = eight(sums, squares, level)
    send_ref[keep_ref.shape[0] :, :] = coded(jnp.concatenate([sums, squares, level, level], axis=0))
    corner = full_ref[half - 256 : half, half - 256 : half].T[256 - quarter :, :]
    corner = pltpu.roll(corner, quarter, 1)[:, :quarter]
    corner = jnp.concatenate([corner, corner], axis=0)
    folded = jnp.concatenate([corner, jnp.zeros((half, half - quarter), F32)], axis=1)
    apart = full_ref[:, half:]
    full_ref[:, :half] = jnp.where(col < quarter, jnp.where(row > col, straight, folded), apart)
    cols = cross_cols(shift, first, half)

    def value(start):
        products = cross_products(col_ref, cols, core, start, *index_parts(start, STEP, half))
        return full_ref[pl.ds(start, STEP), :half] - products

    halved(pos_ref[1], keep_ref, send_ref, value)


def own_merged(msg_ref, stats_ref, rows, samples):
    theirs = decoded(msg_ref[rows:, :], 2)
    sums, squares = stats_ref[:1, :], stats_ref[1:2, :]
    shift = (sums - theirs[:1]) * (1.0 / math.sqrt(2.0 * samples))
    return sums + theirs[:1], squares + theirs[1:2] + shift * shift, shift


def cross_merged(msg_ref, stats_ref, own_shift, rows, samples, first):
    half = stats_ref.shape[1]
    theirs = decoded(msg_ref[rows:, :], 4)
    sums, squares, level = stats_ref[:1, :], stats_ref[1:2, :], stats_ref[2:3, :]
    shift = (sums - theirs[:1]) * (1.0 / math.sqrt(2.0 * samples))
    both = jnp.concatenate([own_shift, shift], axis=1)
    a_shift, b_shift = cross_halves(both, first, half)
    return (
        sums + theirs[:1],
        squares + theirs[1:2] + shift * shift,
        (level + theirs[2:3]) + a_shift * b_shift,
        both,
    )


def passed_on(pos_ref, keep_ref, send_ref, value, split):
    if split:
        halved(pos_ref[2], keep_ref, send_ref, value)
        return keep_ref.shape[0]
    rows = send_ref.shape[0] // STEP * STEP
    for k in range(0, rows, STEP):
        send_ref[k : k + STEP, :] = value(k).astype(BF16)
    return rows


def own_merge_kernel(pos_ref, kept_ref, msg_ref, stats_ref, *refs, samples, split):
    keep_ref = refs[0] if split else None
    send_ref, out_ref, col_ref = refs[-3:]
    rows = kept_ref.shape[0] // STEP * STEP
    half = kept_ref.shape[1] // 2
    sums, squares, shift = own_merged(msg_ref, stats_ref, rows, samples)
    out_ref[...] = eight(sums, squares, shift)
    to_column(shift, col_ref)
    cols = own_cols(shift, half)
    base = pos_ref[3] if split else pos_ref[4]

    def value(offset):
        start = base + offset
        products = own_products(col_ref, cols, start, *index_parts(start, STEP, half))
        here = pl.ds(offset, STEP)
        both = kept_ref[here, :].astype(F32) + msg_ref[here, :].astype(F32)
        return both + jnp.concatenate(products, axis=1)

    done = passed_on(pos_ref, keep_ref, send_ref, value, split)
    send_ref[done:, :] = coded(jnp.concatenate([sums, squares], axis=0))


def cross_merge_kernel(pos_ref, kept_ref, msg_ref, stats_ref, own_ref, *refs, samples, split):
    keep_ref = refs[0] if split else None
    send_ref, out_ref, col_ref = refs[-3:]
    rows = kept_ref.shape[0] // STEP * STEP
    half = kept_ref.shape[1]
    core = pos_ref[0]
    first = core == 0
    sums, squares, level, shift = cross_merged(msg_ref, stats_ref, own_ref[2:3, :], rows, samples, first)
    out_ref[...] = eight(sums, squares, level)
    to_column(shift, col_ref)
    cols = cross_cols(shift, first, half)
    base = pos_ref[3] if split else pos_ref[4]

    def value(offset):
        start = base + offset
        products = cross_products(col_ref, cols, core, start, *index_parts(start, STEP, half))
        here = pl.ds(offset, STEP)
        return kept_ref[here, :].astype(F32) + msg_ref[here, :].astype(F32) + products

    done = passed_on(pos_ref, keep_ref, send_ref, value, split)
    send_ref[done:, :] = coded(jnp.concatenate([sums, squares, level, level], axis=0))


def unbiased(correl, everyone):
    squared = correl * correl
    return squared - (1.0 - squared) * (1.0 / (everyone - 2.0))


def placed_at(rows_part, offset, half):
    blank = jnp.zeros((rows_part.shape[0], half - rows_part.shape[1]), F32)
    return pltpu.roll(jnp.concatenate([rows_part, blank], axis=1), offset, 1)


def own_score_kernel(
    pos_ref, kept_ref, msg_ref, stats_ref, limit_ref, flag_ref, sub_ref,
    out_ref, vec_ref, col_ref, scale_ref, lim_ref, one_ref, two_ref, *, samples,
):
    rows = one_ref.shape[0]
    half = kept_ref.shape[1] // 2
    everyone = 2.0 * samples
    _, squares, shift = own_merged(msg_ref, stats_ref, rows, samples)
    scale = 1.0 / jnp.sqrt(squares * (1.0 / everyone) + VAR_EPS)
    vec_ref[...] = eight(shift, scale)
    to_column(shift, col_ref)
    to_column(scale * (1.0 / everyone), scale_ref)
    to_column(limit_ref[:1, : 2 * half], lim_ref)
    cols, scales = own_cols(shift, half), own_cols(scale, half)
    right_lim = limit_ref[:1, half : 2 * half]
    base = pos_ref[4]
    for k in range(0, rows, STEP):
        start = base + k
        row, col = index_parts(start, STEP, half)
        products = own_products(col_ref, cols, start, row, col)
        norms = own_products(scale_ref, scales, start, row, col)
        left_lim = wide_rows(lim_ref, start, STEP, half)
        gaps = (half + col - row, jnp.where(row == col, 8 * half, jnp.abs(row - col)))
        lims = (left_lim, jnp.where(row < col, left_lim, right_lim))
        for s, ref in ((0, one_ref), (1, two_ref)):
            here = slice(s * half, (s + 1) * half)
            value = kept_ref[k : k + STEP, here].astype(F32) + msg_ref[k : k + STEP, here].astype(F32)
            weight = unbiased((value + products[s]) * norms[s], everyone)
            ref[k : k + STEP, :] = jnp.where(gaps[s].astype(F32) <= lims[s], weight, 0.0).astype(BF16)
    row, col = index_parts(base, rows, half)
    one, two = one_ref[...], two_ref[...]
    zero = jnp.zeros_like(two)
    upper, lower = jnp.where(row < col, two, zero), jnp.where(row > col, two, zero)
    f_left, f_right = flag_ref[:, :half], flag_ref[:, half : 2 * half]
    s_left, s_right = sub_ref[:, :rows], sub_ref[:, 128 : 128 + rows]
    out_ref[:, :half] = dot_n(s_left, upper) + placed_at(dot_t(f_right, one) + dot_t(f_left, upper), base, half)
    out_ref[:, half:] = dot_n(s_left, one) + dot_n(s_right, lower) + placed_at(dot_t(f_right, lower), base, half)


def cross_score_kernel(
    pos_ref, kept_ref, msg_ref, stats_ref, vec_ref, limit_ref, flag_ref, sub_ref, own_ref,
    out_ref, col_ref, scale_ref, lim_ref, three_ref, *, samples,
):
    rows = three_ref.shape[0]
    half = kept_ref.shape[1]
    quarter = half // 2
    core = pos_ref[0]
    first = core == 0
    everyone = 2.0 * samples
    _, squares, level, shift = cross_merged(msg_ref, stats_ref, vec_ref[:1, :], rows, samples, first)
    scale = 1.0 / jnp.sqrt(squares * (1.0 / everyone) + VAR_EPS)
    scale = jnp.concatenate([vec_ref[1:2, :], scale], axis=1)
    limit = limit_ref[:1, :]
    to_column(shift, col_ref)
    to_column(scale * (1.0 / everyone), scale_ref)
    to_column(limit, lim_ref)
    cols, scales = cross_cols(shift, first, half), cross_cols(scale, first, half)
    _, late_lim, _ = cross_cols(limit, first, half)
    base = pos_ref[4]
    for k in range(0, rows, STEP):
        start = base + k
        row, col = index_parts(start, STEP, half)
        fold = col < quarter
        products = cross_products(col_ref, cols, core, start, row, col)
        norms = cross_products(scale_ref, scales, core, start, row, col)
        a_lim = wide_rows(lim_ref, start + 2 * half * core, STEP, half)
        a2_lim = wide_rows(lim_ref, start + half + half * core, STEP, half)
        lims = jnp.where(fold, jnp.where(row > col, a_lim, late_lim), a2_lim)
        near = jnp.where(row == col, 8 * half, 2 * half - jnp.abs(row - col))
        gaps = jnp.where(fold, near, quarter + quarter * core + col - row)
        value = kept_ref[k : k + STEP, :].astype(F32) + msg_ref[k : k + STEP, :].astype(F32)
        weight = unbiased((value + products) * norms, everyone)
        three_ref[k : k + STEP, :] = jnp.where(gaps.astype(F32) <= lims, weight, 0.0).astype(BF16)
    a_scale, b_scale = cross_halves(scale, first, half)
    a_limit, _ = cross_halves(limit, first, half)
    lane = lax.broadcasted_iota(jnp.int32, (1, half), 1)
    level = unbiased(level * (1.0 / everyone) * a_scale * b_scale, everyone)
    mine = (lane >= base) & (lane < base + rows) & (a_limit >= 2.0 * half)
    level = jnp.where(mine, level, 0.0)
    row, col = index_parts(base, rows, half)
    three = three_ref[...]
    zero = jnp.zeros_like(three)
    fold = col < quarter
    straight = jnp.where(fold & (row > col), three, zero)
    folded = jnp.where(fold & (row < col), three, zero)
    apart = jnp.where(fold, zero, three)
    f_a, f_b = flag_ref[:, :half], flag_ref[:, half : 2 * half]
    f_late, f_b3 = flag_ref[:, 2 * half : 3 * half], flag_ref[:, 3 * half :]
    s_a, s_a2, s_late = sub_ref[:, 256 : 256 + rows], sub_ref[:, 384 : 384 + rows], sub_ref[:, 512 : 512 + rows]
    out_a = placed_at(dot_t(f_b, straight), base, half) + pltpu.roll(dot_n(s_late, folded), quarter, 1)
    out_b = dot_n(s_a, straight) + placed_at(dot_t(f_late, folded), lax.rem(base + quarter, half), half)
    out_a = out_a + f_b.astype(F32) * level
    out_b = out_b + f_a.astype(F32) * level
    out_a2 = placed_at(dot_t(f_b3, apart), base, half)
    out_b3 = dot_n(s_a2, apart)
    out_ref[:, :half] = own_ref[:, :half] + pick(first, out_a, out_b3)
    out_ref[:, half : 2 * half] = own_ref[:, half:] + pick(first, out_a2, out_b)
    out_ref[:, 2 * half :] = pick(first, out_b + pltpu.roll(out_b3, quarter, 1), out_a + out_a2)


def local_kernel(pos_ref, annot_ref, chrom_ref, reach_ref, ids_ref, flag_ref, cross_ref, sub_ref, limit_ref, block_ref):
    half = annot_ref.shape[1] // 4
    first = pos_ref[0] == 0
    base = pos_ref[4]
    flags = annot_ref[...].astype(F32)

    def quarters(x):
        return [x[:, k * half : (k + 1) * half] for k in range(4)]

    def local(x):
        one, two, three, four = quarters(x)
        return pick(first, one, three), pick(first, two, four), pick(first, three, two)

    left, right, there = local(flags)
    for k, x in enumerate((left, right, there)):
        flag_ref[:, k * half : (k + 1) * half] = x.astype(BF16)
    a_cols, b_cols, a2_cols = pick(first, left, there), pick(first, there, right), pick(first, right, there)
    b3_cols = pick(first, pltpu.roll(there, half // 2, 1), left)
    for k, x in enumerate((a_cols, b_cols, pltpu.roll(a_cols, half // 2, 1), b3_cols)):
        cross_ref[:, k * half : (k + 1) * half] = x.astype(BF16)
    back = lax.rem(half - base, half)
    late = lax.rem(half + half // 2 - base, half)
    for k, (x, turn) in enumerate(((left, back), (right, back), (a_cols, back), (a2_cols, back), (b_cols, late))):
        sub_ref[:, k * 128 : (k + 1) * 128] = pltpu.roll(x, turn, 1)[:, :128].astype(BF16)

    def line(ref):
        return jnp.concatenate([ref[k : k + 1, :] for k in range(ref.shape[0])], axis=1).astype(F32)

    chrom, reach = line(chrom_ref), line(reach_ref)
    ends = [jnp.sum((chrom <= k).astype(F32), axis=1, keepdims=True) for k in (1, 2, 3)]
    last = jnp.where(chrom == 1, ends[0], jnp.where(chrom == 2, ends[1], ends[2]))
    place = lax.broadcasted_iota(jnp.int32, chrom.shape, 1).astype(F32)
    limit = jnp.concatenate(local(jnp.minimum(reach, last - 1.0 - place)), axis=1)
    limit_ref[...] = jnp.broadcast_to(limit, limit_ref.shape)
    block = jnp.concatenate(local(line(ids_ref)), axis=1)
    block_ref[...] = jnp.broadcast_to(block, block_ref.shape)


def join_kernel(pos_ref, own_ref, other_ref, sums_ref, there_ref, score_ref, out_ref):
    half = other_ref.shape[1]
    first = pos_ref[0] == 0
    nothing = jnp.zeros(other_ref.shape, F32)
    other = other_ref[...]
    score_ref[:, :half] = own_ref[:, :half] + pick(first, nothing, other)
    score_ref[:, half:] = own_ref[:, half:] + pick(first, other, nothing)
    out_ref[...] = sums_ref[...] + there_ref[...]


def block_kernel(pos_ref, score_ref, flag_ref, block_ref, own_ref, msg_ref, sum_ref):
    slab = own_ref.shape[1]
    blocks = block_ref[:1, :]
    number = lax.broadcasted_iota(jnp.int32, (sum_ref.shape[0], blocks.shape[1]), 0).astype(F32)
    hot = jnp.where(number == blocks, 1.0, 0.0).astype(BF16)
    own = score_ref[:, :slab] + flag_ref[:, :slab].astype(F32)
    other = score_ref[:, slab:]
    own_ref[...] = own
    msg_ref[...] = other
    scores = jnp.concatenate([own, other], axis=1)
    high = scores.astype(BF16)
    left = scores - high.astype(F32)
    middle = left.astype(BF16)
    low = (left - middle.astype(F32)).astype(BF16)
    sum_ref[...] = dot_t(hot, high) + dot_t(hot, middle) + dot_t(hot, low)


def call(kernel, inputs, outputs, scratch, flops, moved):
    vmem = pl.BlockSpec(memory_space=pltpu.VMEM)
    smem = pl.BlockSpec(memory_space=pltpu.SMEM)
    return pl.pallas_call(
        kernel,
        out_shape=outputs,
        in_specs=[smem] + [vmem] * (len(inputs) - 1),
        out_specs=jax.tree.map(lambda _: vmem, outputs),
        scratch_shapes=scratch,
        compiler_params=pltpu.CompilerParams(vmem_limit_bytes=VMEM_LIMIT),
        cost_estimate=pl.CostEstimate(flops=flops, bytes_accessed=moved, transcendentals=0),
    )(*inputs)


def body(genotypes, chromosome, blocks, annotation, reach):
    count, slab = genotypes.shape
    half = slab // 2
    quarter = half // 2
    width = 3 * half
    snps = chromosome.shape[0]
    parts = lax.axis_size("samples")
    bits = parts.bit_length() - 1
    core = lax.axis_index("genome")
    place = lax.axis_index("samples")
    order = [list(range(bits)), CORE_ONE_ORDER + list(range(3, bits))]
    bit_at = [(place >> jnp.where(core == 0, order[0][t], order[1][t])) & 1 for t in range(bits)]

    def exchange(x, t):
        route = []
        for s in range(parts):
            for g in range(2):
                route.append((s * 2 + g, (s ^ (1 << order[g][t])) * 2 + g))
        return lax.ppermute(x, ("samples", "genome"), route)

    def across(x):
        return lax.ppermute(x, "genome", [(0, 1), (1, 0)])

    def shape(rows, cols, dtype):
        return jax.ShapeDtypeStruct((rows, cols), dtype)

    base = bit_at[0] * quarter + bit_at[1] * (quarter // 2)
    rows = quarter // 2

    where = jnp.stack([core, bit_at[0], bit_at[1], bit_at[0] * quarter, base]).astype(jnp.int32)
    annot = annotation.shape[0]

    def tiles(x):
        return x.reshape(-1, 128)

    flags, flags_cross, subs, limit, ids = call(
        local_kernel,
        (where, annotation, tiles(chromosome), tiles(reach), tiles(blocks)),
        (
            shape(annot, width, BF16),
            shape(annot, 4 * half, BF16),
            shape(annot, 5 * 128, BF16),
            shape(8, width, F32),
            shape(8, width, F32),
        ),
        [],
        annot * snps * 10,
        annot * snps * 8,
    )
    hot_rows = -(-NBLK // 8) * 8

    own_column = pltpu.VMEM((slab, 128), F32)
    column = pltpu.VMEM((width + quarter, 128), F32)

    def outputs(kept, sent, cols, stat_rows):
        kept_shape = (shape(kept, cols, F32),) if kept else ()
        return kept_shape + (shape(sent + stat_rows, cols, BF16), shape(8, cols, F32))

    keep_a, send_a, stats_a, turned, piece = call(
        own_gram_kernel,
        (where, genotypes),
        outputs(quarter, quarter, slab, 8) + (shape(slab, count, BF16), shape(count, half, BF16)),
        [pltpu.VMEM((half, slab), F32), own_column],
        2 * count * half * half * 3,
        count * slab * 2,
    )
    there = across(piece)
    msg_a = exchange(send_a, 0)
    keep_b, send_b, stats_b = call(
        cross_gram_kernel,
        (where, turned, there, stats_a),
        outputs(quarter, quarter, half, 16),
        [pltpu.VMEM((half, slab), F32), column, pltpu.VMEM((half, count), BF16)],
        2 * count * half * half * 3,
        count * slab * 2,
    )
    msg_b = exchange(send_b, 0)
    samples = float(count)
    for t in range(1, bits):
        split = t == 1
        msg_a, send_b = lax.optimization_barrier((msg_a, send_b)) if split else (msg_a, send_b)
        *kept_a, send_a, stats_a = call(
            functools.partial(own_merge_kernel, samples=samples, split=split),
            (where, keep_a, msg_a, stats_a),
            outputs(rows if split else 0, rows, slab, 8),
            [own_column],
            rows * slab * 8,
            rows * slab * 20,
        )
        msg_a = exchange(send_a, t)
        *kept_b, send_b, stats_b = call(
            functools.partial(cross_merge_kernel, samples=samples, split=split),
            (where, keep_b, msg_b, stats_b, stats_a),
            outputs(rows if split else 0, rows, half, 16),
            [column],
            rows * half * 8,
            rows * half * 20,
        )
        msg_b = exchange(send_b, t)
        keep_a = kept_a[0] if split else send_a
        keep_b = kept_b[0] if split else send_b
        samples = 2 * samples
    scores_a, vectors = call(
        functools.partial(own_score_kernel, samples=samples),
        (where, keep_a, msg_a, stats_a, limit, flags, subs),
        (shape(annot, slab, F32), shape(8, slab, F32)),
        [own_column] * 3 + [pltpu.VMEM((rows, half), BF16)] * 2,
        2 * annot * half * rows * 8,
        rows * slab * 20,
    )
    partial = call(
        functools.partial(cross_score_kernel, samples=samples),
        (where, keep_b, msg_b, stats_b, vectors, limit, flags_cross, subs, scores_a),
        shape(annot, width, F32),
        [column] * 3 + [pltpu.VMEM((rows, half), BF16)],
        2 * annot * half * rows * 8,
        rows * slab * 20,
    )
    for t in (1, 0):
        rounded = partial.astype(jnp.float16)
        partial = rounded.astype(F32) + exchange(rounded, t).astype(F32)
    own, other, sums = call(
        block_kernel,
        (where, partial, flags, ids),
        (shape(annot, slab, F32), shape(annot, half, F32), shape(hot_rows, annot, F32)),
        [],
        2 * annot * width * hot_rows * 3,
        annot * width * 8,
    )
    ld_scores, block_sums = call(
        join_kernel,
        (where, own, across(other), sums, across(sums)),
        (shape(annot, slab, F32), shape(hot_rows, annot, F32)),
        [],
        annot * width,
        annot * width * 8,
    )
    return (ld_scores, block_sums[:NBLK].T)


def solution(mesh):
    placed = (
        P(("groups", "samples"), "genome"),
        P("groups"),
        P("groups"),
        P(None, "groups"),
        P("groups"),
    )
    return jax.shard_map(
        body,
        mesh=mesh,
        in_specs=placed,
        out_specs=(P(None, ("groups", "genome")), P(None, "groups")),
        check_vma=False,
    )
```

```python
import functools
import math

import jax
import jax.numpy as jnp
from jax import lax
from jax.experimental import pallas as pl
from jax.experimental.pallas import tpu as pltpu
from jax.sharding import PartitionSpec as P

NBLK = 200
VAR_EPS = 1e-06
F32 = jnp.float32
BF16 = jnp.bfloat16
CORE_ONE_ORDER = [1, 2, 0]
VMEM_LIMIT = 20 * 1024 * 1024
COPY_LIMIT = 50 * 1024 * 1024


STEP = 48


def pick(first, one, other):
    return jnp.where(first, one, other)


def index_parts(start, count, half):
    row = lax.broadcasted_iota(jnp.int32, (count, half), 0) + start
    col = lax.broadcasted_iota(jnp.int32, (count, half), 1)
    return row, col


def column_table(vectors, start, ref):
    table = eight(*vectors)
    half = table.shape[1]
    if start is not None:
        table = pltpu.roll(table, lax.rem(half - start, half), 1)
    for k in range(ref.shape[0] // 128):
        ref[k * 128 : (k + 1) * 128, :8] = table[:, k * 128 : (k + 1) * 128].T


def table_rows(ref, offset, columns, count=STEP):
    rows = ref[pl.ds(pl.multiple_of(offset, 16), count), :8]
    return tuple(rows[:, k : k + 1] for k in columns)


def coded(stats):
    high = stats.astype(BF16)
    left = stats - high.astype(F32)
    middle = left.astype(BF16)
    low = (left - middle.astype(F32)).astype(BF16)
    blank = jnp.zeros((stats.shape[0] * 8 // 2 - 3 * stats.shape[0], stats.shape[1]), BF16)
    return jnp.concatenate([high, middle, low, blank], axis=0)


def decoded(rows, count):
    parts = rows.astype(F32)
    return parts[:count] + parts[count : 2 * count] + parts[2 * count : 3 * count]


def own_cols(vec, half):
    return vec[:, :half], vec[:, half : 2 * half]


def own_products(rows, cols, row, col):
    (l_rows, r_rows), (left, right) = rows, cols
    return l_rows * right, jnp.where(row < col, l_rows * left, r_rows * right)


def cross_halves(vec, first, half):
    left, right, there = vec[:, :half], vec[:, half : 2 * half], vec[:, 2 * half :]
    return pick(first, left, there), pick(first, there, right)


def cross_cols(vec, first, half):
    vec = jnp.broadcast_to(vec, (8, vec.shape[1]))
    a_cols, b_cols = cross_halves(vec, first, half)
    a_turned = pltpu.roll(a_cols, half // 2, 1)
    b3_cols = pick(first, pltpu.roll(vec[:, 2 * half :], half // 2, 1), vec[:, :half])
    return b_cols[:1], a_turned[:1], b3_cols[:1]


def cross_vectors(vec, first, half):
    a_cols, b_cols = cross_halves(vec, first, half)
    a2_cols = pick(first, vec[:, half : 2 * half], vec[:, 2 * half :])
    b_late = pltpu.roll(jnp.broadcast_to(b_cols, (8, half)), half // 2, 1)[:1]
    return a_cols, a2_cols, b_late


def cross_products(rows, cols, row, col):
    (a_rows, a2_rows, b_rows), (c_b, c_a, c_b3) = rows, cols
    half = row.shape[1]
    return jnp.where(
        col < half // 2, jnp.where(row > col, a_rows * c_b, b_rows * c_a), a2_rows * c_b3
    )


def dot_n(left, right):
    return lax.dot_general(left, right, (((1,), (0,)), ((), ())), preferred_element_type=F32)


def dot_t(left, right):
    return lax.dot_general(left, right, (((1,), (1,)), ((), ())), preferred_element_type=F32)


def squared_sums(ref, start, stop):
    width = ref.shape[1]
    total = jnp.zeros((8, width), F32)
    for k in range(start, stop, 64):
        part = ref[k : k + 64, :].astype(F32)
        total = total + jnp.sum((part * part).reshape(8, 8, width), axis=0)
    return total


def moments(ref, total):
    count = ref.shape[0]
    sums = dot_n(jnp.ones((8, count), BF16), ref[...])[:1]
    shift = sums * (1.0 / math.sqrt(count))
    return sums, jnp.sum(total, axis=0, keepdims=True) - shift * shift, shift


def eight(*rows):
    return jnp.concatenate(list(rows) + [rows[-1]] * (8 - len(rows)), axis=0)


def halved(bit, keep_ref, send_ref, value):
    part = keep_ref.shape[0]
    for k in range(0, part, STEP):
        send_ref[k : k + STEP, :] = value(pl.multiple_of((1 - bit) * part + k, 16)).astype(BF16)
        keep_ref[k : k + STEP, :] = value(pl.multiple_of(bit * part + k, 16))


def own_gram_kernel(
    pos_ref, slab_ref, keep_ref, send_ref, stats_ref, turned_ref, piece_ref, full_ref, col_ref, own_ref, sems,
):
    count, slab = slab_ref.shape
    half = slab // 2
    pieces = sems.shape[0]
    size = count // pieces
    copies = []
    for k in range(pieces):
        here = pl.ds(k * size, size)
        copies.append(pltpu.make_async_copy(slab_ref.at[here, :], own_ref.at[here, :], sems.at[k]))
        copies[k].start()
    total = jnp.zeros((8, slab), F32)
    for k in range(pieces):
        copies[k].wait()
        here = slice(k * size, (k + 1) * size)
        turned_ref[:, here] = own_ref[here, :].T
        total = total + squared_sums(own_ref, k * size, (k + 1) * size)

    @pl.when(pos_ref[0] == 0)
    def _():
        piece_ref[...] = own_ref[:, half:]

    @pl.when(pos_ref[0] != 0)
    def _():
        piece_ref[...] = own_ref[:, :half]

    sums, squares, shift = moments(own_ref, total)
    stats_ref[...] = eight(sums, squares, shift)
    column_table(own_cols(shift, half), None, col_ref)
    left, right = turned_ref[:half, :], turned_ref[half:, :]
    full_ref[:, :half] = dot_n(left, own_ref[:, half:])
    row, col = index_parts(0, half, half)
    full_ref[:, half:] = jnp.where(row < col, dot_n(left, own_ref[:, :half]), dot_n(right, own_ref[:, half:]))
    cols = own_cols(shift, half)

    def value(start):
        rows = table_rows(col_ref, start, (0, 1))
        products = own_products(rows, cols, *index_parts(start, STEP, half))
        return full_ref[pl.ds(start, STEP), :] - jnp.concatenate(products, axis=1)

    halved(pos_ref[1], keep_ref, send_ref, value)
    send_ref[keep_ref.shape[0] :, :] = coded(jnp.concatenate([sums, squares], axis=0))


def cross_gram_kernel(pos_ref, turned_ref, there_ref, own_stats_ref, keep_ref, send_ref, stats_ref, full_ref, col_ref, side_ref):
    half = there_ref.shape[1]
    quarter = half // 2
    core = pos_ref[0]
    first = core == 0
    row, col = index_parts(0, half, half)

    @pl.when(first)
    def _():
        full_ref[:, :half] = dot_n(turned_ref[:half, :], there_ref[...])
        full_ref[:, half:] = pltpu.roll(dot_n(turned_ref[half:, :], there_ref[...]), quarter, 1)

    @pl.when(jnp.logical_not(first))
    def _():
        side_ref[...] = there_ref[...].T
        full_ref[:, :half] = dot_t(side_ref[...], turned_ref[half:, :])
        full_ref[:, half:] = dot_t(side_ref[...], turned_ref[:half, :])

    sums, squares, shift = moments(there_ref, squared_sums(there_ref, 0, there_ref.shape[0]))
    shift = jnp.concatenate([own_stats_ref[2:3, :], shift], axis=1)
    column_table(cross_vectors(shift, first, half), None, col_ref)
    a_shift, b_shift = cross_halves(shift, first, half)
    straight = full_ref[:, :half]
    level = jnp.sum(jnp.where(row == col, straight, 0.0), axis=0, keepdims=True) - a_shift * b_shift
    stats_ref[...] = eight(sums, squares, level)
    send_ref[keep_ref.shape[0] :, :] = coded(jnp.concatenate([sums, squares, level, level], axis=0))
    corner = full_ref[half - 256 : half, half - 256 : half].T[256 - quarter :, :]
    corner = pltpu.roll(corner, quarter, 1)[:, :quarter]
    corner = jnp.concatenate([corner, corner], axis=0)
    folded = jnp.concatenate([corner, jnp.zeros((half, half - quarter), F32)], axis=1)
    apart = full_ref[:, half:]
    full_ref[:, :half] = jnp.where(col < quarter, jnp.where(row > col, straight, folded), apart)
    cols = cross_cols(shift, first, half)

    def value(start):
        rows = table_rows(col_ref, start, (0, 1, 2))
        products = cross_products(rows, cols, *index_parts(start, STEP, half))
        return full_ref[pl.ds(start, STEP), :half] - products

    halved(pos_ref[1], keep_ref, send_ref, value)


def own_merged(msg_ref, stats_ref, rows, samples):
    theirs = decoded(msg_ref[rows:, :], 2)
    sums, squares = stats_ref[:1, :], stats_ref[1:2, :]
    shift = (sums - theirs[:1]) * (1.0 / math.sqrt(2.0 * samples))
    return sums + theirs[:1], squares + theirs[1:2] + shift * shift, shift


def cross_merged(msg_ref, stats_ref, own_shift, rows, samples, first):
    half = stats_ref.shape[1]
    theirs = decoded(msg_ref[rows:, :], 4)
    sums, squares, level = stats_ref[:1, :], stats_ref[1:2, :], stats_ref[2:3, :]
    shift = (sums - theirs[:1]) * (1.0 / math.sqrt(2.0 * samples))
    both = jnp.concatenate([own_shift, shift], axis=1)
    a_shift, b_shift = cross_halves(both, first, half)
    return (
        sums + theirs[:1],
        squares + theirs[1:2] + shift * shift,
        (level + theirs[2:3]) + a_shift * b_shift,
        both,
    )


def passed_on(pos_ref, keep_ref, send_ref, value, split):
    if split:
        halved(pos_ref[2], keep_ref, send_ref, value)
        return keep_ref.shape[0]
    rows = send_ref.shape[0] // STEP * STEP
    for k in range(0, rows, STEP):
        send_ref[k : k + STEP, :] = value(k).astype(BF16)
    return rows


def own_merge_kernel(pos_ref, kept_ref, msg_ref, stats_ref, *refs, samples, split):
    keep_ref = refs[0] if split else None
    send_ref, out_ref, col_ref = refs[-3:]
    rows = kept_ref.shape[0] // STEP * STEP
    half = kept_ref.shape[1] // 2
    sums, squares, shift = own_merged(msg_ref, stats_ref, rows, samples)
    out_ref[...] = eight(sums, squares, shift)
    cols = own_cols(shift, half)
    base = pos_ref[3] if split else pos_ref[4]
    column_table(cols, base, col_ref)

    def value(offset):
        factors = table_rows(col_ref, offset, (0, 1))
        products = own_products(factors, cols, *index_parts(base + offset, STEP, half))
        here = pl.ds(offset, STEP)
        both = kept_ref[here, :].astype(F32) + msg_ref[here, :].astype(F32)
        return both + jnp.concatenate(products, axis=1)

    done = passed_on(pos_ref, keep_ref, send_ref, value, split)
    send_ref[done:, :] = coded(jnp.concatenate([sums, squares], axis=0))


def cross_merge_kernel(pos_ref, kept_ref, msg_ref, stats_ref, own_ref, *refs, samples, split):
    keep_ref = refs[0] if split else None
    send_ref, out_ref, col_ref = refs[-3:]
    rows = kept_ref.shape[0] // STEP * STEP
    half = kept_ref.shape[1]
    core = pos_ref[0]
    first = core == 0
    sums, squares, level, shift = cross_merged(msg_ref, stats_ref, own_ref[2:3, :], rows, samples, first)
    out_ref[...] = eight(sums, squares, level)
    cols = cross_cols(shift, first, half)
    base = pos_ref[3] if split else pos_ref[4]
    column_table(cross_vectors(shift, first, half), base, col_ref)

    def value(offset):
        factors = table_rows(col_ref, offset, (0, 1, 2))
        products = cross_products(factors, cols, *index_parts(base + offset, STEP, half))
        here = pl.ds(offset, STEP)
        return kept_ref[here, :].astype(F32) + msg_ref[here, :].astype(F32) + products

    done = passed_on(pos_ref, keep_ref, send_ref, value, split)
    send_ref[done:, :] = coded(jnp.concatenate([sums, squares, level, level], axis=0))


def unbiased(correl, everyone):
    squared = correl * correl
    return squared - (1.0 - squared) * (1.0 / (everyone - 2.0))


def placed_at(rows_part, offset, half):
    blank = jnp.zeros((rows_part.shape[0], half - rows_part.shape[1]), F32)
    return pltpu.roll(jnp.concatenate([rows_part, blank], axis=1), offset, 1)


def own_score_kernel(
    pos_ref, kept_ref, msg_ref, stats_ref, limit_ref, flag_ref, sub_ref,
    out_ref, vec_ref, col_ref, one_ref, two_ref, *, samples,
):
    rows = one_ref.shape[0]
    half = kept_ref.shape[1] // 2
    everyone = 2.0 * samples
    _, squares, shift = own_merged(msg_ref, stats_ref, rows, samples)
    scale = 1.0 / jnp.sqrt(squares * (1.0 / everyone) + VAR_EPS)
    vec_ref[...] = eight(shift, scale)
    cols, scales = own_cols(shift, half), own_cols(scale, half)
    factors = cols + own_cols(scale * (1.0 / everyone), half) + (limit_ref[:1, :half],)
    column_table(factors, pos_ref[4], col_ref)
    right_lim = limit_ref[:1, half : 2 * half]
    base = pos_ref[4]
    for k in range(0, rows, STEP):
        start = base + k
        row, col = index_parts(start, STEP, half)
        l_shift, r_shift, l_scale, r_scale, left_lim = table_rows(col_ref, k, range(5))
        products = own_products((l_shift, r_shift), cols, row, col)
        norms = own_products((l_scale, r_scale), scales, row, col)
        gaps = (half + col - row, jnp.where(row == col, 8 * half, jnp.abs(row - col)))
        lims = (left_lim, jnp.where(row < col, left_lim, right_lim))
        for s, ref in ((0, one_ref), (1, two_ref)):
            here = slice(s * half, (s + 1) * half)
            value = kept_ref[k : k + STEP, here].astype(F32) + msg_ref[k : k + STEP, here].astype(F32)
            weight = unbiased((value + products[s]) * norms[s], everyone)
            ref[k : k + STEP, :] = jnp.where(gaps[s].astype(F32) <= lims[s], weight, 0.0).astype(BF16)
    row, col = index_parts(base, rows, half)
    one, two = one_ref[...], two_ref[...]
    zero = jnp.zeros_like(two)
    upper, lower = jnp.where(row < col, two, zero), jnp.where(row > col, two, zero)
    f_left, f_right = flag_ref[:, :half], flag_ref[:, half : 2 * half]
    s_left, s_right = sub_ref[:, :rows], sub_ref[:, 128 : 128 + rows]
    out_ref[:, :half] = dot_n(s_left, upper) + placed_at(dot_t(f_right, one) + dot_t(f_left, upper), base, half)
    out_ref[:, half:] = dot_n(s_left, one) + dot_n(s_right, lower) + placed_at(dot_t(f_right, lower), base, half)


def cross_score_kernel(
    pos_ref, kept_ref, msg_ref, stats_ref, vec_ref, limit_ref, flag_ref, sub_ref, own_ref,
    out_ref, col_ref, three_ref, *, samples,
):
    rows = three_ref.shape[0]
    half = kept_ref.shape[1]
    quarter = half // 2
    core = pos_ref[0]
    first = core == 0
    everyone = 2.0 * samples
    _, squares, level, shift = cross_merged(msg_ref, stats_ref, vec_ref[:1, :], rows, samples, first)
    scale = 1.0 / jnp.sqrt(squares * (1.0 / everyone) + VAR_EPS)
    scale = jnp.concatenate([vec_ref[1:2, :], scale], axis=1)
    limit = limit_ref[:1, :]
    factors = cross_vectors(shift, first, half)
    factors = factors + cross_vectors(scale * (1.0 / everyone), first, half)
    column_table(factors + cross_vectors(limit, first, half)[:2], pos_ref[4], col_ref)
    cols, scales = cross_cols(shift, first, half), cross_cols(scale, first, half)
    _, late_lim, _ = cross_cols(limit, first, half)
    base = pos_ref[4]
    for k in range(0, rows, STEP):
        start = base + k
        row, col = index_parts(start, STEP, half)
        fold = col < quarter
        parts = table_rows(col_ref, k, range(8))
        a_lim, a2_lim = parts[6:]
        products = cross_products(parts[:3], cols, row, col)
        norms = cross_products(parts[3:6], scales, row, col)
        lims = jnp.where(fold, jnp.where(row > col, a_lim, late_lim), a2_lim)
        near = jnp.where(row == col, 8 * half, 2 * half - jnp.abs(row - col))
        gaps = jnp.where(fold, near, quarter + quarter * core + col - row)
        value = kept_ref[k : k + STEP, :].astype(F32) + msg_ref[k : k + STEP, :].astype(F32)
        weight = unbiased((value + products) * norms, everyone)
        three_ref[k : k + STEP, :] = jnp.where(gaps.astype(F32) <= lims, weight, 0.0).astype(BF16)
    a_scale, b_scale = cross_halves(scale, first, half)
    a_limit, _ = cross_halves(limit, first, half)
    lane = lax.broadcasted_iota(jnp.int32, (1, half), 1)
    level = unbiased(level * (1.0 / everyone) * a_scale * b_scale, everyone)
    mine = (lane >= base) & (lane < base + rows) & (a_limit >= 2.0 * half)
    level = jnp.where(mine, level, 0.0)
    row, col = index_parts(base, rows, half)
    three = three_ref[...]
    zero = jnp.zeros_like(three)
    fold = col < quarter
    straight = jnp.where(fold & (row > col), three, zero)
    folded = jnp.where(fold & (row < col), three, zero)
    apart = jnp.where(fold, zero, three)
    f_a, f_b = flag_ref[:, :half], flag_ref[:, half : 2 * half]
    f_late, f_b3 = flag_ref[:, 2 * half : 3 * half], flag_ref[:, 3 * half :]
    s_a, s_a2, s_late = sub_ref[:, 256 : 256 + rows], sub_ref[:, 384 : 384 + rows], sub_ref[:, 512 : 512 + rows]
    out_a = placed_at(dot_t(f_b, straight), base, half) + pltpu.roll(dot_n(s_late, folded), quarter, 1)
    out_b = dot_n(s_a, straight) + placed_at(dot_t(f_late, folded), lax.rem(base + quarter, half), half)
    out_a = out_a + f_b.astype(F32) * level
    out_b = out_b + f_a.astype(F32) * level
    out_a2 = placed_at(dot_t(f_b3, apart), base, half)
    out_b3 = dot_n(s_a2, apart)
    out_ref[:, :half] = own_ref[:, :half] + pick(first, out_a, out_b3)
    out_ref[:, half : 2 * half] = own_ref[:, half:] + pick(first, out_a2, out_b)
    out_ref[:, 2 * half :] = pick(first, out_b + pltpu.roll(out_b3, quarter, 1), out_a + out_a2)


def local_kernel(pos_ref, annot_ref, chrom_ref, reach_ref, ids_ref, flag_ref, cross_ref, sub_ref, limit_ref, block_ref):
    half = annot_ref.shape[1] // 4
    first = pos_ref[0] == 0
    base = pos_ref[4]
    flags = annot_ref[...].astype(F32)

    def quarters(x):
        return [x[:, k * half : (k + 1) * half] for k in range(4)]

    def local(x):
        one, two, three, four = quarters(x)
        return pick(first, one, three), pick(first, two, four), pick(first, three, two)

    left, right, there = local(flags)
    for k, x in enumerate((left, right, there)):
        flag_ref[:, k * half : (k + 1) * half] = x.astype(BF16)
    a_cols, b_cols, a2_cols = pick(first, left, there), pick(first, there, right), pick(first, right, there)
    b3_cols = pick(first, pltpu.roll(there, half // 2, 1), left)
    for k, x in enumerate((a_cols, b_cols, pltpu.roll(a_cols, half // 2, 1), b3_cols)):
        cross_ref[:, k * half : (k + 1) * half] = x.astype(BF16)
    back = lax.rem(half - base, half)
    late = lax.rem(half + half // 2 - base, half)
    for k, (x, turn) in enumerate(((left, back), (right, back), (a_cols, back), (a2_cols, back), (b_cols, late))):
        sub_ref[:, k * 128 : (k + 1) * 128] = pltpu.roll(x, turn, 1)[:, :128].astype(BF16)

    def line(ref):
        return jnp.concatenate([ref[k : k + 1, :] for k in range(ref.shape[0])], axis=1).astype(F32)

    chrom, reach = line(chrom_ref), line(reach_ref)
    ends = [jnp.sum((chrom <= k).astype(F32), axis=1, keepdims=True) for k in (1, 2, 3)]
    last = jnp.where(chrom == 1, ends[0], jnp.where(chrom == 2, ends[1], ends[2]))
    place = lax.broadcasted_iota(jnp.int32, chrom.shape, 1).astype(F32)
    limit = jnp.concatenate(local(jnp.minimum(reach, last - 1.0 - place)), axis=1)
    limit_ref[...] = jnp.broadcast_to(limit, limit_ref.shape)
    block = jnp.concatenate(local(line(ids_ref)), axis=1)
    block_ref[...] = jnp.broadcast_to(block, block_ref.shape)


def join_kernel(pos_ref, own_ref, other_ref, sums_ref, there_ref, score_ref, out_ref):
    half = other_ref.shape[1]
    first = pos_ref[0] == 0
    nothing = jnp.zeros(other_ref.shape, F32)
    other = other_ref[...]
    score_ref[:, :half] = own_ref[:, :half] + pick(first, nothing, other)
    score_ref[:, half:] = own_ref[:, half:] + pick(first, other, nothing)
    out_ref[...] = sums_ref[...] + there_ref[...]


def block_kernel(pos_ref, score_ref, flag_ref, block_ref, own_ref, msg_ref, sum_ref):
    slab = own_ref.shape[1]
    blocks = block_ref[:1, :]
    number = lax.broadcasted_iota(jnp.int32, (sum_ref.shape[0], blocks.shape[1]), 0).astype(F32)
    hot = jnp.where(number == blocks, 1.0, 0.0).astype(BF16)
    own = score_ref[:, :slab] + flag_ref[:, :slab].astype(F32)
    other = score_ref[:, slab:]
    own_ref[...] = own
    msg_ref[...] = other
    scores = jnp.concatenate([own, other], axis=1)
    high = scores.astype(BF16)
    left = scores - high.astype(F32)
    middle = left.astype(BF16)
    low = (left - middle.astype(F32)).astype(BF16)
    sum_ref[...] = dot_t(hot, high) + dot_t(hot, middle) + dot_t(hot, low)


def call(kernel, inputs, outputs, scratch, flops, moved, space=pltpu.VMEM, limit=VMEM_LIMIT):
    vmem = pl.BlockSpec(memory_space=pltpu.VMEM)
    source = pl.BlockSpec(memory_space=space)
    smem = pl.BlockSpec(memory_space=pltpu.SMEM)
    return pl.pallas_call(
        kernel,
        out_shape=outputs,
        in_specs=[smem] + [source] * (len(inputs) - 1),
        out_specs=jax.tree.map(lambda _: vmem, outputs),
        scratch_shapes=scratch,
        compiler_params=pltpu.CompilerParams(vmem_limit_bytes=limit),
        cost_estimate=pl.CostEstimate(flops=flops, bytes_accessed=moved, transcendentals=0),
    )(*inputs)


def body(genotypes, chromosome, blocks, annotation, reach):
    count, slab = genotypes.shape
    half = slab // 2
    quarter = half // 2
    width = 3 * half
    snps = chromosome.shape[0]
    parts = lax.axis_size("samples")
    bits = parts.bit_length() - 1
    core = lax.axis_index("genome")
    place = lax.axis_index("samples")
    order = [list(range(bits)), CORE_ONE_ORDER + list(range(3, bits))]
    bit_at = [(place >> jnp.where(core == 0, order[0][t], order[1][t])) & 1 for t in range(bits)]

    def exchange(x, t):
        route = []
        for s in range(parts):
            for g in range(2):
                route.append((s * 2 + g, (s ^ (1 << order[g][t])) * 2 + g))
        return lax.ppermute(x, ("samples", "genome"), route)

    def across(x):
        return lax.ppermute(x, "genome", [(0, 1), (1, 0)])

    def shape(rows, cols, dtype):
        return jax.ShapeDtypeStruct((rows, cols), dtype)

    base = bit_at[0] * quarter + bit_at[1] * (quarter // 2)
    rows = quarter // 2

    where = jnp.stack([core, bit_at[0], bit_at[1], bit_at[0] * quarter, base]).astype(jnp.int32)
    annot = annotation.shape[0]

    def tiles(x):
        return x.reshape(-1, 128)

    flags, flags_cross, subs, limit, ids = call(
        local_kernel,
        (where, annotation, tiles(chromosome), tiles(reach), tiles(blocks)),
        (
            shape(annot, width, BF16),
            shape(annot, 4 * half, BF16),
            shape(annot, 5 * 128, BF16),
            shape(8, width, F32),
            shape(8, width, F32),
        ),
        [],
        annot * snps * 10,
        annot * snps * 8,
    )
    hot_rows = -(-NBLK // 8) * 8

    def table_of(count):
        return pltpu.VMEM((-(-count // 128) * 128, 128), F32)

    table = table_of(rows)

    def outputs(kept, sent, cols, stat_rows):
        kept_shape = (shape(kept, cols, F32),) if kept else ()
        return kept_shape + (shape(sent + stat_rows, cols, BF16), shape(8, cols, F32))

    keep_a, send_a, stats_a, turned, piece = call(
        own_gram_kernel,
        (where, genotypes),
        outputs(quarter, quarter, slab, 8) + (shape(slab, count, BF16), shape(count, half, BF16)),
        [pltpu.VMEM((half, slab), F32), table_of(half), pltpu.VMEM((count, slab), BF16), pltpu.SemaphoreType.DMA((8,))],
        2 * count * half * half * 3,
        count * slab * 2,
        pltpu.HBM,
        COPY_LIMIT,
    )
    there = across(piece)
    msg_a = exchange(send_a, 0)
    keep_b, send_b, stats_b = call(
        cross_gram_kernel,
        (where, turned, there, stats_a),
        outputs(quarter, quarter, half, 16),
        [pltpu.VMEM((half, slab), F32), table_of(half), pltpu.VMEM((half, count), BF16)],
        2 * count * half * half * 3,
        count * slab * 2,
    )
    msg_b = exchange(send_b, 0)
    samples = float(count)
    for t in range(1, bits):
        split = t == 1
        msg_a, send_b = lax.optimization_barrier((msg_a, send_b)) if split else (msg_a, send_b)
        *kept_a, send_a, stats_a = call(
            functools.partial(own_merge_kernel, samples=samples, split=split),
            (where, keep_a, msg_a, stats_a),
            outputs(rows if split else 0, rows, slab, 8),
            [table_of(quarter) if split else table],
            rows * slab * 8,
            rows * slab * 20,
        )
        msg_a = exchange(send_a, t)
        *kept_b, send_b, stats_b = call(
            functools.partial(cross_merge_kernel, samples=samples, split=split),
            (where, keep_b, msg_b, stats_b, stats_a),
            outputs(rows if split else 0, rows, half, 16),
            [table_of(quarter) if split else table],
            rows * half * 8,
            rows * half * 20,
        )
        msg_b = exchange(send_b, t)
        keep_a = kept_a[0] if split else send_a
        keep_b = kept_b[0] if split else send_b
        samples = 2 * samples
    scores_a, vectors = call(
        functools.partial(own_score_kernel, samples=samples),
        (where, keep_a, msg_a, stats_a, limit, flags, subs),
        (shape(annot, slab, F32), shape(8, slab, F32)),
        [table] + [pltpu.VMEM((rows, half), BF16)] * 2,
        2 * annot * half * rows * 8,
        rows * slab * 20,
    )
    partial = call(
        functools.partial(cross_score_kernel, samples=samples),
        (where, keep_b, msg_b, stats_b, vectors, limit, flags_cross, subs, scores_a),
        shape(annot, width, F32),
        [table] + [pltpu.VMEM((rows, half), BF16)],
        2 * annot * half * rows * 8,
        rows * slab * 20,
    )
    for t in (1, 0):
        rounded = partial.astype(jnp.float16)
        partial = rounded.astype(F32) + exchange(rounded, t).astype(F32)
    own, other, sums = call(
        block_kernel,
        (where, partial, flags, ids),
        (shape(annot, slab, F32), shape(annot, half, F32), shape(hot_rows, annot, F32)),
        [],
        2 * annot * width * hot_rows * 3,
        annot * width * 8,
    )
    ld_scores, block_sums = call(
        join_kernel,
        (where, own, across(other), sums, across(sums)),
        (shape(annot, slab, F32), shape(hot_rows, annot, F32)),
        [],
        annot * width,
        annot * width * 8,
    )
    return (ld_scores, block_sums[:NBLK].T)


def solution(mesh):
    placed = (
        P(("groups", "samples"), "genome"),
        P("groups"),
        P("groups"),
        P(None, "groups"),
        P("groups"),
    )
    return jax.shard_map(
        body,
        mesh=mesh,
        in_specs=placed,
        out_specs=(P(None, ("groups", "genome")), P(None, "groups")),
        check_vma=False,
    )
```

```python
import functools
import math

import jax
import jax.numpy as jnp
from jax import lax
from jax.experimental import pallas as pl
from jax.experimental.pallas import tpu as pltpu
from jax.sharding import PartitionSpec as P

NBLK = 200
VAR_EPS = 1e-06
F32 = jnp.float32
BF16 = jnp.bfloat16
ORDERS = [[0, 1, 2], [1, 2, 0]]
ROUNDS = [[0, 1], [2, 1]]
VMEM_LIMIT = 20 * 1024 * 1024


STEP = 48


def pick(first, one, other):
    return jnp.where(first, one, other)


def index_parts(start, count, half):
    row = lax.broadcasted_iota(jnp.int32, (count, half), 0) + start
    col = lax.broadcasted_iota(jnp.int32, (count, half), 1)
    return row, col


def column_table(vectors, start, ref):
    table = eight(*vectors)
    half = table.shape[1]
    if start is not None:
        table = pltpu.roll(table, lax.rem(half - start, half), 1)
    for n in range(len(vectors)):
        for k in range(ref.shape[1] // 128):
            here = slice(k * 128, (k + 1) * 128)
            ref[n, here, :] = jnp.broadcast_to(table[n : n + 1, here], (128, 128)).T


def table_rows(ref, offset, columns, half):
    here = pl.ds(pl.multiple_of(offset, 16), STEP)
    return tuple(jnp.concatenate([ref[n, here, :]] * (half // 128), axis=1) for n in columns)


def high_low(values):
    high = values.astype(BF16)
    return high, (values - high.astype(F32)).astype(BF16)


def coded(sums, exact):
    high, low = high_low(sums)
    first, left = high_low(exact)
    third = (exact - first.astype(F32) - left.astype(F32)).astype(BF16)
    rows = coded_rows(sums.shape[0], exact.shape[0])
    gap = rows - 2 * sums.shape[0] - 3 * exact.shape[0]
    blank = [jnp.zeros((gap, sums.shape[1]), BF16)] if gap else []
    return jnp.concatenate([high, low, first, left, third] + blank, axis=0)


def coded_rows(many, exact):
    return -(-(2 * many + 3 * exact) // (24 * exact - 16)) * (24 * exact - 16)


def decoded(rows, many, exact):
    parts = rows.astype(F32)
    sums = parts[:many] + parts[many : 2 * many]
    at = 2 * many
    return sums, parts[at : at + exact] + parts[at + exact : at + 2 * exact] + parts[at + 2 * exact : at + 3 * exact]


def list_rows(many):
    return -(-many // 8) * 8


def put_stats(ref, sums, exact):
    many, width = sums.shape
    gap = list_rows(many) - many
    rows = [sums] + ([jnp.zeros((gap, width), F32)] if gap else [])
    rows = rows + [exact, jnp.zeros((8 - exact.shape[0], width), F32)]
    ref[...] = jnp.concatenate(rows, axis=0)


def merged(bit, msg_ref, stats_ref, rows, many, exact):
    theirs, added = decoded(msg_ref[rows:, :], many, exact)
    mine = stats_ref[:many, :]
    place = list_rows(many)
    both = pick(
        bit == 0, jnp.concatenate([mine, theirs], axis=0), jnp.concatenate([theirs, mine], axis=0)
    )
    return both, stats_ref[place : place + exact, :] + added


def two_parts(values):
    high, low = high_low(values)
    return high.astype(F32) + low.astype(F32)


def own_cols(vec, half):
    return vec[:, :half], vec[:, half : 2 * half]


def own_products(rows, cols, row, col):
    (l_rows, r_rows), (left, right) = rows, cols
    return l_rows * right, jnp.where(row < col, l_rows * left, r_rows * right)


def cross_halves(vec, first, half):
    left, right, there = vec[:, :half], vec[:, half : 2 * half], vec[:, 2 * half :]
    return pick(first, left, there), pick(first, there, right)


def cross_cols(vec, first, half):
    vec = jnp.broadcast_to(vec, (8, vec.shape[1]))
    a_cols, b_cols = cross_halves(vec, first, half)
    a_turned = pltpu.roll(a_cols, half // 2, 1)
    b3_cols = pick(first, pltpu.roll(vec[:, 2 * half :], half // 2, 1), vec[:, :half])
    return b_cols[:1], a_turned[:1], b3_cols[:1]


def cross_vectors(vec, first, half):
    a_cols, b_cols = cross_halves(vec, first, half)
    a2_cols = pick(first, vec[:, half : 2 * half], vec[:, 2 * half :])
    b_late = pltpu.roll(jnp.broadcast_to(b_cols, (8, half)), half // 2, 1)[:1]
    return a_cols, a2_cols, b_late


def cross_products(rows, cols, row, col):
    (a_rows, a2_rows, b_rows), (c_b, c_a, c_b3) = rows, cols
    half = row.shape[1]
    return jnp.where(
        col < half // 2, jnp.where(row > col, a_rows * c_b, b_rows * c_a), a2_rows * c_b3
    )


def dot_n(left, right):
    return lax.dot_general(left, right, (((1,), (0,)), ((), ())), preferred_element_type=F32)


def dot_t(left, right):
    return lax.dot_general(left, right, (((1,), (1,)), ((), ())), preferred_element_type=F32)


def squared_sums(ref, start, stop):
    width = ref.shape[1]
    total = jnp.zeros((8, width), F32)
    for k in range(start, stop, 64):
        part = ref[k : k + 64, :].astype(F32)
        total = total + jnp.sum((part * part).reshape(8, 8, width), axis=0)
    return total


def moments(ref, total):
    count = ref.shape[0]
    sums = dot_n(jnp.ones((8, count), BF16), ref[...])[:1]
    shift = sums * (1.0 / math.sqrt(count))
    return sums, jnp.sum(total, axis=0, keepdims=True) - shift * shift, shift


def eight(*rows):
    return jnp.concatenate(list(rows) + [rows[-1]] * (8 - len(rows)), axis=0)


def halved(bit, keep_ref, send_ref, value):
    part = keep_ref.shape[0]
    for k in range(0, part, STEP):
        send_ref[k : k + STEP, :] = value(pl.multiple_of((1 - bit) * part + k, 16)).astype(BF16)
        keep_ref[k : k + STEP, :] = value(pl.multiple_of(bit * part + k, 16))


def own_gram_kernel(pos_ref, own_ref, keep_ref, send_ref, stats_ref, turned_ref, piece_ref, full_ref, col_ref):
    count, slab = own_ref.shape
    half = slab // 2

    @pl.when(pos_ref[0] == 0)
    def _():
        piece_ref[...] = own_ref[:, half:]

    @pl.when(pos_ref[0] != 0)
    def _():
        piece_ref[...] = own_ref[:, :half]

    turned_ref[...] = own_ref[...].T
    sums, squares, shift = moments(own_ref, squared_sums(own_ref, 0, count))
    sums = two_parts(sums)
    put_stats(stats_ref, sums, jnp.concatenate([squares, shift], axis=0))
    column_table(own_cols(shift, half), None, col_ref)
    left, right = turned_ref[:half, :], turned_ref[half:, :]
    full_ref[:, :half] = dot_n(left, own_ref[:, half:])
    row, col = index_parts(0, half, half)
    full_ref[:, half:] = jnp.where(row < col, dot_n(left, own_ref[:, :half]), dot_n(right, own_ref[:, half:]))
    cols = own_cols(shift, half)

    def value(start):
        rows = table_rows(col_ref, start, (0, 1), half)
        products = own_products(rows, cols, *index_parts(start, STEP, half))
        return full_ref[pl.ds(start, STEP), :] - jnp.concatenate(products, axis=1)

    halved(pos_ref[3], keep_ref, send_ref, value)
    send_ref[keep_ref.shape[0] :, :] = coded(sums, squares)


def cross_gram_kernel(pos_ref, turned_ref, there_ref, own_stats_ref, keep_ref, send_ref, stats_ref, full_ref, col_ref, side_ref):
    half = there_ref.shape[1]
    quarter = half // 2
    core = pos_ref[0]
    first = core == 0
    row, col = index_parts(0, half, half)

    @pl.when(first)
    def _():
        full_ref[:, :half] = dot_n(turned_ref[:half, :], there_ref[...])
        full_ref[:, half:] = pltpu.roll(dot_n(turned_ref[half:, :], there_ref[...]), quarter, 1)

    @pl.when(jnp.logical_not(first))
    def _():
        side_ref[...] = there_ref[...].T
        full_ref[:, :half] = dot_t(side_ref[...], turned_ref[half:, :])
        full_ref[:, half:] = dot_t(side_ref[...], turned_ref[:half, :])

    sums, squares, shift = moments(there_ref, squared_sums(there_ref, 0, there_ref.shape[0]))
    shift = jnp.concatenate([own_stats_ref[list_rows(1) + 1 : list_rows(1) + 2, :], shift], axis=1)
    column_table(cross_vectors(shift, first, half), None, col_ref)
    a_shift, b_shift = cross_halves(shift, first, half)
    straight = full_ref[:, :half]
    level = jnp.sum(jnp.where(row == col, straight, 0.0), axis=0, keepdims=True) - a_shift * b_shift
    sums = two_parts(sums)
    exact = jnp.concatenate([squares, level], axis=0)
    put_stats(stats_ref, sums, exact)
    send_ref[keep_ref.shape[0] :, :] = coded(sums, exact)
    corner = full_ref[half - 256 : half, half - 256 : half].T[256 - quarter :, :]
    corner = pltpu.roll(corner, quarter, 1)[:, :quarter]
    corner = jnp.concatenate([corner, corner], axis=0)
    folded = jnp.concatenate([corner, jnp.zeros((half, half - quarter), F32)], axis=1)
    apart = full_ref[:, half:]
    full_ref[:, :half] = jnp.where(col < quarter, jnp.where(row > col, straight, folded), apart)
    cols = cross_cols(shift, first, half)

    def value(start):
        rows = table_rows(col_ref, start, (0, 1, 2), half)
        products = cross_products(rows, cols, *index_parts(start, STEP, half))
        return full_ref[pl.ds(start, STEP), :half] - products

    halved(pos_ref[3], keep_ref, send_ref, value)


def merge_kernel(pos_ref, kept_ref, msg_ref, stats_ref, *refs, rows_in, bits, many, exact, split):
    keep_ref = refs[-3] if split else None
    send_ref, out_ref = refs[-2:]
    rows = rows_in

    def value(offset):
        here = pl.ds(offset, STEP)
        return kept_ref[here, :].astype(F32) + msg_ref[here, :].astype(F32)

    if split:
        halved(pos_ref[bits[1]], keep_ref, send_ref, value)
        done = keep_ref.shape[0]
    else:
        done = rows
        for k in range(0, rows, STEP):
            send_ref[k : k + STEP, :] = value(k).astype(BF16)
    sums, more = merged(pos_ref[bits[0]], msg_ref, stats_ref, rows, many, exact)
    put_stats(out_ref, sums, more)
    send_ref[done:, :] = coded(sums, more)


def deviations(sums, samples):
    mean = jnp.sum(sums, axis=0, keepdims=True) * (1.0 / sums.shape[0])
    return (sums - mean) * (1.0 / math.sqrt(samples))


def outer_sums(left, right):
    (l_high, l_low), (r_high, r_low) = high_low(left), high_low(right)
    left = jnp.concatenate([l_high, l_high, l_low], axis=0)
    right = jnp.concatenate([r_high, r_low, r_high], axis=0)
    return lax.dot_general(left, right, (((0,), (0,)), ((), ())), preferred_element_type=F32)


def from_row(vec, start):
    half = vec.shape[1]
    return pltpu.roll(vec, lax.rem(half - start, half), 1)[:, :128]


def unbiased(correl, everyone):
    squared = correl * correl
    return squared - (1.0 - squared) * (1.0 / (everyone - 2.0))


def placed_at(rows_part, offset, half):
    blank = jnp.zeros((rows_part.shape[0], half - rows_part.shape[1]), F32)
    return pltpu.roll(jnp.concatenate([rows_part, blank], axis=1), offset, 1)


def own_score_kernel(
    pos_ref, kept_ref, msg_ref, stats_ref, limit_ref, flag_ref, sub_ref,
    out_ref, vec_ref, col_ref, one_ref, two_ref, *, bit, many, samples,
):
    rows = one_ref.shape[0]
    half = kept_ref.shape[1] // 2
    everyone = 2.0 * many * samples
    base = pos_ref[2]
    sums, squares = merged(pos_ref[bit], msg_ref, stats_ref, rows, many, 1)
    apart = deviations(sums, samples)
    squares = squares + jnp.sum(apart * apart, axis=0, keepdims=True)
    scale = 1.0 / jnp.sqrt(squares * (1.0 / everyone) + VAR_EPS)
    put_stats(vec_ref, apart, scale)
    scales = own_cols(scale, half)
    factors = own_cols(scale * (1.0 / everyone), half) + (limit_ref[:1, :half],)
    column_table(factors, base, col_ref)
    left, right = own_cols(apart, half)
    l_rows = from_row(left, base)
    products = outer_sums(l_rows, right), outer_sums(l_rows, left), outer_sums(from_row(right, base), right)
    right_lim = limit_ref[:1, half : 2 * half]
    for k in range(0, rows, STEP):
        start = base + k
        row, col = index_parts(start, STEP, half)
        l_scale, r_scale, left_lim = table_rows(col_ref, k, range(3), half)
        one, upper, lower = (x[k : k + STEP] for x in products)
        shifts = one, jnp.where(row < col, upper, lower)
        norms = own_products((l_scale, r_scale), scales, row, col)
        gaps = (half + col - row, jnp.where(row == col, 8 * half, jnp.abs(row - col)))
        lims = (left_lim, jnp.where(row < col, left_lim, right_lim))
        for s, ref in ((0, one_ref), (1, two_ref)):
            here = slice(s * half, (s + 1) * half)
            value = kept_ref[k : k + STEP, here].astype(F32) + msg_ref[k : k + STEP, here].astype(F32)
            weight = unbiased((value + shifts[s]) * norms[s], everyone)
            ref[k : k + STEP, :] = jnp.where(gaps[s].astype(F32) <= lims[s], weight, 0.0).astype(BF16)
    row, col = index_parts(base, rows, half)
    one, two = one_ref[...], two_ref[...]
    zero = jnp.zeros_like(two)
    upper, lower = jnp.where(row < col, two, zero), jnp.where(row > col, two, zero)
    f_left, f_right = flag_ref[:, :half], flag_ref[:, half : 2 * half]
    s_left, s_right = sub_ref[:, :rows], sub_ref[:, 128 : 128 + rows]
    out_ref[:, :half] = dot_n(s_left, upper) + placed_at(dot_t(f_right, one) + dot_t(f_left, upper), base, half)
    out_ref[:, half:] = dot_n(s_left, one) + dot_n(s_right, lower) + placed_at(dot_t(f_right, lower), base, half)


def cross_score_kernel(
    pos_ref, kept_ref, msg_ref, stats_ref, vec_ref, limit_ref, flag_ref, sub_ref, own_ref,
    out_ref, col_ref, three_ref, *, bit, many, samples,
):
    rows = three_ref.shape[0]
    half = kept_ref.shape[1]
    quarter = half // 2
    core = pos_ref[0]
    first = core == 0
    everyone = 2.0 * many * samples
    base = pos_ref[2]
    sums, exact = merged(pos_ref[bit], msg_ref, stats_ref, rows, many, 2)
    apart = deviations(sums, samples)
    squares = exact[:1] + jnp.sum(apart * apart, axis=0, keepdims=True)
    place = list_rows(2 * many)
    apart = jnp.concatenate([vec_ref[: 2 * many, :], apart], axis=1)
    a_apart, b_apart = cross_halves(apart, first, half)
    level = exact[1:2] + jnp.sum(a_apart * b_apart, axis=0, keepdims=True)
    scale = 1.0 / jnp.sqrt(squares * (1.0 / everyone) + VAR_EPS)
    scale = jnp.concatenate([vec_ref[place : place + 1, :], scale], axis=1)
    limit = limit_ref[:1, :]
    factors = cross_vectors(scale * (1.0 / everyone), first, half)
    column_table(factors + cross_vectors(limit, first, half)[:2], base, col_ref)
    scales = cross_cols(scale, first, half)
    there = apart[:, 2 * half :]
    a2_apart = pick(first, apart[:, half : 2 * half], there)
    b3_apart = pick(first, pltpu.roll(there, quarter, 1), apart[:, :half])
    late_a, late_b = pltpu.roll(a_apart, quarter, 1), pltpu.roll(b_apart, quarter, 1)
    shifts = (
        outer_sums(from_row(a_apart, base), b_apart),
        outer_sums(from_row(late_b, base), late_a),
        outer_sums(from_row(a2_apart, base), b3_apart),
    )
    _, late_lim, _ = cross_cols(limit, first, half)
    for k in range(0, rows, STEP):
        start = base + k
        row, col = index_parts(start, STEP, half)
        fold = col < quarter
        parts = table_rows(col_ref, k, range(5), half)
        a_lim, a2_lim = parts[3:]
        straight, late, apart = (x[k : k + STEP] for x in shifts)
        products = jnp.where(fold, jnp.where(row > col, straight, late), apart)
        norms = cross_products(parts[:3], scales, row, col)
        lims = jnp.where(fold, jnp.where(row > col, a_lim, late_lim), a2_lim)
        near = jnp.where(row == col, 8 * half, 2 * half - jnp.abs(row - col))
        gaps = jnp.where(fold, near, quarter + quarter * core + col - row)
        value = kept_ref[k : k + STEP, :].astype(F32) + msg_ref[k : k + STEP, :].astype(F32)
        weight = unbiased((value + products) * norms, everyone)
        three_ref[k : k + STEP, :] = jnp.where(gaps.astype(F32) <= lims, weight, 0.0).astype(BF16)
    a_scale, b_scale = cross_halves(scale, first, half)
    a_limit, _ = cross_halves(limit, first, half)
    lane = lax.broadcasted_iota(jnp.int32, (1, half), 1)
    level = unbiased(level * (1.0 / everyone) * a_scale * b_scale, everyone)
    mine = (lane >= base) & (lane < base + rows) & (a_limit >= 2.0 * half)
    level = jnp.where(mine, level, 0.0)
    row, col = index_parts(base, rows, half)
    three = three_ref[...]
    zero = jnp.zeros_like(three)
    fold = col < quarter
    straight = jnp.where(fold & (row > col), three, zero)
    folded = jnp.where(fold & (row < col), three, zero)
    apart = jnp.where(fold, zero, three)
    f_a, f_b = flag_ref[:, :half], flag_ref[:, half : 2 * half]
    f_late, f_b3 = flag_ref[:, 2 * half : 3 * half], flag_ref[:, 3 * half :]
    s_a, s_a2, s_late = sub_ref[:, 256 : 256 + rows], sub_ref[:, 384 : 384 + rows], sub_ref[:, 512 : 512 + rows]
    out_a = placed_at(dot_t(f_b, straight), base, half) + pltpu.roll(dot_n(s_late, folded), quarter, 1)
    out_b = dot_n(s_a, straight) + placed_at(dot_t(f_late, folded), lax.rem(base + quarter, half), half)
    out_a = out_a + f_b.astype(F32) * level
    out_b = out_b + f_a.astype(F32) * level
    out_a2 = placed_at(dot_t(f_b3, apart), base, half)
    out_b3 = dot_n(s_a2, apart)
    out_ref[:, :half] = own_ref[:, :half] + pick(first, out_a, out_b3)
    out_ref[:, half : 2 * half] = own_ref[:, half:] + pick(first, out_a2, out_b)
    out_ref[:, 2 * half :] = pick(first, out_b + pltpu.roll(out_b3, quarter, 1), out_a + out_a2)


def local_kernel(pos_ref, annot_ref, chrom_ref, reach_ref, ids_ref, flag_ref, cross_ref, sub_ref, limit_ref, hot_ref):
    half = annot_ref.shape[1] // 4
    first = pos_ref[0] == 0
    base = pos_ref[2]
    flags = annot_ref[...].astype(F32)

    def quarters(x):
        return [x[:, k * half : (k + 1) * half] for k in range(4)]

    def local(x):
        one, two, three, four = quarters(x)
        return pick(first, one, three), pick(first, two, four), pick(first, three, two)

    left, right, there = local(flags)
    for k, x in enumerate((left, right, there)):
        flag_ref[:, k * half : (k + 1) * half] = x.astype(BF16)
    a_cols, b_cols, a2_cols = pick(first, left, there), pick(first, there, right), pick(first, right, there)
    b3_cols = pick(first, pltpu.roll(there, half // 2, 1), left)
    for k, x in enumerate((a_cols, b_cols, pltpu.roll(a_cols, half // 2, 1), b3_cols)):
        cross_ref[:, k * half : (k + 1) * half] = x.astype(BF16)
    back = lax.rem(half - base, half)
    late = lax.rem(half + half // 2 - base, half)
    for k, (x, turn) in enumerate(((left, back), (right, back), (a_cols, back), (a2_cols, back), (b_cols, late))):
        sub_ref[:, k * 128 : (k + 1) * 128] = pltpu.roll(x, turn, 1)[:, :128].astype(BF16)

    def line(ref):
        return jnp.concatenate([ref[k : k + 1, :] for k in range(ref.shape[0])], axis=1).astype(F32)

    chrom, reach = line(chrom_ref), line(reach_ref)
    ends = [jnp.sum((chrom <= k).astype(F32), axis=1, keepdims=True) for k in (1, 2, 3)]
    last = jnp.where(chrom == 1, ends[0], jnp.where(chrom == 2, ends[1], ends[2]))
    place = lax.broadcasted_iota(jnp.int32, chrom.shape, 1).astype(F32)
    limit = jnp.concatenate(local(jnp.minimum(reach, last - 1.0 - place)), axis=1)
    limit_ref[...] = jnp.broadcast_to(limit, limit_ref.shape)
    block = jnp.concatenate(local(line(ids_ref)), axis=1)
    tall = jnp.broadcast_to(block, (128, block.shape[1]))
    for k in range(block.shape[1] // 128):
        rows = tall[:, k * 128 : (k + 1) * 128].T
        for n in range(hot_ref.shape[1] // 128):
            number = (lax.broadcasted_iota(jnp.int32, rows.shape, 1) + n * 128).astype(F32)
            hot_ref[k * 128 : (k + 1) * 128, n * 128 : (n + 1) * 128] = jnp.where(number == rows, 1.0, 0.0).astype(BF16)


def block_kernel(pos_ref, score_ref, flag_ref, hot_ref, sum_ref):
    slab = flag_ref.shape[1] // 3 * 2
    hot = hot_ref[...]
    own = score_ref[:, :slab] + flag_ref[:, :slab].astype(F32)
    scores = jnp.concatenate([own, score_ref[:, slab:]], axis=1)
    high = scores.astype(BF16)
    left = scores - high.astype(F32)
    sum_ref[...] = (dot_n(high, hot) + dot_n(left.astype(BF16), hot)).T[: sum_ref.shape[0], :]


def call(kernel, inputs, outputs, scratch, flops, moved):
    vmem = pl.BlockSpec(memory_space=pltpu.VMEM)
    smem = pl.BlockSpec(memory_space=pltpu.SMEM)
    return pl.pallas_call(
        kernel,
        out_shape=outputs,
        in_specs=[smem] + [vmem] * (len(inputs) - 1),
        out_specs=jax.tree.map(lambda _: vmem, outputs),
        scratch_shapes=scratch,
        compiler_params=pltpu.CompilerParams(vmem_limit_bytes=VMEM_LIMIT),
        cost_estimate=pl.CostEstimate(flops=flops, bytes_accessed=moved, transcendentals=0),
    )(*inputs)


def body(genotypes, chromosome, blocks, annotation, reach):
    count, slab = genotypes.shape
    half = slab // 2
    quarter = half // 2
    width = 3 * half
    snps = chromosome.shape[0]
    parts = lax.axis_size("samples")
    bits = parts.bit_length() - 1
    core = lax.axis_index("genome")
    place = lax.axis_index("samples")
    order = [first + list(range(3, bits)) for first in ORDERS]
    bit_at = [(place >> jnp.where(core == 0, order[0][t], order[1][t])) & 1 for t in range(bits)]

    def exchange(x, t, order=order):
        route = []
        for s in range(parts):
            for g in range(2):
                route.append((s * 2 + g, (s ^ (1 << order[g][t])) * 2 + g))
        return lax.ppermute(x, ("samples", "genome"), route)

    def across(x):
        return lax.ppermute(x, "genome", [(0, 1), (1, 0)])

    def shape(rows, cols, dtype):
        return jax.ShapeDtypeStruct((rows, cols), dtype)

    base = bit_at[0] * quarter + bit_at[1] * (quarter // 2)
    rows = quarter // 2

    where = jnp.stack([core, place, base] + bit_at).astype(jnp.int32)
    annot = annotation.shape[0]

    hot_rows = -(-NBLK // 8) * 8

    def tiles(x):
        return x.reshape(-1, 128)

    flags, flags_cross, subs, limit, hot = call(
        local_kernel,
        (where, annotation, tiles(chromosome), tiles(reach), tiles(blocks)),
        (
            shape(annot, width, BF16),
            shape(annot, 4 * half, BF16),
            shape(annot, 5 * 128, BF16),
            shape(8, width, F32),
            shape(width, -(-hot_rows // 128) * 128, BF16),
        ),
        [],
        annot * snps * 10,
        annot * snps * 8,
    )
    def table_of(vectors, count):
        return pltpu.VMEM((vectors, -(-count // 128) * 128, 128), F32)

    def outputs(kept, sent, cols, many, exact):
        kept_shape = (shape(kept, cols, F32),) if kept else ()
        coded_shape = shape(sent + coded_rows(many, exact), cols, BF16)
        return kept_shape + (coded_shape, shape(list_rows(many) + 8, cols, F32))

    keep_a, send_a, stats_a, turned, piece = call(
        own_gram_kernel,
        (where, genotypes),
        outputs(quarter, quarter, slab, 1, 1)
        + (shape(slab, count, BF16), shape(count, half, BF16)),
        [pltpu.VMEM((half, slab), F32), table_of(2, half)],
        2 * count * half * half * 3,
        count * slab * 2,
    )
    there = across(piece)
    msg_a = exchange(send_a, 0)
    keep_b, send_b, stats_b = call(
        cross_gram_kernel,
        (where, turned, there, stats_a),
        outputs(quarter, quarter, half, 1, 2),
        [pltpu.VMEM((half, slab), F32), table_of(3, half), pltpu.VMEM((half, count), BF16)],
        2 * count * half * half * 3,
        count * slab * 2,
    )
    msg_b = exchange(send_b, 0)

    def merge(keep, msg, stats, cols, t, exact, *after):
        split = t == 1
        *kept, send, stats = call(
            functools.partial(merge_kernel, rows_in=quarter if split else rows, bits=(2 + t, 3 + t), many=1 << (t - 1), exact=exact, split=split),
            (where, keep, msg, stats) + after,
            outputs(rows if split else 0, rows, cols, 1 << t, exact),
            [],
            rows * cols * 8,
            rows * cols * 20,
        )
        return (kept[0] if split else send), send, stats

    for t in range(1, bits):
        if t == 1:
            msg_a, send_b = lax.optimization_barrier((msg_a, send_b))
        keep_a, send_a, stats_a = merge(keep_a, msg_a, stats_a, slab, t, 1)
        msg_a = exchange(send_a, t)
        keep_b, send_b, stats_b = merge(keep_b, msg_b, stats_b, half, t, 2, stats_a)
        msg_b = exchange(send_b, t)
    last = {"bit": 2 + bits, "many": parts // 2, "samples": float(count)}
    scores_a, vectors = call(
        functools.partial(own_score_kernel, **last),
        (where, keep_a, msg_a, stats_a, limit, flags, subs),
        (shape(annot, slab, F32), shape(list_rows(parts) + 8, slab, F32)),
        [table_of(3, rows)] + [pltpu.VMEM((rows, half), BF16)] * 2,
        2 * annot * half * rows * 8,
        rows * slab * 20,
    )
    partial = call(
        functools.partial(cross_score_kernel, **last),
        (where, keep_b, msg_b, stats_b, vectors, limit, flags_cross, subs, scores_a),
        shape(annot, width, F32),
        [table_of(5, rows)] + [pltpu.VMEM((rows, half), BF16)],
        2 * annot * half * rows * 8,
        rows * slab * 20,
    )
    for t in range(2):
        rounded = partial.astype(jnp.float16)
        partial = rounded.astype(F32) + exchange(rounded, t, ROUNDS).astype(F32)
    arrived = across(partial[:, slab:])
    sums = call(
        block_kernel,
        (where, partial, flags, hot),
        shape(hot_rows, annot, F32),
        [],
        2 * annot * width * hot_rows * 2,
        annot * width * 8,
    )
    nothing = jnp.zeros_like(arrived)
    ld_scores = (partial[:, :slab] + flags[:, :slab].astype(F32)) + jnp.where(
        core == 0,
        jnp.concatenate([nothing, arrived], axis=1),
        jnp.concatenate([arrived, nothing], axis=1),
    )
    sums_there = across(sums)
    sums, ld_scores = lax.optimization_barrier((sums, ld_scores))
    return (ld_scores, (sums + sums_there)[:NBLK].T)


def solution(mesh):
    placed = (
        P(("groups", "samples"), "genome"),
        P("groups"),
        P("groups"),
        P(None, "groups"),
        P("groups"),
    )
    return jax.shard_map(
        body,
        mesh=mesh,
        in_specs=placed,
        out_specs=(P(None, ("groups", "genome")), P(None, "groups")),
        check_vma=False,
    )
```

```python
import functools
import math

import jax
import jax.numpy as jnp
from jax import lax
from jax.experimental import pallas as pl
from jax.experimental.pallas import tpu as pltpu
from jax.sharding import PartitionSpec as P

NBLK = 200
VAR_EPS = 1e-06
F32 = jnp.float32
BF16 = jnp.bfloat16
ORDERS = [[0, 1, 2], [1, 2, 0]]
ROUNDS = [[0, 1], [2, 1]]
VMEM_LIMIT = 20 * 1024 * 1024


STEP = 48


def pick(first, one, other):
    return jnp.where(first, one, other)


def index_parts(start, count, half):
    row = lax.broadcasted_iota(jnp.int32, (count, half), 0) + start
    col = lax.broadcasted_iota(jnp.int32, (count, half), 1)
    return row, col


def column_table(vectors, start, ref):
    table = eight(*vectors)
    half = table.shape[1]
    if start is not None:
        table = pltpu.roll(table, lax.rem(half - start, half), 1)
    for n in range(len(vectors)):
        for k in range(ref.shape[1] // 128):
            here = slice(k * 128, (k + 1) * 128)
            ref[n, here, :] = jnp.broadcast_to(table[n : n + 1, here], (128, 128)).T


def table_rows(ref, offset, columns, half):
    here = pl.ds(pl.multiple_of(offset, 16), STEP)
    return tuple(jnp.concatenate([ref[n, here, :]] * (half // 128), axis=1) for n in columns)


def high_low(values):
    high = values.astype(BF16)
    return high, (values - high.astype(F32)).astype(BF16)


def coded(sums, exact):
    high, low = high_low(sums)
    first, left = high_low(exact)
    third = (exact - first.astype(F32) - left.astype(F32)).astype(BF16)
    rows = coded_rows(sums.shape[0], exact.shape[0])
    gap = rows - 2 * sums.shape[0] - 3 * exact.shape[0]
    blank = [jnp.zeros((gap, sums.shape[1]), BF16)] if gap else []
    return jnp.concatenate([high, low, first, left, third] + blank, axis=0)


def coded_rows(many, exact):
    return -(-(2 * many + 3 * exact) // (24 * exact - 16)) * (24 * exact - 16)


def decoded(rows, many, exact):
    parts = rows.astype(F32)
    sums = parts[:many] + parts[many : 2 * many]
    at = 2 * many
    return sums, parts[at : at + exact] + parts[at + exact : at + 2 * exact] + parts[at + 2 * exact : at + 3 * exact]


def list_rows(many):
    return -(-many // 8) * 8


def put_stats(ref, sums, exact):
    many, width = sums.shape
    gap = list_rows(many) - many
    rows = [sums] + ([jnp.zeros((gap, width), F32)] if gap else [])
    rows = rows + [exact, jnp.zeros((8 - exact.shape[0], width), F32)]
    ref[...] = jnp.concatenate(rows, axis=0)


def merged(bit, msg_ref, stats_ref, rows, many, exact):
    theirs, added = decoded(msg_ref[rows:, :], many, exact)
    mine = stats_ref[:many, :]
    place = list_rows(many)
    both = pick(
        bit == 0, jnp.concatenate([mine, theirs], axis=0), jnp.concatenate([theirs, mine], axis=0)
    )
    return both, stats_ref[place : place + exact, :] + added


def two_parts(values):
    high, low = high_low(values)
    return high.astype(F32) + low.astype(F32)


def own_cols(vec, half):
    return vec[:, :half], vec[:, half : 2 * half]


def own_products(rows, cols, row, col):
    (l_rows, r_rows), (left, right) = rows, cols
    return l_rows * right, jnp.where(row < col, l_rows * left, r_rows * right)


def cross_halves(vec, first, half):
    left, right, there = vec[:, :half], vec[:, half : 2 * half], vec[:, 2 * half :]
    return pick(first, left, there), pick(first, there, right)


def cross_cols(vec, first, half):
    vec = jnp.broadcast_to(vec, (8, vec.shape[1]))
    a_cols, b_cols = cross_halves(vec, first, half)
    a_turned = pltpu.roll(a_cols, half // 2, 1)
    b3_cols = pick(first, pltpu.roll(vec[:, 2 * half :], half // 2, 1), vec[:, :half])
    return b_cols[:1], a_turned[:1], b3_cols[:1]


def cross_vectors(vec, first, half):
    a_cols, b_cols = cross_halves(vec, first, half)
    a2_cols = pick(first, vec[:, half : 2 * half], vec[:, 2 * half :])
    b_late = pltpu.roll(jnp.broadcast_to(b_cols, (8, half)), half // 2, 1)[:1]
    return a_cols, a2_cols, b_late


def cross_products(rows, cols, row, col):
    (a_rows, a2_rows, b_rows), (c_b, c_a, c_b3) = rows, cols
    half = row.shape[1]
    return jnp.where(
        col < half // 2, jnp.where(row > col, a_rows * c_b, b_rows * c_a), a2_rows * c_b3
    )


def dot_n(left, right):
    return lax.dot_general(left, right, (((1,), (0,)), ((), ())), preferred_element_type=F32)


def dot_t(left, right):
    return lax.dot_general(left, right, (((1,), (1,)), ((), ())), preferred_element_type=F32)


def squared_sums(ref, start, stop):
    width = ref.shape[1]
    total = jnp.zeros((8, width), F32)
    for k in range(start, stop, 64):
        part = ref[k : k + 64, :].astype(F32)
        total = total + jnp.sum((part * part).reshape(8, 8, width), axis=0)
    return total


def moments(ref, total):
    count = ref.shape[0]
    sums = dot_n(jnp.ones((8, count), BF16), ref[...])[:1]
    shift = sums * (1.0 / math.sqrt(count))
    return sums, jnp.sum(total, axis=0, keepdims=True) - shift * shift, shift


def eight(*rows):
    return jnp.concatenate(list(rows) + [rows[-1]] * (8 - len(rows)), axis=0)


def halved(bit, keep_ref, send_ref, value):
    part = keep_ref.shape[0]
    for k in range(0, part, STEP):
        send_ref[k : k + STEP, :] = value(pl.multiple_of((1 - bit) * part + k, 16)).astype(BF16)
        keep_ref[k : k + STEP, :] = value(pl.multiple_of(bit * part + k, 16))


def own_gram_kernel(pos_ref, own_ref, keep_ref, send_ref, stats_ref, turned_ref, piece_ref, full_ref, col_ref):
    count, slab = own_ref.shape
    half = slab // 2

    @pl.when(pos_ref[0] == 0)
    def _():
        piece_ref[...] = own_ref[:, half:]

    @pl.when(pos_ref[0] != 0)
    def _():
        piece_ref[...] = own_ref[:, :half]

    turned_ref[...] = own_ref[...].T
    sums, squares, shift = moments(own_ref, squared_sums(own_ref, 0, count))
    sums = two_parts(sums)
    put_stats(stats_ref, sums, jnp.concatenate([squares, shift], axis=0))
    column_table(own_cols(shift, half), None, col_ref)
    left, right = turned_ref[:half, :], turned_ref[half:, :]
    full_ref[:, :half] = dot_n(left, own_ref[:, half:])
    row, col = index_parts(0, half, half)
    full_ref[:, half:] = jnp.where(row < col, dot_n(left, own_ref[:, :half]), dot_n(right, own_ref[:, half:]))
    cols = own_cols(shift, half)

    def value(start):
        rows = table_rows(col_ref, start, (0, 1), half)
        products = own_products(rows, cols, *index_parts(start, STEP, half))
        return full_ref[pl.ds(start, STEP), :] - jnp.concatenate(products, axis=1)

    halved(pos_ref[3], keep_ref, send_ref, value)
    send_ref[keep_ref.shape[0] :, :] = coded(sums, squares)


def cross_gram_kernel(pos_ref, turned_ref, there_ref, own_stats_ref, keep_ref, send_ref, stats_ref, full_ref, col_ref, side_ref):
    half = there_ref.shape[1]
    quarter = half // 2
    core = pos_ref[0]
    first = core == 0
    row, col = index_parts(0, half, half)

    @pl.when(first)
    def _():
        full_ref[:, :half] = dot_n(turned_ref[:half, :], there_ref[...])
        full_ref[:, half:] = pltpu.roll(dot_n(turned_ref[half:, :], there_ref[...]), quarter, 1)

    @pl.when(jnp.logical_not(first))
    def _():
        side_ref[...] = there_ref[...].T
        full_ref[:, :half] = dot_t(side_ref[...], turned_ref[half:, :])
        full_ref[:, half:] = dot_t(side_ref[...], turned_ref[:half, :])

    sums, squares, shift = moments(there_ref, squared_sums(there_ref, 0, there_ref.shape[0]))
    shift = jnp.concatenate([own_stats_ref[list_rows(1) + 1 : list_rows(1) + 2, :], shift], axis=1)
    column_table(cross_vectors(shift, first, half), None, col_ref)
    a_shift, b_shift = cross_halves(shift, first, half)
    straight = full_ref[:, :half]
    level = jnp.sum(jnp.where(row == col, straight, 0.0), axis=0, keepdims=True) - a_shift * b_shift
    sums = two_parts(sums)
    exact = jnp.concatenate([squares, level], axis=0)
    put_stats(stats_ref, sums, exact)
    send_ref[keep_ref.shape[0] :, :] = coded(sums, exact)
    corner = full_ref[half - 256 : half, half - 256 : half].T[256 - quarter :, :]
    corner = pltpu.roll(corner, quarter, 1)[:, :quarter]
    corner = jnp.concatenate([corner, corner], axis=0)
    folded = jnp.concatenate([corner, jnp.zeros((half, half - quarter), F32)], axis=1)
    apart = full_ref[:, half:]
    full_ref[:, :half] = jnp.where(col < quarter, jnp.where(row > col, straight, folded), apart)
    cols = cross_cols(shift, first, half)

    def value(start):
        rows = table_rows(col_ref, start, (0, 1, 2), half)
        products = cross_products(rows, cols, *index_parts(start, STEP, half))
        return full_ref[pl.ds(start, STEP), :half] - products

    halved(pos_ref[3], keep_ref, send_ref, value)


def merge_kernel(pos_ref, kept_ref, msg_ref, stats_ref, *refs, rows_in, bits, many, exact, split):
    keep_ref = refs[-3] if split else None
    send_ref, out_ref = refs[-2:]
    rows = rows_in

    def value(offset):
        here = pl.ds(offset, STEP)
        return kept_ref[here, :].astype(F32) + msg_ref[here, :].astype(F32)

    if split:
        halved(pos_ref[bits[1]], keep_ref, send_ref, value)
        done = keep_ref.shape[0]
    else:
        done = rows
        for k in range(0, rows, STEP):
            send_ref[k : k + STEP, :] = value(k).astype(BF16)
    sums, more = merged(pos_ref[bits[0]], msg_ref, stats_ref, rows, many, exact)
    put_stats(out_ref, sums, more)
    send_ref[done:, :] = coded(sums, more)


def deviations(sums, samples):
    mean = jnp.sum(sums, axis=0, keepdims=True) * (1.0 / sums.shape[0])
    return (sums - mean) * (1.0 / math.sqrt(samples))


def outer_sums(left, right):
    (l_high, l_low), (r_high, r_low) = high_low(left), high_low(right)
    left = jnp.concatenate([l_high, l_high, l_low], axis=0)
    right = jnp.concatenate([r_high, r_low, r_high], axis=0)
    return lax.dot_general(left, right, (((0,), (0,)), ((), ())), preferred_element_type=F32)


def from_row(vec, start):
    half = vec.shape[1]
    return pltpu.roll(vec, lax.rem(half - start, half), 1)[:, :128]


def unbiased(correl, everyone):
    squared = correl * correl
    return squared - (1.0 - squared) * (1.0 / (everyone - 2.0))


def placed_at(rows_part, offset, half):
    blank = jnp.zeros((rows_part.shape[0], half - rows_part.shape[1]), F32)
    return pltpu.roll(jnp.concatenate([rows_part, blank], axis=1), offset, 1)


def own_score_kernel(
    pos_ref, kept_ref, msg_ref, stats_ref, limit_ref, flag_ref, sub_ref,
    out_ref, vec_ref, col_ref, one_ref, two_ref, *, bit, many, samples,
):
    rows = one_ref.shape[0]
    half = kept_ref.shape[1] // 2
    everyone = 2.0 * many * samples
    base = pos_ref[2]
    sums, squares = merged(pos_ref[bit], msg_ref, stats_ref, rows, many, 1)
    apart = deviations(sums, samples)
    squares = squares + jnp.sum(apart * apart, axis=0, keepdims=True)
    scale = 1.0 / jnp.sqrt(squares * (1.0 / everyone) + VAR_EPS)
    put_stats(vec_ref, apart, scale)
    scales = own_cols(scale, half)
    factors = own_cols(scale * (1.0 / everyone), half) + (limit_ref[:1, :half],)
    column_table(factors, base, col_ref)
    left, right = own_cols(apart, half)
    l_rows = from_row(left, base)
    products = outer_sums(l_rows, right), outer_sums(l_rows, left), outer_sums(from_row(right, base), right)
    right_lim = limit_ref[:1, half : 2 * half]
    for k in range(0, rows, STEP):
        start = base + k
        row, col = index_parts(start, STEP, half)
        l_scale, r_scale, left_lim = table_rows(col_ref, k, range(3), half)
        one, upper, lower = (x[k : k + STEP] for x in products)
        shifts = one, jnp.where(row < col, upper, lower)
        norms = own_products((l_scale, r_scale), scales, row, col)
        gaps = (half + col - row, jnp.where(row == col, 8 * half, jnp.abs(row - col)))
        lims = (left_lim, jnp.where(row < col, left_lim, right_lim))
        for s, ref in ((0, one_ref), (1, two_ref)):
            here = slice(s * half, (s + 1) * half)
            value = kept_ref[k : k + STEP, here].astype(F32) + msg_ref[k : k + STEP, here].astype(F32)
            weight = unbiased((value + shifts[s]) * norms[s], everyone)
            ref[k : k + STEP, :] = jnp.where(gaps[s].astype(F32) <= lims[s], weight, 0.0).astype(BF16)
    row, col = index_parts(base, rows, half)
    one, two = one_ref[...], two_ref[...]
    zero = jnp.zeros_like(two)
    upper, lower = jnp.where(row < col, two, zero), jnp.where(row > col, two, zero)
    f_left, f_right = flag_ref[:, :half], flag_ref[:, half : 2 * half]
    s_left, s_right = sub_ref[:, :rows], sub_ref[:, 128 : 128 + rows]
    out_ref[:, :half] = dot_n(s_left, upper) + placed_at(dot_t(f_right, one) + dot_t(f_left, upper), base, half)
    out_ref[:, half:] = dot_n(s_left, one) + dot_n(s_right, lower) + placed_at(dot_t(f_right, lower), base, half)


def cross_score_kernel(
    pos_ref, kept_ref, msg_ref, stats_ref, vec_ref, limit_ref, flag_ref, sub_ref, own_ref,
    out_ref, col_ref, three_ref, *, bit, many, samples,
):
    rows = three_ref.shape[0]
    half = kept_ref.shape[1]
    quarter = half // 2
    core = pos_ref[0]
    first = core == 0
    everyone = 2.0 * many * samples
    base = pos_ref[2]
    sums, exact = merged(pos_ref[bit], msg_ref, stats_ref, rows, many, 2)
    apart = deviations(sums, samples)
    squares = exact[:1] + jnp.sum(apart * apart, axis=0, keepdims=True)
    place = list_rows(2 * many)
    apart = jnp.concatenate([vec_ref[: 2 * many, :], apart], axis=1)
    a_apart, b_apart = cross_halves(apart, first, half)
    level = exact[1:2] + jnp.sum(a_apart * b_apart, axis=0, keepdims=True)
    scale = 1.0 / jnp.sqrt(squares * (1.0 / everyone) + VAR_EPS)
    scale = jnp.concatenate([vec_ref[place : place + 1, :], scale], axis=1)
    limit = limit_ref[:1, :]
    factors = cross_vectors(scale * (1.0 / everyone), first, half)
    column_table(factors + cross_vectors(limit, first, half)[:2], base, col_ref)
    scales = cross_cols(scale, first, half)
    there = apart[:, 2 * half :]
    a2_apart = pick(first, apart[:, half : 2 * half], there)
    b3_apart = pick(first, pltpu.roll(there, quarter, 1), apart[:, :half])
    late_a, late_b = pltpu.roll(a_apart, quarter, 1), pltpu.roll(b_apart, quarter, 1)
    shifts = (
        outer_sums(from_row(a_apart, base), b_apart),
        outer_sums(from_row(late_b, base), late_a),
        outer_sums(from_row(a2_apart, base), b3_apart),
    )
    _, late_lim, _ = cross_cols(limit, first, half)
    for k in range(0, rows, STEP):
        start = base + k
        row, col = index_parts(start, STEP, half)
        fold = col < quarter
        parts = table_rows(col_ref, k, range(5), half)
        a_lim, a2_lim = parts[3:]
        straight, late, apart = (x[k : k + STEP] for x in shifts)
        products = jnp.where(fold, jnp.where(row > col, straight, late), apart)
        norms = cross_products(parts[:3], scales, row, col)
        lims = jnp.where(fold, jnp.where(row > col, a_lim, late_lim), a2_lim)
        near = jnp.where(row == col, 8 * half, 2 * half - jnp.abs(row - col))
        gaps = jnp.where(fold, near, quarter + quarter * core + col - row)
        value = kept_ref[k : k + STEP, :].astype(F32) + msg_ref[k : k + STEP, :].astype(F32)
        weight = unbiased((value + products) * norms, everyone)
        three_ref[k : k + STEP, :] = jnp.where(gaps.astype(F32) <= lims, weight, 0.0).astype(BF16)
    a_scale, b_scale = cross_halves(scale, first, half)
    a_limit, _ = cross_halves(limit, first, half)
    lane = lax.broadcasted_iota(jnp.int32, (1, half), 1)
    level = unbiased(level * (1.0 / everyone) * a_scale * b_scale, everyone)
    mine = (lane >= base) & (lane < base + rows) & (a_limit >= 2.0 * half)
    level = jnp.where(mine, level, 0.0)
    row, col = index_parts(base, rows, half)
    three = three_ref[...]
    zero = jnp.zeros_like(three)
    fold = col < quarter
    straight = jnp.where(fold & (row > col), three, zero)
    folded = jnp.where(fold & (row < col), three, zero)
    apart = jnp.where(fold, zero, three)
    f_a, f_b = flag_ref[:, :half], flag_ref[:, half : 2 * half]
    f_late, f_b3 = flag_ref[:, 2 * half : 3 * half], flag_ref[:, 3 * half :]
    s_a, s_a2, s_late = sub_ref[:, 256 : 256 + rows], sub_ref[:, 384 : 384 + rows], sub_ref[:, 512 : 512 + rows]
    out_a = placed_at(dot_t(f_b, straight), base, half) + pltpu.roll(dot_n(s_late, folded), quarter, 1)
    out_b = dot_n(s_a, straight) + placed_at(dot_t(f_late, folded), lax.rem(base + quarter, half), half)
    out_a = out_a + f_b.astype(F32) * level
    out_b = out_b + f_a.astype(F32) * level
    out_a2 = placed_at(dot_t(f_b3, apart), base, half)
    out_b3 = dot_n(s_a2, apart)
    out_ref[:, :half] = own_ref[:, :half] + pick(first, out_a, out_b3)
    out_ref[:, half : 2 * half] = own_ref[:, half:] + pick(first, out_a2, out_b)
    out_ref[:, 2 * half :] = pick(first, out_b + pltpu.roll(out_b3, quarter, 1), out_a + out_a2)


def local_kernel(pos_ref, annot_ref, chrom_ref, reach_ref, ids_ref, flag_ref, cross_ref, sub_ref, limit_ref, hot_ref):
    half = annot_ref.shape[1] // 4
    first = pos_ref[0] == 0
    base = pos_ref[2]
    flags = annot_ref[...].astype(F32)

    def quarters(x):
        return [x[:, k * half : (k + 1) * half] for k in range(4)]

    def local(x):
        one, two, three, four = quarters(x)
        return pick(first, one, three), pick(first, two, four), pick(first, three, two)

    left, right, there = local(flags)
    for k, x in enumerate((left, right, there)):
        flag_ref[:, k * half : (k + 1) * half] = x.astype(BF16)
    a_cols, b_cols, a2_cols = pick(first, left, there), pick(first, there, right), pick(first, right, there)
    b3_cols = pick(first, pltpu.roll(there, half // 2, 1), left)
    for k, x in enumerate((a_cols, b_cols, pltpu.roll(a_cols, half // 2, 1), b3_cols)):
        cross_ref[:, k * half : (k + 1) * half] = x.astype(BF16)
    back = lax.rem(half - base, half)
    late = lax.rem(half + half // 2 - base, half)
    for k, (x, turn) in enumerate(((left, back), (right, back), (a_cols, back), (a2_cols, back), (b_cols, late))):
        sub_ref[:, k * 128 : (k + 1) * 128] = pltpu.roll(x, turn, 1)[:, :128].astype(BF16)

    def line(ref):
        return jnp.concatenate([ref[k : k + 1, :] for k in range(ref.shape[0])], axis=1).astype(F32)

    chrom, reach = line(chrom_ref), line(reach_ref)
    ends = [jnp.sum((chrom <= k).astype(F32), axis=1, keepdims=True) for k in (1, 2, 3)]
    last = jnp.where(chrom == 1, ends[0], jnp.where(chrom == 2, ends[1], ends[2]))
    place = lax.broadcasted_iota(jnp.int32, chrom.shape, 1).astype(F32)
    limit = jnp.concatenate(local(jnp.minimum(reach, last - 1.0 - place)), axis=1)
    limit_ref[...] = jnp.broadcast_to(limit, limit_ref.shape)
    block = jnp.concatenate(local(line(ids_ref)), axis=1)
    number = lax.broadcasted_iota(jnp.int32, hot_ref.shape, 0).astype(F32)
    hot_ref[...] = jnp.where(number == block, 1.0, 0.0).astype(BF16)


def block_kernel(pos_ref, score_ref, flag_ref, hot_ref, sum_ref):
    slab = flag_ref.shape[1] // 3 * 2
    hot = hot_ref[...]
    own = score_ref[:, :slab] + flag_ref[:, :slab].astype(F32)
    scores = jnp.concatenate([own, score_ref[:, slab:]], axis=1)
    high = scores.astype(BF16)
    left = (scores - high.astype(F32)).astype(BF16)
    gap = jnp.zeros((128 - scores.shape[0], scores.shape[1]), BF16)
    both = dot_t(hot, jnp.concatenate([high, gap, left, gap], axis=0))
    sum_ref[...] = (both[:, :128] + both[:, 128:])[:, : sum_ref.shape[1]]


def call(kernel, inputs, outputs, scratch, flops, moved):
    vmem = pl.BlockSpec(memory_space=pltpu.VMEM)
    smem = pl.BlockSpec(memory_space=pltpu.SMEM)
    return pl.pallas_call(
        kernel,
        out_shape=outputs,
        in_specs=[smem] + [vmem] * (len(inputs) - 1),
        out_specs=jax.tree.map(lambda _: vmem, outputs),
        scratch_shapes=scratch,
        compiler_params=pltpu.CompilerParams(vmem_limit_bytes=VMEM_LIMIT),
        cost_estimate=pl.CostEstimate(flops=flops, bytes_accessed=moved, transcendentals=0),
    )(*inputs)


def body(genotypes, chromosome, blocks, annotation, reach):
    count, slab = genotypes.shape
    half = slab // 2
    quarter = half // 2
    width = 3 * half
    snps = chromosome.shape[0]
    parts = lax.axis_size("samples")
    bits = parts.bit_length() - 1
    core = lax.axis_index("genome")
    place = lax.axis_index("samples")
    order = [first + list(range(3, bits)) for first in ORDERS]
    bit_at = [(place >> jnp.where(core == 0, order[0][t], order[1][t])) & 1 for t in range(bits)]

    def exchange(x, t, order=order):
        route = []
        for s in range(parts):
            for g in range(2):
                route.append((s * 2 + g, (s ^ (1 << order[g][t])) * 2 + g))
        return lax.ppermute(x, ("samples", "genome"), route)

    def across(x):
        return lax.ppermute(x, "genome", [(0, 1), (1, 0)])

    def shape(rows, cols, dtype):
        return jax.ShapeDtypeStruct((rows, cols), dtype)

    base = bit_at[0] * quarter + bit_at[1] * (quarter // 2)
    rows = quarter // 2

    where = jnp.stack([core, place, base] + bit_at).astype(jnp.int32)
    annot = annotation.shape[0]

    hot_rows = -(-NBLK // 8) * 8

    def tiles(x):
        return x.reshape(-1, 128)

    flags, flags_cross, subs, limit, hot = call(
        local_kernel,
        (where, annotation, tiles(chromosome), tiles(reach), tiles(blocks)),
        (
            shape(annot, width, BF16),
            shape(annot, 4 * half, BF16),
            shape(annot, 5 * 128, BF16),
            shape(8, width, F32),
            shape(hot_rows, width, BF16),
        ),
        [],
        annot * snps * 10,
        annot * snps * 8,
    )
    def table_of(vectors, count):
        return pltpu.VMEM((vectors, -(-count // 128) * 128, 128), F32)

    def outputs(kept, sent, cols, many, exact):
        kept_shape = (shape(kept, cols, F32),) if kept else ()
        coded_shape = shape(sent + coded_rows(many, exact), cols, BF16)
        return kept_shape + (coded_shape, shape(list_rows(many) + 8, cols, F32))

    keep_a, send_a, stats_a, turned, piece = call(
        own_gram_kernel,
        (where, genotypes),
        outputs(quarter, quarter, slab, 1, 1)
        + (shape(slab, count, BF16), shape(count, half, BF16)),
        [pltpu.VMEM((half, slab), F32), table_of(2, half)],
        2 * count * half * half * 3,
        count * slab * 2,
    )
    there = across(piece)
    msg_a = exchange(send_a, 0)
    keep_b, send_b, stats_b = call(
        cross_gram_kernel,
        (where, turned, there, stats_a),
        outputs(quarter, quarter, half, 1, 2),
        [pltpu.VMEM((half, slab), F32), table_of(3, half), pltpu.VMEM((half, count), BF16)],
        2 * count * half * half * 3,
        count * slab * 2,
    )
    msg_b = exchange(send_b, 0)

    def merge(keep, msg, stats, cols, t, exact, *after):
        split = t == 1
        *kept, send, stats = call(
            functools.partial(merge_kernel, rows_in=quarter if split else rows, bits=(2 + t, 3 + t), many=1 << (t - 1), exact=exact, split=split),
            (where, keep, msg, stats) + after,
            outputs(rows if split else 0, rows, cols, 1 << t, exact),
            [],
            rows * cols * 8,
            rows * cols * 20,
        )
        return (kept[0] if split else send), send, stats

    for t in range(1, bits):
        if t == 1:
            msg_a, send_b = lax.optimization_barrier((msg_a, send_b))
        keep_a, send_a, stats_a = merge(keep_a, msg_a, stats_a, slab, t, 1)
        msg_a = exchange(send_a, t)
        keep_b, send_b, stats_b = merge(keep_b, msg_b, stats_b, half, t, 2, stats_a)
        msg_b = exchange(send_b, t)
    last = {"bit": 2 + bits, "many": parts // 2, "samples": float(count)}
    scores_a, vectors = call(
        functools.partial(own_score_kernel, **last),
        (where, keep_a, msg_a, stats_a, limit, flags, subs),
        (shape(annot, slab, F32), shape(list_rows(parts) + 8, slab, F32)),
        [table_of(3, rows)] + [pltpu.VMEM((rows, half), BF16)] * 2,
        2 * annot * half * rows * 8,
        rows * slab * 20,
    )
    partial = call(
        functools.partial(cross_score_kernel, **last),
        (where, keep_b, msg_b, stats_b, vectors, limit, flags_cross, subs, scores_a),
        shape(annot, width, F32),
        [table_of(5, rows)] + [pltpu.VMEM((rows, half), BF16)],
        2 * annot * half * rows * 8,
        rows * slab * 20,
    )
    cut = -(-width // 256) * 128
    pieces = [partial[:, :cut], partial[:, cut:]]
    for t in range(2):
        rounded = [x.astype(jnp.float16) for x in pieces]
        pieces = [x.astype(F32) + exchange(x, t, ROUNDS).astype(F32) for x in rounded]
    partial = jnp.concatenate(pieces, axis=1)
    arrived = across(partial[:, slab:])
    sums = call(
        block_kernel,
        (where, partial, flags, hot),
        shape(hot_rows, annot, F32),
        [],
        2 * annot * width * hot_rows * 2,
        annot * width * 8,
    )
    nothing = jnp.zeros_like(arrived)
    ld_scores = (partial[:, :slab] + flags[:, :slab].astype(F32)) + jnp.where(
        core == 0,
        jnp.concatenate([nothing, arrived], axis=1),
        jnp.concatenate([arrived, nothing], axis=1),
    )
    sums_there = across(sums)
    sums, ld_scores = lax.optimization_barrier((sums, ld_scores))
    return (ld_scores, (sums + sums_there)[:NBLK].T)


def solution(mesh):
    placed = (
        P(("groups", "samples"), "genome"),
        P("groups"),
        P("groups"),
        P(None, "groups"),
        P("groups"),
    )
    return jax.shard_map(
        body,
        mesh=mesh,
        in_specs=placed,
        out_specs=(P(None, ("groups", "genome")), P(None, "groups")),
        check_vma=False,
    )
```

```python
import functools
import math

import jax
import jax.numpy as jnp
from jax import lax
from jax.experimental import pallas as pl
from jax.experimental.pallas import tpu as pltpu
from jax.sharding import PartitionSpec as P

NBLK = 200
VAR_EPS = 1e-06
F32 = jnp.float32
BF16 = jnp.bfloat16
ORDERS = [[0, 1, 2], [1, 2, 0]]
ROUNDS = [[0, 1], [1, 2]]
VMEM_LIMIT = 20 * 1024 * 1024


STEP = 48


def pick(first, one, other):
    return jnp.where(first, one, other)


def index_parts(start, count, half):
    row = lax.broadcasted_iota(jnp.int32, (count, half), 0) + start
    col = lax.broadcasted_iota(jnp.int32, (count, half), 1)
    return row, col


def column_table(vectors, start, ref):
    table = eight(*vectors)
    half = table.shape[1]
    if start is not None:
        table = pltpu.roll(table, lax.rem(half - start, half), 1)
    for n in range(len(vectors)):
        for k in range(ref.shape[1] // 128):
            here = slice(k * 128, (k + 1) * 128)
            ref[n, here, :] = jnp.broadcast_to(table[n : n + 1, here], (128, 128)).T


def table_rows(ref, offset, columns, half):
    here = pl.ds(pl.multiple_of(offset, 16), STEP)
    return tuple(jnp.concatenate([ref[n, here, :]] * (half // 128), axis=1) for n in columns)


def high_low(values):
    high = values.astype(BF16)
    return high, (values - high.astype(F32)).astype(BF16)


def coded(sums, exact):
    high, low = high_low(sums)
    first, left = high_low(exact)
    third = (exact - first.astype(F32) - left.astype(F32)).astype(BF16)
    rows = coded_rows(sums.shape[0], exact.shape[0])
    gap = rows - 2 * sums.shape[0] - 3 * exact.shape[0]
    blank = [jnp.zeros((gap, sums.shape[1]), BF16)] if gap else []
    return jnp.concatenate([high, low, first, left, third] + blank, axis=0)


def coded_rows(many, exact):
    return -(-(2 * many + 3 * exact) // (24 * exact - 16)) * (24 * exact - 16)


def decoded(rows, many, exact):
    parts = rows.astype(F32)
    sums = parts[:many] + parts[many : 2 * many]
    at = 2 * many
    return sums, parts[at : at + exact] + parts[at + exact : at + 2 * exact] + parts[at + 2 * exact : at + 3 * exact]


def list_rows(many):
    return -(-many // 8) * 8


def put_stats(ref, sums, exact):
    many, width = sums.shape
    gap = list_rows(many) - many
    rows = [sums] + ([jnp.zeros((gap, width), F32)] if gap else [])
    rows = rows + [exact, jnp.zeros((8 - exact.shape[0], width), F32)]
    ref[...] = jnp.concatenate(rows, axis=0)


def merged(bit, msg_ref, stats_ref, rows, many, exact):
    theirs, added = decoded(msg_ref[rows:, :], many, exact)
    mine = stats_ref[:many, :]
    place = list_rows(many)
    both = pick(
        bit == 0, jnp.concatenate([mine, theirs], axis=0), jnp.concatenate([theirs, mine], axis=0)
    )
    return both, stats_ref[place : place + exact, :] + added


def two_parts(values):
    high, low = high_low(values)
    return high.astype(F32) + low.astype(F32)


def own_cols(vec, half):
    return vec[:, :half], vec[:, half : 2 * half]


def own_products(rows, cols, row, col):
    (l_rows, r_rows), (left, right) = rows, cols
    return l_rows * right, jnp.where(row < col, l_rows * left, r_rows * right)


def cross_halves(vec, first, half):
    left, right, there = vec[:, :half], vec[:, half : 2 * half], vec[:, 2 * half :]
    return pick(first, left, there), pick(first, there, right)


def cross_cols(vec, first, half):
    vec = jnp.broadcast_to(vec, (8, vec.shape[1]))
    a_cols, b_cols = cross_halves(vec, first, half)
    a_turned = pltpu.roll(a_cols, half // 2, 1)
    b3_cols = pick(first, pltpu.roll(vec[:, 2 * half :], half // 2, 1), vec[:, :half])
    return b_cols[:1], a_turned[:1], b3_cols[:1]


def cross_vectors(vec, first, half):
    a_cols, b_cols = cross_halves(vec, first, half)
    a2_cols = pick(first, vec[:, half : 2 * half], vec[:, 2 * half :])
    b_late = pltpu.roll(jnp.broadcast_to(b_cols, (8, half)), half // 2, 1)[:1]
    return a_cols, a2_cols, b_late


def cross_products(rows, cols, row, col):
    (a_rows, a2_rows, b_rows), (c_b, c_a, c_b3) = rows, cols
    half = row.shape[1]
    return jnp.where(
        col < half // 2, jnp.where(row > col, a_rows * c_b, b_rows * c_a), a2_rows * c_b3
    )


def dot_n(left, right):
    return lax.dot_general(left, right, (((1,), (0,)), ((), ())), preferred_element_type=F32)


def dot_t(left, right):
    return lax.dot_general(left, right, (((1,), (1,)), ((), ())), preferred_element_type=F32)


def squared_sums(ref, start, stop):
    width = ref.shape[1]
    total = jnp.zeros((8, width), F32)
    for k in range(start, stop, 64):
        part = ref[k : k + 64, :].astype(F32)
        total = total + jnp.sum((part * part).reshape(8, 8, width), axis=0)
    return total


def moments(ref, total):
    count = ref.shape[0]
    sums = dot_n(jnp.ones((8, count), BF16), ref[...])[:1]
    shift = sums * (1.0 / math.sqrt(count))
    return sums, jnp.sum(total, axis=0, keepdims=True) - shift * shift, shift


def eight(*rows):
    return jnp.concatenate(list(rows) + [rows[-1]] * (8 - len(rows)), axis=0)


def halved(bit, keep_ref, send_ref, value):
    part = keep_ref.shape[0]
    for k in range(0, part, STEP):
        send_ref[k : k + STEP, :] = value(pl.multiple_of((1 - bit) * part + k, 16)).astype(BF16)
        keep_ref[k : k + STEP, :] = value(pl.multiple_of(bit * part + k, 16))


def own_gram_kernel(pos_ref, own_ref, keep_ref, send_ref, stats_ref, turned_ref, piece_ref, full_ref, col_ref):
    count, slab = own_ref.shape
    half = slab // 2

    @pl.when(pos_ref[0] == 0)
    def _():
        piece_ref[...] = own_ref[:, half:]

    @pl.when(pos_ref[0] != 0)
    def _():
        piece_ref[...] = own_ref[:, :half]

    turned_ref[...] = own_ref[...].T
    sums, squares, shift = moments(own_ref, squared_sums(own_ref, 0, count))
    sums = two_parts(sums)
    put_stats(stats_ref, sums, jnp.concatenate([squares, shift], axis=0))
    column_table(own_cols(shift, half), None, col_ref)
    left, right = turned_ref[:half, :], turned_ref[half:, :]
    full_ref[:, :half] = dot_n(left, own_ref[:, half:])
    row, col = index_parts(0, half, half)
    full_ref[:, half:] = jnp.where(row < col, dot_n(left, own_ref[:, :half]), dot_n(right, own_ref[:, half:]))
    cols = own_cols(shift, half)

    def value(start):
        rows = table_rows(col_ref, start, (0, 1), half)
        products = own_products(rows, cols, *index_parts(start, STEP, half))
        return full_ref[pl.ds(start, STEP), :] - jnp.concatenate(products, axis=1)

    halved(pos_ref[3], keep_ref, send_ref, value)
    send_ref[keep_ref.shape[0] :, :] = coded(sums, squares)


def cross_gram_kernel(pos_ref, turned_ref, there_ref, own_stats_ref, keep_ref, send_ref, stats_ref, full_ref, col_ref, side_ref):
    half = there_ref.shape[1]
    quarter = half // 2
    core = pos_ref[0]
    first = core == 0
    row, col = index_parts(0, half, half)

    @pl.when(first)
    def _():
        full_ref[:, :half] = dot_n(turned_ref[:half, :], there_ref[...])
        full_ref[:, half:] = pltpu.roll(dot_n(turned_ref[half:, :], there_ref[...]), quarter, 1)

    @pl.when(jnp.logical_not(first))
    def _():
        side_ref[...] = there_ref[...].T
        full_ref[:, :half] = dot_t(side_ref[...], turned_ref[half:, :])
        full_ref[:, half:] = dot_t(side_ref[...], turned_ref[:half, :])

    sums, squares, shift = moments(there_ref, squared_sums(there_ref, 0, there_ref.shape[0]))
    shift = jnp.concatenate([own_stats_ref[list_rows(1) + 1 : list_rows(1) + 2, :], shift], axis=1)
    column_table(cross_vectors(shift, first, half), None, col_ref)
    a_shift, b_shift = cross_halves(shift, first, half)
    straight = full_ref[:, :half]
    level = jnp.sum(jnp.where(row == col, straight, 0.0), axis=0, keepdims=True) - a_shift * b_shift
    sums = two_parts(sums)
    exact = jnp.concatenate([squares, level], axis=0)
    put_stats(stats_ref, sums, exact)
    send_ref[keep_ref.shape[0] :, :] = coded(sums, exact)
    corner = full_ref[half - 256 : half, half - 256 : half].T[256 - quarter :, :]
    corner = pltpu.roll(corner, quarter, 1)[:, :quarter]
    corner = jnp.concatenate([corner, corner], axis=0)
    folded = jnp.concatenate([corner, jnp.zeros((half, half - quarter), F32)], axis=1)
    apart = full_ref[:, half:]
    full_ref[:, :half] = jnp.where(col < quarter, jnp.where(row > col, straight, folded), apart)
    cols = cross_cols(shift, first, half)

    def value(start):
        rows = table_rows(col_ref, start, (0, 1, 2), half)
        products = cross_products(rows, cols, *index_parts(start, STEP, half))
        return full_ref[pl.ds(start, STEP), :half] - products

    halved(pos_ref[3], keep_ref, send_ref, value)


def merge_kernel(pos_ref, kept_ref, msg_ref, stats_ref, *refs, rows_in, bits, many, exact, split):
    keep_ref = refs[-3] if split else None
    send_ref, out_ref = refs[-2:]
    rows = rows_in

    def value(offset):
        here = pl.ds(offset, STEP)
        return kept_ref[here, :].astype(F32) + msg_ref[here, :].astype(F32)

    if split:
        halved(pos_ref[bits[1]], keep_ref, send_ref, value)
        done = keep_ref.shape[0]
    else:
        done = rows
        for k in range(0, rows, STEP):
            send_ref[k : k + STEP, :] = value(k).astype(BF16)
    sums, more = merged(pos_ref[bits[0]], msg_ref, stats_ref, rows, many, exact)
    put_stats(out_ref, sums, more)
    send_ref[done:, :] = coded(sums, more)


def deviations(sums, samples):
    mean = jnp.sum(sums, axis=0, keepdims=True) * (1.0 / sums.shape[0])
    return (sums - mean) * (1.0 / math.sqrt(samples))


def outer_sums(left, right):
    (l_high, l_low), (r_high, r_low) = high_low(left), high_low(right)
    left = jnp.concatenate([l_high, l_high, l_low], axis=0)
    right = jnp.concatenate([r_high, r_low, r_high], axis=0)
    return lax.dot_general(left, right, (((0,), (0,)), ((), ())), preferred_element_type=F32)


def from_row(vec, start):
    half = vec.shape[1]
    return pltpu.roll(vec, lax.rem(half - start, half), 1)[:, :128]


def unbiased(correl, everyone):
    squared = correl * correl
    return squared - (1.0 - squared) * (1.0 / (everyone - 2.0))


def placed_at(rows_part, offset, half):
    blank = jnp.zeros((rows_part.shape[0], half - rows_part.shape[1]), F32)
    return pltpu.roll(jnp.concatenate([rows_part, blank], axis=1), offset, 1)


def own_score_kernel(
    pos_ref, kept_ref, msg_ref, stats_ref, limit_ref, flag_ref, sub_ref,
    out_ref, vec_ref, col_ref, one_ref, two_ref, *, bit, many, samples,
):
    rows = one_ref.shape[0]
    half = kept_ref.shape[1] // 2
    everyone = 2.0 * many * samples
    base = pos_ref[2]
    sums, squares = merged(pos_ref[bit], msg_ref, stats_ref, rows, many, 1)
    apart = deviations(sums, samples)
    squares = squares + jnp.sum(apart * apart, axis=0, keepdims=True)
    scale = 1.0 / jnp.sqrt(squares * (1.0 / everyone) + VAR_EPS)
    put_stats(vec_ref, apart, scale)
    scales = own_cols(scale, half)
    factors = own_cols(scale * (1.0 / everyone), half) + (limit_ref[:1, :half],)
    column_table(factors, base, col_ref)
    left, right = own_cols(apart, half)
    l_rows = from_row(left, base)
    products = outer_sums(l_rows, right), outer_sums(l_rows, left), outer_sums(from_row(right, base), right)
    right_lim = limit_ref[:1, half : 2 * half]
    for k in range(0, rows, STEP):
        start = base + k
        row, col = index_parts(start, STEP, half)
        l_scale, r_scale, left_lim = table_rows(col_ref, k, range(3), half)
        one, upper, lower = (x[k : k + STEP] for x in products)
        shifts = one, jnp.where(row < col, upper, lower)
        norms = own_products((l_scale, r_scale), scales, row, col)
        gaps = (half + col - row, jnp.where(row == col, 8 * half, jnp.abs(row - col)))
        lims = (left_lim, jnp.where(row < col, left_lim, right_lim))
        for s, ref in ((0, one_ref), (1, two_ref)):
            here = slice(s * half, (s + 1) * half)
            value = kept_ref[k : k + STEP, here].astype(F32) + msg_ref[k : k + STEP, here].astype(F32)
            weight = unbiased((value + shifts[s]) * norms[s], everyone)
            ref[k : k + STEP, :] = jnp.where(gaps[s].astype(F32) <= lims[s], weight, 0.0).astype(BF16)
    row, col = index_parts(base, rows, half)
    one, two = one_ref[...], two_ref[...]
    zero = jnp.zeros_like(two)
    upper, lower = jnp.where(row < col, two, zero), jnp.where(row > col, two, zero)
    f_left, f_right = flag_ref[:, :half], flag_ref[:, half : 2 * half]
    s_left, s_right = sub_ref[:, :rows], sub_ref[:, 128 : 128 + rows]
    out_ref[:, :half] = dot_n(s_left, upper) + placed_at(dot_t(f_right, one) + dot_t(f_left, upper), base, half)
    out_ref[:, half:] = dot_n(s_left, one) + dot_n(s_right, lower) + placed_at(dot_t(f_right, lower), base, half)


def cross_score_kernel(
    pos_ref, kept_ref, msg_ref, stats_ref, vec_ref, limit_ref, flag_ref, sub_ref, own_ref,
    out_ref, col_ref, three_ref, *, bit, many, samples,
):
    rows = three_ref.shape[0]
    half = kept_ref.shape[1]
    quarter = half // 2
    core = pos_ref[0]
    first = core == 0
    everyone = 2.0 * many * samples
    base = pos_ref[2]
    sums, exact = merged(pos_ref[bit], msg_ref, stats_ref, rows, many, 2)
    apart = deviations(sums, samples)
    squares = exact[:1] + jnp.sum(apart * apart, axis=0, keepdims=True)
    place = list_rows(2 * many)
    apart = jnp.concatenate([vec_ref[: 2 * many, :], apart], axis=1)
    a_apart, b_apart = cross_halves(apart, first, half)
    level = exact[1:2] + jnp.sum(a_apart * b_apart, axis=0, keepdims=True)
    scale = 1.0 / jnp.sqrt(squares * (1.0 / everyone) + VAR_EPS)
    scale = jnp.concatenate([vec_ref[place : place + 1, :], scale], axis=1)
    limit = limit_ref[:1, :]
    factors = cross_vectors(scale * (1.0 / everyone), first, half)
    column_table(factors + cross_vectors(limit, first, half)[:2], base, col_ref)
    scales = cross_cols(scale, first, half)
    there = apart[:, 2 * half :]
    a2_apart = pick(first, apart[:, half : 2 * half], there)
    b3_apart = pick(first, pltpu.roll(there, quarter, 1), apart[:, :half])
    late_a, late_b = pltpu.roll(a_apart, quarter, 1), pltpu.roll(b_apart, quarter, 1)
    shifts = (
        outer_sums(from_row(a_apart, base), b_apart),
        outer_sums(from_row(late_b, base), late_a),
        outer_sums(from_row(a2_apart, base), b3_apart),
    )
    _, late_lim, _ = cross_cols(limit, first, half)
    for k in range(0, rows, STEP):
        start = base + k
        row, col = index_parts(start, STEP, half)
        fold = col < quarter
        parts = table_rows(col_ref, k, range(5), half)
        a_lim, a2_lim = parts[3:]
        straight, late, apart = (x[k : k + STEP] for x in shifts)
        products = jnp.where(fold, jnp.where(row > col, straight, late), apart)
        norms = cross_products(parts[:3], scales, row, col)
        lims = jnp.where(fold, jnp.where(row > col, a_lim, late_lim), a2_lim)
        near = jnp.where(row == col, 8 * half, 2 * half - jnp.abs(row - col))
        gaps = jnp.where(fold, near, quarter + quarter * core + col - row)
        value = kept_ref[k : k + STEP, :].astype(F32) + msg_ref[k : k + STEP, :].astype(F32)
        weight = unbiased((value + products) * norms, everyone)
        three_ref[k : k + STEP, :] = jnp.where(gaps.astype(F32) <= lims, weight, 0.0).astype(BF16)
    a_scale, b_scale = cross_halves(scale, first, half)
    a_limit, _ = cross_halves(limit, first, half)
    lane = lax.broadcasted_iota(jnp.int32, (1, half), 1)
    level = unbiased(level * (1.0 / everyone) * a_scale * b_scale, everyone)
    mine = (lane >= base) & (lane < base + rows) & (a_limit >= 2.0 * half)
    level = jnp.where(mine, level, 0.0)
    row, col = index_parts(base, rows, half)
    three = three_ref[...]
    zero = jnp.zeros_like(three)
    fold = col < quarter
    straight = jnp.where(fold & (row > col), three, zero)
    folded = jnp.where(fold & (row < col), three, zero)
    apart = jnp.where(fold, zero, three)
    f_a, f_b = flag_ref[:, :half], flag_ref[:, half : 2 * half]
    f_late, f_b3 = flag_ref[:, 2 * half : 3 * half], flag_ref[:, 3 * half :]
    s_a, s_a2, s_late = sub_ref[:, 256 : 256 + rows], sub_ref[:, 384 : 384 + rows], sub_ref[:, 512 : 512 + rows]
    out_a = placed_at(dot_t(f_b, straight), base, half) + pltpu.roll(dot_n(s_late, folded), quarter, 1)
    out_b = dot_n(s_a, straight) + placed_at(dot_t(f_late, folded), lax.rem(base + quarter, half), half)
    out_a = out_a + f_b.astype(F32) * level
    out_b = out_b + f_a.astype(F32) * level
    out_a2 = placed_at(dot_t(f_b3, apart), base, half)
    out_b3 = dot_n(s_a2, apart)
    out_ref[:, :half] = own_ref[:, :half] + pick(first, out_a, out_b3)
    out_ref[:, half : 2 * half] = own_ref[:, half:] + pick(first, out_a2, out_b)
    out_ref[:, 2 * half :] = pick(first, out_b + pltpu.roll(out_b3, quarter, 1), out_a + out_a2)


def local_kernel(pos_ref, annot_ref, chrom_ref, reach_ref, ids_ref, flag_ref, cross_ref, sub_ref, limit_ref, hot_ref):
    half = annot_ref.shape[1] // 4
    first = pos_ref[0] == 0
    base = pos_ref[2]
    flags = annot_ref[...].astype(F32)

    def quarters(x):
        return [x[:, k * half : (k + 1) * half] for k in range(4)]

    def local(x):
        one, two, three, four = quarters(x)
        return pick(first, one, three), pick(first, two, four), pick(first, three, two)

    left, right, there = local(flags)
    for k, x in enumerate((left, right, there)):
        flag_ref[:, k * half : (k + 1) * half] = x.astype(BF16)
    a_cols, b_cols, a2_cols = pick(first, left, there), pick(first, there, right), pick(first, right, there)
    b3_cols = pick(first, pltpu.roll(there, half // 2, 1), left)
    for k, x in enumerate((a_cols, b_cols, pltpu.roll(a_cols, half // 2, 1), b3_cols)):
        cross_ref[:, k * half : (k + 1) * half] = x.astype(BF16)
    back = lax.rem(half - base, half)
    late = lax.rem(half + half // 2 - base, half)
    for k, (x, turn) in enumerate(((left, back), (right, back), (a_cols, back), (a2_cols, back), (b_cols, late))):
        sub_ref[:, k * 128 : (k + 1) * 128] = pltpu.roll(x, turn, 1)[:, :128].astype(BF16)

    def line(ref):
        return jnp.concatenate([ref[k : k + 1, :] for k in range(ref.shape[0])], axis=1).astype(F32)

    chrom, reach = line(chrom_ref), line(reach_ref)
    ends = [jnp.sum((chrom <= k).astype(F32), axis=1, keepdims=True) for k in (1, 2, 3)]
    last = jnp.where(chrom == 1, ends[0], jnp.where(chrom == 2, ends[1], ends[2]))
    place = lax.broadcasted_iota(jnp.int32, chrom.shape, 1).astype(F32)
    limit = jnp.concatenate(local(jnp.minimum(reach, last - 1.0 - place)), axis=1)
    limit_ref[...] = jnp.broadcast_to(limit, limit_ref.shape)
    block = jnp.concatenate(local(line(ids_ref)), axis=1)
    number = lax.broadcasted_iota(jnp.int32, hot_ref.shape, 0).astype(F32)
    hot_ref[...] = jnp.where(number == block, 1.0, 0.0).astype(BF16)


def block_kernel(pos_ref, score_ref, flag_ref, hot_ref, sum_ref):
    slab = flag_ref.shape[1] // 3 * 2
    hot = hot_ref[...]
    own = score_ref[:, :slab] + flag_ref[:, :slab].astype(F32)
    scores = jnp.concatenate([own, score_ref[:, slab:]], axis=1)
    high = scores.astype(BF16)
    left = (scores - high.astype(F32)).astype(BF16)
    gap = jnp.zeros((128 - scores.shape[0], scores.shape[1]), BF16)
    both = dot_t(hot, jnp.concatenate([high, gap, left, gap], axis=0))
    sum_ref[...] = (both[:, :128] + both[:, 128:])[:, : sum_ref.shape[1]]


def call(kernel, inputs, outputs, scratch, flops, moved):
    vmem = pl.BlockSpec(memory_space=pltpu.VMEM)
    smem = pl.BlockSpec(memory_space=pltpu.SMEM)
    return pl.pallas_call(
        kernel,
        out_shape=outputs,
        in_specs=[smem] + [vmem] * (len(inputs) - 1),
        out_specs=jax.tree.map(lambda _: vmem, outputs),
        scratch_shapes=scratch,
        compiler_params=pltpu.CompilerParams(vmem_limit_bytes=VMEM_LIMIT),
        cost_estimate=pl.CostEstimate(flops=flops, bytes_accessed=moved, transcendentals=0),
    )(*inputs)


def body(genotypes, chromosome, blocks, annotation, reach):
    count, slab = genotypes.shape
    half = slab // 2
    quarter = half // 2
    width = 3 * half
    snps = chromosome.shape[0]
    parts = lax.axis_size("samples")
    bits = parts.bit_length() - 1
    core = lax.axis_index("genome")
    place = lax.axis_index("samples")
    order = [first + list(range(3, bits)) for first in ORDERS]
    bit_at = [(place >> jnp.where(core == 0, order[0][t], order[1][t])) & 1 for t in range(bits)]

    def exchange(x, t, order=order):
        route = []
        for s in range(parts):
            for g in range(2):
                route.append((s * 2 + g, (s ^ (1 << order[g][t])) * 2 + g))
        return lax.ppermute(x, ("samples", "genome"), route)

    def across(x):
        return lax.ppermute(x, "genome", [(0, 1), (1, 0)])

    def shape(rows, cols, dtype):
        return jax.ShapeDtypeStruct((rows, cols), dtype)

    base = bit_at[0] * quarter + bit_at[1] * (quarter // 2)
    rows = quarter // 2

    where = jnp.stack([core, place, base] + bit_at).astype(jnp.int32)
    annot = annotation.shape[0]

    hot_rows = -(-NBLK // 8) * 8

    def tiles(x):
        return x.reshape(-1, 128)

    flags, flags_cross, subs, limit, hot = call(
        local_kernel,
        (where, annotation, tiles(chromosome), tiles(reach), tiles(blocks)),
        (
            shape(annot, width, BF16),
            shape(annot, 4 * half, BF16),
            shape(annot, 5 * 128, BF16),
            shape(8, width, F32),
            shape(hot_rows, width, BF16),
        ),
        [],
        annot * snps * 10,
        annot * snps * 8,
    )
    def table_of(vectors, count):
        return pltpu.VMEM((vectors, -(-count // 128) * 128, 128), F32)

    def outputs(kept, sent, cols, many, exact):
        kept_shape = (shape(kept, cols, F32),) if kept else ()
        coded_shape = shape(sent + coded_rows(many, exact), cols, BF16)
        return kept_shape + (coded_shape, shape(list_rows(many) + 8, cols, F32))

    keep_a, send_a, stats_a, turned, piece = call(
        own_gram_kernel,
        (where, genotypes),
        outputs(quarter, quarter, slab, 1, 1)
        + (shape(slab, count, BF16), shape(count, half, BF16)),
        [pltpu.VMEM((half, slab), F32), table_of(2, half)],
        2 * count * half * half * 3,
        count * slab * 2,
    )
    there = across(piece)
    msg_a = exchange(send_a, 0)
    keep_b, send_b, stats_b = call(
        cross_gram_kernel,
        (where, turned, there, stats_a),
        outputs(quarter, quarter, half, 1, 2),
        [pltpu.VMEM((half, slab), F32), table_of(3, half), pltpu.VMEM((half, count), BF16)],
        2 * count * half * half * 3,
        count * slab * 2,
    )
    msg_b = exchange(send_b, 0)

    def merge(keep, msg, stats, cols, t, exact, *after):
        split = t == 1
        *kept, send, stats = call(
            functools.partial(merge_kernel, rows_in=quarter if split else rows, bits=(2 + t, 3 + t), many=1 << (t - 1), exact=exact, split=split),
            (where, keep, msg, stats) + after,
            outputs(rows if split else 0, rows, cols, 1 << t, exact),
            [],
            rows * cols * 8,
            rows * cols * 20,
        )
        return (kept[0] if split else send), send, stats

    for t in range(1, bits):
        if t == 1:
            msg_a, send_b = lax.optimization_barrier((msg_a, send_b))
        keep_a, send_a, stats_a = merge(keep_a, msg_a, stats_a, slab, t, 1)
        msg_a = exchange(send_a, t)
        keep_b, send_b, stats_b = merge(keep_b, msg_b, stats_b, half, t, 2, stats_a)
        msg_b = exchange(send_b, t)
    last = {"bit": 2 + bits, "many": parts // 2, "samples": float(count)}
    scores_a, vectors = call(
        functools.partial(own_score_kernel, **last),
        (where, keep_a, msg_a, stats_a, limit, flags, subs),
        (shape(annot, slab, F32), shape(list_rows(parts) + 8, slab, F32)),
        [table_of(3, rows)] + [pltpu.VMEM((rows, half), BF16)] * 2,
        2 * annot * half * rows * 8,
        rows * slab * 20,
    )
    partial = call(
        functools.partial(cross_score_kernel, **last),
        (where, keep_b, msg_b, stats_b, vectors, limit, flags_cross, subs, scores_a),
        shape(annot, width, F32),
        [table_of(5, rows)] + [pltpu.VMEM((rows, half), BF16)],
        2 * annot * half * rows * 8,
        rows * slab * 20,
    )
    cut = -(-width // 256) * 128
    pieces = [partial[:, :cut], partial[:, cut:]]
    for t in range(2):
        rounded = [x.astype(jnp.float16) for x in pieces]
        pieces = [x.astype(F32) + exchange(x, t, ROUNDS).astype(F32) for x in rounded]
    partial = jnp.concatenate(pieces, axis=1)
    arrived = across(partial[:, slab:])
    sums = call(
        block_kernel,
        (where, partial, flags, hot),
        shape(hot_rows, annot, F32),
        [],
        2 * annot * width * hot_rows * 2,
        annot * width * 8,
    )
    nothing = jnp.zeros_like(arrived)
    ld_scores = (partial[:, :slab] + flags[:, :slab].astype(F32)) + jnp.where(
        core == 0,
        jnp.concatenate([nothing, arrived], axis=1),
        jnp.concatenate([arrived, nothing], axis=1),
    )
    sums_there = across(sums)
    sums, ld_scores = lax.optimization_barrier((sums, ld_scores))
    return (ld_scores, (sums + sums_there)[:NBLK].T)


def solution(mesh):
    placed = (
        P(("groups", "samples"), "genome"),
        P("groups"),
        P("groups"),
        P(None, "groups"),
        P("groups"),
    )
    return jax.shard_map(
        body,
        mesh=mesh,
        in_specs=placed,
        out_specs=(P(None, ("groups", "genome")), P(None, "groups")),
        check_vma=False,
    )
```

```python
import functools
import math

import jax
import jax.numpy as jnp
from jax import lax
from jax.experimental import pallas as pl
from jax.experimental.pallas import tpu as pltpu
from jax.sharding import PartitionSpec as P

NBLK = 200
VAR_EPS = 1e-06
F32 = jnp.float32
BF16 = jnp.bfloat16
ORDERS = [[0, 1, 2], [1, 2, 0]]
ROUNDS = [[0, 1], [1, 2]]
VMEM_LIMIT = 20 * 1024 * 1024


STEP = 48


def pick(first, one, other):
    return jnp.where(first, one, other)


def index_parts(start, count, half):
    row = lax.broadcasted_iota(jnp.int32, (count, half), 0) + start
    col = lax.broadcasted_iota(jnp.int32, (count, half), 1)
    return row, col


def column_table(vectors, start, ref):
    table = eight(*vectors)
    half = table.shape[1]
    if start is not None:
        table = pltpu.roll(table, lax.rem(half - start, half), 1)
    for n in range(len(vectors)):
        for k in range(ref.shape[1] // 128):
            here = slice(k * 128, (k + 1) * 128)
            ref[n, here, :] = jnp.broadcast_to(table[n : n + 1, here], (128, 128)).T


def table_rows(ref, offset, columns, half):
    here = pl.ds(pl.multiple_of(offset, 16), STEP)
    return tuple(jnp.concatenate([ref[n, here, :]] * (half // 128), axis=1) for n in columns)


def high_low(values):
    high = values.astype(BF16)
    return high, (values - high.astype(F32)).astype(BF16)


def coded(sums, exact):
    high, low = high_low(sums)
    first, left = high_low(exact)
    third = (exact - first.astype(F32) - left.astype(F32)).astype(BF16)
    rows = coded_rows(sums.shape[0], exact.shape[0])
    gap = rows - 2 * sums.shape[0] - 3 * exact.shape[0]
    blank = [jnp.zeros((gap, sums.shape[1]), BF16)] if gap else []
    return jnp.concatenate([high, low, first, left, third] + blank, axis=0)


def coded_rows(many, exact):
    return -(-(2 * many + 3 * exact) // (24 * exact - 16)) * (24 * exact - 16)


def decoded(rows, many, exact):
    parts = rows.astype(F32)
    sums = parts[:many] + parts[many : 2 * many]
    at = 2 * many
    return sums, parts[at : at + exact] + parts[at + exact : at + 2 * exact] + parts[at + 2 * exact : at + 3 * exact]


def list_rows(many):
    return -(-many // 8) * 8


def put_stats(ref, sums, exact):
    many, width = sums.shape
    gap = list_rows(many) - many
    rows = [sums] + ([jnp.zeros((gap, width), F32)] if gap else [])
    rows = rows + [exact, jnp.zeros((8 - exact.shape[0], width), F32)]
    ref[...] = jnp.concatenate(rows, axis=0)


def merged(bit, msg_ref, stats_ref, rows, many, exact):
    theirs, added = decoded(msg_ref[rows:, :], many, exact)
    mine = stats_ref[:many, :]
    place = list_rows(many)
    both = pick(
        bit == 0, jnp.concatenate([mine, theirs], axis=0), jnp.concatenate([theirs, mine], axis=0)
    )
    return both, stats_ref[place : place + exact, :] + added


def two_parts(values):
    high, low = high_low(values)
    return high.astype(F32) + low.astype(F32)


def own_cols(vec, half):
    return vec[:, :half], vec[:, half : 2 * half]


def own_products(rows, cols, row, col):
    (l_rows, r_rows), (left, right) = rows, cols
    return l_rows * right, jnp.where(row < col, l_rows * left, r_rows * right)


def cross_halves(vec, first, half):
    left, right, there = vec[:, :half], vec[:, half : 2 * half], vec[:, 2 * half :]
    return pick(first, left, there), pick(first, there, right)


def cross_cols(vec, first, half):
    vec = jnp.broadcast_to(vec, (8, vec.shape[1]))
    a_cols, b_cols = cross_halves(vec, first, half)
    a_turned = pltpu.roll(a_cols, half // 2, 1)
    b3_cols = pick(first, pltpu.roll(vec[:, 2 * half :], half // 2, 1), vec[:, :half])
    return b_cols[:1], a_turned[:1], b3_cols[:1]


def cross_vectors(vec, first, half):
    a_cols, b_cols = cross_halves(vec, first, half)
    a2_cols = pick(first, vec[:, half : 2 * half], vec[:, 2 * half :])
    b_late = pltpu.roll(jnp.broadcast_to(b_cols, (8, half)), half // 2, 1)[:1]
    return a_cols, a2_cols, b_late


def cross_products(rows, cols, row, col):
    (a_rows, a2_rows, b_rows), (c_b, c_a, c_b3) = rows, cols
    half = row.shape[1]
    return jnp.where(
        col < half // 2, jnp.where(row > col, a_rows * c_b, b_rows * c_a), a2_rows * c_b3
    )


def dot_n(left, right):
    return lax.dot_general(left, right, (((1,), (0,)), ((), ())), preferred_element_type=F32)


def dot_t(left, right):
    return lax.dot_general(left, right, (((1,), (1,)), ((), ())), preferred_element_type=F32)


def squared_sums(ref, start, stop):
    width = ref.shape[1]
    total = jnp.zeros((8, width), F32)
    for k in range(start, stop, 64):
        part = ref[k : k + 64, :].astype(F32)
        total = total + jnp.sum((part * part).reshape(8, 8, width), axis=0)
    return total


def moments(ref, total):
    count = ref.shape[0]
    sums = dot_n(jnp.ones((8, count), BF16), ref[...])[:1]
    shift = sums * (1.0 / math.sqrt(count))
    return sums, jnp.sum(total, axis=0, keepdims=True) - shift * shift, shift


def eight(*rows):
    return jnp.concatenate(list(rows) + [rows[-1]] * (8 - len(rows)), axis=0)


def halved(bit, keep_ref, send_ref, value):
    part = keep_ref.shape[0]
    for k in range(0, part, STEP):
        send_ref[k : k + STEP, :] = value(pl.multiple_of((1 - bit) * part + k, 16)).astype(BF16)
        keep_ref[k : k + STEP, :] = value(pl.multiple_of(bit * part + k, 16))


def own_gram_kernel(pos_ref, own_ref, keep_ref, send_ref, stats_ref, turned_ref, piece_ref, full_ref, col_ref):
    count, slab = own_ref.shape
    half = slab // 2

    @pl.when(pos_ref[0] == 0)
    def _():
        piece_ref[...] = own_ref[:, half:]

    @pl.when(pos_ref[0] != 0)
    def _():
        piece_ref[...] = own_ref[:, :half]

    turned_ref[...] = own_ref[...].T
    sums, squares, shift = moments(own_ref, squared_sums(own_ref, 0, count))
    sums = two_parts(sums)
    put_stats(stats_ref, sums, jnp.concatenate([squares, shift], axis=0))
    column_table(own_cols(shift, half), None, col_ref)
    left, right = turned_ref[:half, :], turned_ref[half:, :]
    full_ref[:, :half] = dot_n(left, own_ref[:, half:])
    row, col = index_parts(0, half, half)
    full_ref[:, half:] = jnp.where(row < col, dot_n(left, own_ref[:, :half]), dot_n(right, own_ref[:, half:]))
    cols = own_cols(shift, half)

    def value(start):
        rows = table_rows(col_ref, start, (0, 1), half)
        products = own_products(rows, cols, *index_parts(start, STEP, half))
        return full_ref[pl.ds(start, STEP), :] - jnp.concatenate(products, axis=1)

    halved(pos_ref[3], keep_ref, send_ref, value)
    send_ref[keep_ref.shape[0] :, :] = coded(sums, squares)


def cross_gram_kernel(pos_ref, turned_ref, there_ref, own_stats_ref, keep_ref, send_ref, stats_ref, full_ref, col_ref, side_ref):
    half = there_ref.shape[1]
    quarter = half // 2
    core = pos_ref[0]
    first = core == 0
    row, col = index_parts(0, half, half)

    @pl.when(first)
    def _():
        full_ref[:, :half] = dot_n(turned_ref[:half, :], there_ref[...])
        full_ref[:, half:] = pltpu.roll(dot_n(turned_ref[half:, :], there_ref[...]), quarter, 1)

    @pl.when(jnp.logical_not(first))
    def _():
        side_ref[...] = there_ref[...].T
        full_ref[:, :half] = dot_t(side_ref[...], turned_ref[half:, :])
        full_ref[:, half:] = dot_t(side_ref[...], turned_ref[:half, :])

    sums, squares, shift = moments(there_ref, squared_sums(there_ref, 0, there_ref.shape[0]))
    shift = jnp.concatenate([own_stats_ref[list_rows(1) + 1 : list_rows(1) + 2, :], shift], axis=1)
    column_table(cross_vectors(shift, first, half), None, col_ref)
    a_shift, b_shift = cross_halves(shift, first, half)
    straight = full_ref[:, :half]
    level = jnp.sum(jnp.where(row == col, straight, 0.0), axis=0, keepdims=True) - a_shift * b_shift
    sums = two_parts(sums)
    exact = jnp.concatenate([squares, level], axis=0)
    put_stats(stats_ref, sums, exact)
    send_ref[keep_ref.shape[0] :, :] = coded(sums, exact)
    corner = full_ref[half - 256 : half, half - 256 : half].T[256 - quarter :, :]
    corner = pltpu.roll(corner, quarter, 1)[:, :quarter]
    corner = jnp.concatenate([corner, corner], axis=0)
    folded = jnp.concatenate([corner, jnp.zeros((half, half - quarter), F32)], axis=1)
    apart = full_ref[:, half:]
    full_ref[:, :half] = jnp.where(col < quarter, jnp.where(row > col, straight, folded), apart)
    cols = cross_cols(shift, first, half)

    def value(start):
        rows = table_rows(col_ref, start, (0, 1, 2), half)
        products = cross_products(rows, cols, *index_parts(start, STEP, half))
        return full_ref[pl.ds(start, STEP), :half] - products

    halved(pos_ref[3], keep_ref, send_ref, value)


def merge_kernel(pos_ref, kept_ref, msg_ref, stats_ref, *refs, rows_in, bits, many, exact, split):
    keep_ref = refs[-3] if split else None
    send_ref, out_ref = refs[-2:]
    rows = rows_in

    def value(offset):
        here = pl.ds(offset, STEP)
        return kept_ref[here, :].astype(F32) + msg_ref[here, :].astype(F32)

    if split:
        halved(pos_ref[bits[1]], keep_ref, send_ref, value)
        done = keep_ref.shape[0]
    else:
        done = rows
        for k in range(0, rows, STEP):
            send_ref[k : k + STEP, :] = value(k).astype(BF16)
    sums, more = merged(pos_ref[bits[0]], msg_ref, stats_ref, rows, many, exact)
    put_stats(out_ref, sums, more)
    send_ref[done:, :] = coded(sums, more)


def deviations(sums, samples):
    mean = jnp.sum(sums, axis=0, keepdims=True) * (1.0 / sums.shape[0])
    return (sums - mean) * (1.0 / math.sqrt(samples))


def outer_sums(left, right):
    (l_high, l_low), (r_high, r_low) = high_low(left), high_low(right)
    left = jnp.concatenate([l_high, l_high, l_low], axis=0)
    right = jnp.concatenate([r_high, r_low, r_high], axis=0)
    return lax.dot_general(left, right, (((0,), (0,)), ((), ())), preferred_element_type=F32)


def from_row(vec, start):
    half = vec.shape[1]
    return pltpu.roll(vec, lax.rem(half - start, half), 1)[:, :128]


def unbiased(correl, everyone):
    squared = correl * correl
    return squared - (1.0 - squared) * (1.0 / (everyone - 2.0))


def placed_at(rows_part, offset, half):
    blank = jnp.zeros((rows_part.shape[0], half - rows_part.shape[1]), F32)
    return pltpu.roll(jnp.concatenate([rows_part, blank], axis=1), offset, 1)


def own_score_kernel(
    pos_ref, kept_ref, msg_ref, stats_ref, limit_ref, flag_ref, sub_ref,
    out_ref, vec_ref, col_ref, one_ref, two_ref, *, bit, many, samples,
):
    rows = one_ref.shape[0]
    half = kept_ref.shape[1] // 2
    everyone = 2.0 * many * samples
    base = pos_ref[2]
    sums, squares = merged(pos_ref[bit], msg_ref, stats_ref, rows, many, 1)
    apart = deviations(sums, samples)
    squares = squares + jnp.sum(apart * apart, axis=0, keepdims=True)
    scale = 1.0 / jnp.sqrt(squares * (1.0 / everyone) + VAR_EPS)
    put_stats(vec_ref, apart, scale)
    scales = own_cols(scale, half)
    factors = own_cols(scale * (1.0 / everyone), half) + (limit_ref[:1, :half],)
    column_table(factors, base, col_ref)
    left, right = own_cols(apart, half)
    l_rows = from_row(left, base)
    products = outer_sums(l_rows, right), outer_sums(l_rows, left), outer_sums(from_row(right, base), right)
    right_lim = limit_ref[:1, half : 2 * half]
    for k in range(0, rows, STEP):
        start = base + k
        row, col = index_parts(start, STEP, half)
        l_scale, r_scale, left_lim = table_rows(col_ref, k, range(3), half)
        one, upper, lower = (x[k : k + STEP] for x in products)
        shifts = one, jnp.where(row < col, upper, lower)
        norms = own_products((l_scale, r_scale), scales, row, col)
        gaps = (half + col - row, jnp.where(row == col, 8 * half, jnp.abs(row - col)))
        lims = (left_lim, jnp.where(row < col, left_lim, right_lim))
        for s, ref in ((0, one_ref), (1, two_ref)):
            here = slice(s * half, (s + 1) * half)
            value = kept_ref[k : k + STEP, here].astype(F32) + msg_ref[k : k + STEP, here].astype(F32)
            weight = unbiased((value + shifts[s]) * norms[s], everyone)
            ref[k : k + STEP, :] = jnp.where(gaps[s].astype(F32) <= lims[s], weight, 0.0).astype(BF16)
    row, col = index_parts(base, rows, half)
    one, two = one_ref[...], two_ref[...]
    zero = jnp.zeros_like(two)
    upper, lower = jnp.where(row < col, two, zero), jnp.where(row > col, two, zero)
    f_left, f_right = flag_ref[:, :half], flag_ref[:, half : 2 * half]
    s_left, s_right = sub_ref[:, :rows], sub_ref[:, 128 : 128 + rows]
    out_ref[:, :half] = dot_n(s_left, upper) + placed_at(dot_t(f_right, one) + dot_t(f_left, upper), base, half)
    out_ref[:, half:] = dot_n(s_left, one) + dot_n(s_right, lower) + placed_at(dot_t(f_right, lower), base, half)


def cross_score_kernel(
    pos_ref, kept_ref, msg_ref, stats_ref, vec_ref, limit_ref, flag_ref, sub_ref, own_ref,
    out_ref, col_ref, three_ref, *, bit, many, samples,
):
    rows = three_ref.shape[0]
    half = kept_ref.shape[1]
    quarter = half // 2
    core = pos_ref[0]
    first = core == 0
    everyone = 2.0 * many * samples
    base = pos_ref[2]
    sums, exact = merged(pos_ref[bit], msg_ref, stats_ref, rows, many, 2)
    apart = deviations(sums, samples)
    squares = exact[:1] + jnp.sum(apart * apart, axis=0, keepdims=True)
    place = list_rows(2 * many)
    apart = jnp.concatenate([vec_ref[: 2 * many, :], apart], axis=1)
    a_apart, b_apart = cross_halves(apart, first, half)
    level = exact[1:2] + jnp.sum(a_apart * b_apart, axis=0, keepdims=True)
    scale = 1.0 / jnp.sqrt(squares * (1.0 / everyone) + VAR_EPS)
    scale = jnp.concatenate([vec_ref[place : place + 1, :], scale], axis=1)
    limit = limit_ref[:1, :]
    factors = cross_vectors(scale * (1.0 / everyone), first, half)
    column_table(factors + cross_vectors(limit, first, half)[:2], base, col_ref)
    scales = cross_cols(scale, first, half)
    there = apart[:, 2 * half :]
    a2_apart = pick(first, apart[:, half : 2 * half], there)
    b3_apart = pick(first, pltpu.roll(there, quarter, 1), apart[:, :half])
    late_a, late_b = pltpu.roll(a_apart, quarter, 1), pltpu.roll(b_apart, quarter, 1)
    shifts = (
        outer_sums(from_row(a_apart, base), b_apart),
        outer_sums(from_row(late_b, base), late_a),
        outer_sums(from_row(a2_apart, base), b3_apart),
    )
    _, late_lim, _ = cross_cols(limit, first, half)
    for k in range(0, rows, STEP):
        start = base + k
        row, col = index_parts(start, STEP, half)
        fold = col < quarter
        parts = table_rows(col_ref, k, range(5), half)
        a_lim, a2_lim = parts[3:]
        straight, late, apart = (x[k : k + STEP] for x in shifts)
        products = jnp.where(fold, jnp.where(row > col, straight, late), apart)
        norms = cross_products(parts[:3], scales, row, col)
        lims = jnp.where(fold, jnp.where(row > col, a_lim, late_lim), a2_lim)
        near = jnp.where(row == col, 8 * half, 2 * half - jnp.abs(row - col))
        gaps = jnp.where(fold, near, quarter + quarter * core + col - row)
        value = kept_ref[k : k + STEP, :].astype(F32) + msg_ref[k : k + STEP, :].astype(F32)
        weight = unbiased((value + products) * norms, everyone)
        three_ref[k : k + STEP, :] = jnp.where(gaps.astype(F32) <= lims, weight, 0.0).astype(BF16)
    a_scale, b_scale = cross_halves(scale, first, half)
    a_limit, _ = cross_halves(limit, first, half)
    lane = lax.broadcasted_iota(jnp.int32, (1, half), 1)
    level = unbiased(level * (1.0 / everyone) * a_scale * b_scale, everyone)
    mine = (lane >= base) & (lane < base + rows) & (a_limit >= 2.0 * half)
    level = jnp.where(mine, level, 0.0)
    row, col = index_parts(base, rows, half)
    three = three_ref[...]
    zero = jnp.zeros_like(three)
    fold = col < quarter
    straight = jnp.where(fold & (row > col), three, zero)
    folded = jnp.where(fold & (row < col), three, zero)
    apart = jnp.where(fold, zero, three)
    f_a, f_b = flag_ref[:, :half], flag_ref[:, half : 2 * half]
    f_late, f_b3 = flag_ref[:, 2 * half : 3 * half], flag_ref[:, 3 * half :]
    s_a, s_a2, s_late = sub_ref[:, 256 : 256 + rows], sub_ref[:, 384 : 384 + rows], sub_ref[:, 512 : 512 + rows]
    out_a = placed_at(dot_t(f_b, straight), base, half) + pltpu.roll(dot_n(s_late, folded), quarter, 1)
    out_b = dot_n(s_a, straight) + placed_at(dot_t(f_late, folded), lax.rem(base + quarter, half), half)
    out_a = out_a + f_b.astype(F32) * level
    out_b = out_b + f_a.astype(F32) * level
    out_a2 = placed_at(dot_t(f_b3, apart), base, half)
    out_b3 = dot_n(s_a2, apart)
    out_ref[:, :half] = own_ref[:, :half] + pick(first, out_a, out_b3)
    out_ref[:, half : 2 * half] = own_ref[:, half:] + pick(first, out_a2, out_b)
    out_ref[:, 2 * half :] = pick(first, out_b + pltpu.roll(out_b3, quarter, 1), out_a + out_a2)


def local_kernel(pos_ref, annot_ref, chrom_ref, reach_ref, ids_ref, flag_ref, cross_ref, sub_ref, limit_ref, hot_ref):
    half = annot_ref.shape[1] // 4
    first = pos_ref[0] == 0
    base = pos_ref[2]
    flags = annot_ref[...].astype(F32)

    def quarters(x):
        return [x[:, k * half : (k + 1) * half] for k in range(4)]

    def local(x):
        one, two, three, four = quarters(x)
        return pick(first, one, three), pick(first, two, four), pick(first, three, two)

    left, right, there = local(flags)
    for k, x in enumerate((left, right, there)):
        flag_ref[:, k * half : (k + 1) * half] = x.astype(BF16)
    a_cols, b_cols, a2_cols = pick(first, left, there), pick(first, there, right), pick(first, right, there)
    b3_cols = pick(first, pltpu.roll(there, half // 2, 1), left)
    for k, x in enumerate((a_cols, b_cols, pltpu.roll(a_cols, half // 2, 1), b3_cols)):
        cross_ref[:, k * half : (k + 1) * half] = x.astype(BF16)
    back = lax.rem(half - base, half)
    late = lax.rem(half + half // 2 - base, half)
    for k, (x, turn) in enumerate(((left, back), (right, back), (a_cols, back), (a2_cols, back), (b_cols, late))):
        sub_ref[:, k * 128 : (k + 1) * 128] = pltpu.roll(x, turn, 1)[:, :128].astype(BF16)

    def line(ref):
        return jnp.concatenate([ref[k : k + 1, :] for k in range(ref.shape[0])], axis=1).astype(F32)

    chrom, reach = line(chrom_ref), line(reach_ref)
    ends = [jnp.sum((chrom <= k).astype(F32), axis=1, keepdims=True) for k in (1, 2, 3)]
    last = jnp.where(chrom == 1, ends[0], jnp.where(chrom == 2, ends[1], ends[2]))
    place = lax.broadcasted_iota(jnp.int32, chrom.shape, 1).astype(F32)
    limit = jnp.concatenate(local(jnp.minimum(reach, last - 1.0 - place)), axis=1)
    limit_ref[...] = jnp.broadcast_to(limit, limit_ref.shape)
    block = jnp.concatenate(local(line(ids_ref)), axis=1)
    number = lax.broadcasted_iota(jnp.int32, hot_ref.shape, 0).astype(F32)
    hot_ref[...] = jnp.where(number == block, 1.0, 0.0).astype(BF16)


def block_kernel(pos_ref, score_ref, flag_ref, hot_ref, sum_ref):
    slab = flag_ref.shape[1] // 3 * 2
    hot = hot_ref[...]
    own = score_ref[:, :slab] + flag_ref[:, :slab].astype(F32)
    scores = jnp.concatenate([own, score_ref[:, slab:]], axis=1)
    high = scores.astype(BF16)
    left = (scores - high.astype(F32)).astype(BF16)
    gap = jnp.zeros((128 - scores.shape[0], scores.shape[1]), BF16)
    both = dot_t(hot, jnp.concatenate([high, gap, left, gap], axis=0))
    sum_ref[...] = (both[:, :128] + both[:, 128:])[:, : sum_ref.shape[1]]


def call(kernel, inputs, outputs, scratch, flops, moved):
    vmem = pl.BlockSpec(memory_space=pltpu.VMEM)
    smem = pl.BlockSpec(memory_space=pltpu.SMEM)
    return pl.pallas_call(
        kernel,
        out_shape=outputs,
        in_specs=[smem] + [vmem] * (len(inputs) - 1),
        out_specs=jax.tree.map(lambda _: vmem, outputs),
        scratch_shapes=scratch,
        compiler_params=pltpu.CompilerParams(vmem_limit_bytes=VMEM_LIMIT),
        cost_estimate=pl.CostEstimate(flops=flops, bytes_accessed=moved, transcendentals=0),
    )(*inputs)


def body(genotypes, chromosome, blocks, annotation, reach):
    count, slab = genotypes.shape
    half = slab // 2
    quarter = half // 2
    width = 3 * half
    snps = chromosome.shape[0]
    parts = lax.axis_size("samples")
    bits = parts.bit_length() - 1
    core = lax.axis_index("genome")
    place = lax.axis_index("samples")
    order = [first + list(range(3, bits)) for first in ORDERS]
    bit_at = [(place >> jnp.where(core == 0, order[0][t], order[1][t])) & 1 for t in range(bits)]

    def exchange(x, t, order=order):
        route = []
        for s in range(parts):
            for g in range(2):
                route.append((s * 2 + g, (s ^ (1 << order[g][t])) * 2 + g))
        return lax.ppermute(x, ("samples", "genome"), route)

    def across(x):
        return lax.ppermute(x, "genome", [(0, 1), (1, 0)])

    def shape(rows, cols, dtype):
        return jax.ShapeDtypeStruct((rows, cols), dtype)

    base = bit_at[0] * quarter + bit_at[1] * (quarter // 2)
    rows = quarter // 2

    where = jnp.stack([core, place, base] + bit_at).astype(jnp.int32)
    annot = annotation.shape[0]

    hot_rows = -(-NBLK // 8) * 8

    def tiles(x):
        return x.reshape(-1, 128)

    flags, flags_cross, subs, limit, hot = call(
        local_kernel,
        (where, annotation, tiles(chromosome), tiles(reach), tiles(blocks)),
        (
            shape(annot, width, BF16),
            shape(annot, 4 * half, BF16),
            shape(annot, 5 * 128, BF16),
            shape(8, width, F32),
            shape(hot_rows, width, BF16),
        ),
        [],
        annot * snps * 10,
        annot * snps * 8,
    )
    def table_of(vectors, count):
        return pltpu.VMEM((vectors, -(-count // 128) * 128, 128), F32)

    def outputs(kept, sent, cols, many, exact):
        kept_shape = (shape(kept, cols, F32),) if kept else ()
        coded_shape = shape(sent + coded_rows(many, exact), cols, BF16)
        return kept_shape + (coded_shape, shape(list_rows(many) + 8, cols, F32))

    keep_a, send_a, stats_a, turned, piece = call(
        own_gram_kernel,
        (where, genotypes),
        outputs(quarter, quarter, slab, 1, 1)
        + (shape(slab, count, BF16), shape(count, half, BF16)),
        [pltpu.VMEM((half, slab), F32), table_of(2, half)],
        2 * count * half * half * 3,
        count * slab * 2,
    )
    there = across(piece)
    msg_a = exchange(send_a, 0)
    keep_b, send_b, stats_b = call(
        cross_gram_kernel,
        (where, turned, there, stats_a),
        outputs(quarter, quarter, half, 1, 2),
        [pltpu.VMEM((half, slab), F32), table_of(3, half), pltpu.VMEM((half, count), BF16)],
        2 * count * half * half * 3,
        count * slab * 2,
    )
    msg_b = exchange(send_b, 0)

    def merge(keep, msg, stats, cols, t, exact, *after):
        split = t == 1
        *kept, send, stats = call(
            functools.partial(merge_kernel, rows_in=quarter if split else rows, bits=(2 + t, 3 + t), many=1 << (t - 1), exact=exact, split=split),
            (where, keep, msg, stats) + after,
            outputs(rows if split else 0, rows, cols, 1 << t, exact),
            [],
            rows * cols * 8,
            rows * cols * 20,
        )
        return (kept[0] if split else send), send, stats

    for t in range(1, bits):
        if t == 1:
            msg_a, send_b = lax.optimization_barrier((msg_a, send_b))
        keep_a, send_a, stats_a = merge(keep_a, msg_a, stats_a, slab, t, 1)
        msg_a = exchange(send_a, t)
        keep_b, send_b, stats_b = merge(keep_b, msg_b, stats_b, half, t, 2, stats_a)
        msg_b = exchange(send_b, t)
    last = {"bit": 2 + bits, "many": parts // 2, "samples": float(count)}
    scores_a, vectors = call(
        functools.partial(own_score_kernel, **last),
        (where, keep_a, msg_a, stats_a, limit, flags, subs),
        (shape(annot, slab, F32), shape(list_rows(parts) + 8, slab, F32)),
        [table_of(3, rows)] + [pltpu.VMEM((rows, half), BF16)] * 2,
        2 * annot * half * rows * 8,
        rows * slab * 20,
    )
    partial = call(
        functools.partial(cross_score_kernel, **last),
        (where, keep_b, msg_b, stats_b, vectors, limit, flags_cross, subs, scores_a),
        shape(annot, width, F32),
        [table_of(5, rows)] + [pltpu.VMEM((rows, half), BF16)],
        2 * annot * half * rows * 8,
        rows * slab * 20,
    )
    cut = -(-width // 256) * 128
    pieces = [partial[:, :cut], partial[:, cut:]]
    for t in range(2):
        rounded = [x.astype(jnp.float16) for x in pieces]
        pieces = [x.astype(F32) + exchange(x, t, ROUNDS).astype(F32) for x in rounded]
    partial = jnp.concatenate(pieces, axis=1)
    arrived = across(partial[:, slab:])
    sums = call(
        block_kernel,
        (where, partial, flags, hot),
        shape(hot_rows, annot, F32),
        [],
        2 * annot * width * hot_rows * 2,
        annot * width * 8,
    )
    nothing = jnp.zeros_like(arrived)
    ld_scores = (partial[:, :slab] + flags[:, :slab].astype(F32)) + jnp.where(
        core == 0,
        jnp.concatenate([nothing, arrived], axis=1),
        jnp.concatenate([arrived, nothing], axis=1),
    )
    sums = sums.astype(jnp.float16)
    sums, sums_there = sums.astype(F32), across(sums).astype(F32)
    sums, ld_scores = lax.optimization_barrier((sums, ld_scores))
    return (ld_scores, (sums + sums_there)[:NBLK].T)


def solution(mesh):
    placed = (
        P(("groups", "samples"), "genome"),
        P("groups"),
        P("groups"),
        P(None, "groups"),
        P("groups"),
    )
    return jax.shard_map(
        body,
        mesh=mesh,
        in_specs=placed,
        out_specs=(P(None, ("groups", "genome")), P(None, "groups")),
        check_vma=False,
    )
```

```python
import functools
import math

import jax
import jax.numpy as jnp
from jax import lax
from jax.experimental import pallas as pl
from jax.experimental.pallas import tpu as pltpu
from jax.sharding import PartitionSpec as P

NBLK = 200
VAR_EPS = 1e-06
F32 = jnp.float32
BF16 = jnp.bfloat16
ORDERS = [[0, 1, 2], [1, 2, 0]]
ROUNDS = [[0, 1], [1, 2]]
VMEM_LIMIT = 20 * 1024 * 1024


STEP = 48


def pick(first, one, other):
    return jnp.where(first, one, other)


def index_parts(start, count, half):
    row = lax.broadcasted_iota(jnp.int32, (count, half), 0) + start
    col = lax.broadcasted_iota(jnp.int32, (count, half), 1)
    return row, col


def column_table(vectors, start, ref):
    table = eight(*vectors)
    half = table.shape[1]
    if start is not None:
        table = pltpu.roll(table, lax.rem(half - start, half), 1)
    for n in range(len(vectors)):
        for k in range(ref.shape[1] // 128):
            here = slice(k * 128, (k + 1) * 128)
            ref[n, here, :] = jnp.broadcast_to(table[n : n + 1, here], (128, 128)).T


def table_rows(ref, offset, columns, half):
    here = pl.ds(pl.multiple_of(offset, 16), STEP)
    return tuple(jnp.concatenate([ref[n, here, :]] * (half // 128), axis=1) for n in columns)


def high_low(values):
    high = values.astype(BF16)
    return high, (values - high.astype(F32)).astype(BF16)


def coded(sums, exact):
    high, low = high_low(sums)
    first, left = high_low(exact)
    third = (exact - first.astype(F32) - left.astype(F32)).astype(BF16)
    rows = coded_rows(sums.shape[0], exact.shape[0])
    gap = rows - 2 * sums.shape[0] - 3 * exact.shape[0]
    blank = [jnp.zeros((gap, sums.shape[1]), BF16)] if gap else []
    return jnp.concatenate([high, low, first, left, third] + blank, axis=0)


def coded_rows(many, exact):
    return -(-(2 * many + 3 * exact) // (24 * exact - 16)) * (24 * exact - 16)


def decoded(rows, many, exact):
    parts = rows.astype(F32)
    sums = parts[:many] + parts[many : 2 * many]
    at = 2 * many
    return sums, parts[at : at + exact] + parts[at + exact : at + 2 * exact] + parts[at + 2 * exact : at + 3 * exact]


def list_rows(many):
    return -(-many // 8) * 8


def put_stats(ref, sums, exact):
    many, width = sums.shape
    gap = list_rows(many) - many
    rows = [sums] + ([jnp.zeros((gap, width), F32)] if gap else [])
    rows = rows + [exact, jnp.zeros((8 - exact.shape[0], width), F32)]
    ref[...] = jnp.concatenate(rows, axis=0)


def merged(bit, msg_ref, stats_ref, rows, many, exact):
    theirs, added = decoded(msg_ref[rows:, :], many, exact)
    mine = stats_ref[:many, :]
    place = list_rows(many)
    both = pick(
        bit == 0, jnp.concatenate([mine, theirs], axis=0), jnp.concatenate([theirs, mine], axis=0)
    )
    return both, stats_ref[place : place + exact, :] + added


def two_parts(values):
    high, low = high_low(values)
    return high.astype(F32) + low.astype(F32)


def own_cols(vec, half):
    return vec[:, :half], vec[:, half : 2 * half]


def own_products(rows, cols, row, col):
    (l_rows, r_rows), (left, right) = rows, cols
    return l_rows * right, jnp.where(row < col, l_rows * left, r_rows * right)


def cross_halves(vec, first, half):
    left, right, there = vec[:, :half], vec[:, half : 2 * half], vec[:, 2 * half :]
    return pick(first, left, there), pick(first, there, right)


def cross_cols(vec, first, half):
    vec = jnp.broadcast_to(vec, (8, vec.shape[1]))
    a_cols, b_cols = cross_halves(vec, first, half)
    a_turned = pltpu.roll(a_cols, half // 2, 1)
    b3_cols = pick(first, pltpu.roll(vec[:, 2 * half :], half // 2, 1), vec[:, :half])
    return b_cols[:1], a_turned[:1], b3_cols[:1]


def cross_vectors(vec, first, half):
    a_cols, b_cols = cross_halves(vec, first, half)
    a2_cols = pick(first, vec[:, half : 2 * half], vec[:, 2 * half :])
    b_late = pltpu.roll(jnp.broadcast_to(b_cols, (8, half)), half // 2, 1)[:1]
    return a_cols, a2_cols, b_late


def cross_products(rows, cols, row, col):
    (a_rows, a2_rows, b_rows), (c_b, c_a, c_b3) = rows, cols
    half = row.shape[1]
    return jnp.where(
        col < half // 2, jnp.where(row > col, a_rows * c_b, b_rows * c_a), a2_rows * c_b3
    )


def dot_n(left, right):
    return lax.dot_general(left, right, (((1,), (0,)), ((), ())), preferred_element_type=F32)


def dot_t(left, right):
    return lax.dot_general(left, right, (((1,), (1,)), ((), ())), preferred_element_type=F32)


def squared_sums(ref, start, stop):
    width = ref.shape[1]
    total = jnp.zeros((8, width), F32)
    for k in range(start, stop, 64):
        part = ref[k : k + 64, :].astype(F32)
        total = total + jnp.sum((part * part).reshape(8, 8, width), axis=0)
    return total


def moments(ref, total):
    count = ref.shape[0]
    sums = dot_n(jnp.ones((8, count), BF16), ref[...])[:1]
    shift = sums * (1.0 / math.sqrt(count))
    return sums, jnp.sum(total, axis=0, keepdims=True) - shift * shift, shift


def eight(*rows):
    return jnp.concatenate(list(rows) + [rows[-1]] * (8 - len(rows)), axis=0)


def halved(bit, keep_ref, send_ref, value):
    part = keep_ref.shape[0]
    for k in range(0, part, STEP):
        send_ref[k : k + STEP, :] = value(pl.multiple_of((1 - bit) * part + k, 16)).astype(BF16)
        keep_ref[k : k + STEP, :] = value(pl.multiple_of(bit * part + k, 16))


def own_gram_kernel(pos_ref, own_ref, keep_ref, send_ref, stats_ref, turned_ref, piece_ref, full_ref, col_ref):
    count, slab = own_ref.shape
    half = slab // 2

    @pl.when(pos_ref[0] == 0)
    def _():
        piece_ref[...] = own_ref[:, half:]

    @pl.when(pos_ref[0] != 0)
    def _():
        piece_ref[...] = own_ref[:, :half]

    turned_ref[...] = own_ref[...].T
    sums, squares, shift = moments(own_ref, squared_sums(own_ref, 0, count))
    sums = two_parts(sums)
    put_stats(stats_ref, sums, jnp.concatenate([squares, shift], axis=0))
    column_table(own_cols(shift, half), None, col_ref)
    left, right = turned_ref[:half, :], turned_ref[half:, :]
    full_ref[:, :half] = dot_n(left, own_ref[:, half:])
    row, col = index_parts(0, half, half)
    full_ref[:, half:] = jnp.where(row < col, dot_n(left, own_ref[:, :half]), dot_n(right, own_ref[:, half:]))
    cols = own_cols(shift, half)

    def value(start):
        rows = table_rows(col_ref, start, (0, 1), half)
        products = own_products(rows, cols, *index_parts(start, STEP, half))
        return full_ref[pl.ds(start, STEP), :] - jnp.concatenate(products, axis=1)

    halved(pos_ref[3], keep_ref, send_ref, value)
    send_ref[keep_ref.shape[0] :, :] = coded(sums, squares)


def cross_gram_kernel(pos_ref, turned_ref, there_ref, own_stats_ref, keep_ref, send_ref, stats_ref, full_ref, col_ref, side_ref):
    half = there_ref.shape[1]
    quarter = half // 2
    core = pos_ref[0]
    first = core == 0
    row, col = index_parts(0, half, half)

    @pl.when(first)
    def _():
        full_ref[:, :half] = dot_n(turned_ref[:half, :], there_ref[...])
        full_ref[:, half:] = pltpu.roll(dot_n(turned_ref[half:, :], there_ref[...]), quarter, 1)

    @pl.when(jnp.logical_not(first))
    def _():
        side_ref[...] = there_ref[...].T
        full_ref[:, :half] = dot_t(side_ref[...], turned_ref[half:, :])
        full_ref[:, half:] = dot_t(side_ref[...], turned_ref[:half, :])

    sums, squares, shift = moments(there_ref, squared_sums(there_ref, 0, there_ref.shape[0]))
    shift = jnp.concatenate([own_stats_ref[list_rows(1) + 1 : list_rows(1) + 2, :], shift], axis=1)
    column_table(cross_vectors(shift, first, half), None, col_ref)
    a_shift, b_shift = cross_halves(shift, first, half)
    straight = full_ref[:, :half]
    level = jnp.sum(jnp.where(row == col, straight, 0.0), axis=0, keepdims=True) - a_shift * b_shift
    sums = two_parts(sums)
    exact = jnp.concatenate([squares, level], axis=0)
    put_stats(stats_ref, sums, exact)
    send_ref[keep_ref.shape[0] :, :] = coded(sums, exact)
    corner = full_ref[half - 256 : half, half - 256 : half].T[256 - quarter :, :]
    corner = pltpu.roll(corner, quarter, 1)[:, :quarter]
    corner = jnp.concatenate([corner, corner], axis=0)
    folded = jnp.concatenate([corner, jnp.zeros((half, half - quarter), F32)], axis=1)
    apart = full_ref[:, half:]
    full_ref[:, :half] = jnp.where(col < quarter, jnp.where(row > col, straight, folded), apart)
    cols = cross_cols(shift, first, half)

    def value(start):
        rows = table_rows(col_ref, start, (0, 1, 2), half)
        products = cross_products(rows, cols, *index_parts(start, STEP, half))
        return full_ref[pl.ds(start, STEP), :half] - products

    halved(pos_ref[3], keep_ref, send_ref, value)


def merge_kernel(pos_ref, kept_ref, msg_ref, stats_ref, *refs, rows_in, bits, many, exact, split):
    keep_ref = refs[-3] if split else None
    send_ref, out_ref = refs[-2:]
    rows = rows_in

    def value(offset):
        here = pl.ds(offset, STEP)
        return kept_ref[here, :].astype(F32) + msg_ref[here, :].astype(F32)

    if split:
        halved(pos_ref[bits[1]], keep_ref, send_ref, value)
        done = keep_ref.shape[0]
    else:
        done = rows
        for k in range(0, rows, STEP):
            send_ref[k : k + STEP, :] = value(k).astype(BF16)
    sums, more = merged(pos_ref[bits[0]], msg_ref, stats_ref, rows, many, exact)
    put_stats(out_ref, sums, more)
    send_ref[done:, :] = coded(sums, more)


def deviations(sums, samples):
    mean = jnp.sum(sums, axis=0, keepdims=True) * (1.0 / sums.shape[0])
    return (sums - mean) * (1.0 / math.sqrt(samples))


def outer_sums(left, right):
    (l_high, l_low), (r_high, r_low) = high_low(left), high_low(right)
    left = jnp.concatenate([l_high, l_high, l_low], axis=0)
    right = jnp.concatenate([r_high, r_low, r_high], axis=0)
    return lax.dot_general(left, right, (((0,), (0,)), ((), ())), preferred_element_type=F32)


def from_row(vec, start):
    half = vec.shape[1]
    return pltpu.roll(vec, lax.rem(half - start, half), 1)[:, :128]


def unbiased(correl, everyone):
    squared = correl * correl
    return squared - (1.0 - squared) * (1.0 / (everyone - 2.0))


def placed_at(rows_part, offset, half):
    blank = jnp.zeros((rows_part.shape[0], half - rows_part.shape[1]), F32)
    return pltpu.roll(jnp.concatenate([rows_part, blank], axis=1), offset, 1)


def own_score_kernel(
    pos_ref, kept_ref, msg_ref, stats_ref, limit_ref, flag_ref, sub_ref,
    out_ref, vec_ref, col_ref, one_ref, two_ref, *, bit, many, samples,
):
    rows = one_ref.shape[0]
    half = kept_ref.shape[1] // 2
    everyone = 2.0 * many * samples
    base = pos_ref[2]
    sums, squares = merged(pos_ref[bit], msg_ref, stats_ref, rows, many, 1)
    apart = deviations(sums, samples)
    squares = squares + jnp.sum(apart * apart, axis=0, keepdims=True)
    scale = 1.0 / jnp.sqrt(squares * (1.0 / everyone) + VAR_EPS)
    put_stats(vec_ref, apart, scale)
    scales = own_cols(scale, half)
    factors = own_cols(scale * (1.0 / everyone), half) + (limit_ref[:1, :half],)
    column_table(factors, base, col_ref)
    left, right = own_cols(apart, half)
    l_rows = from_row(left, base)
    products = outer_sums(l_rows, right), outer_sums(l_rows, left), outer_sums(from_row(right, base), right)
    right_lim = limit_ref[:1, half : 2 * half]
    for k in range(0, rows, STEP):
        start = base + k
        row, col = index_parts(start, STEP, half)
        l_scale, r_scale, left_lim = table_rows(col_ref, k, range(3), half)
        one, upper, lower = (x[k : k + STEP] for x in products)
        shifts = one, jnp.where(row < col, upper, lower)
        norms = own_products((l_scale, r_scale), scales, row, col)
        gaps = (half + col - row, jnp.where(row == col, 8 * half, jnp.abs(row - col)))
        lims = (left_lim, jnp.where(row < col, left_lim, right_lim))
        for s, ref in ((0, one_ref), (1, two_ref)):
            here = slice(s * half, (s + 1) * half)
            value = kept_ref[k : k + STEP, here].astype(F32) + msg_ref[k : k + STEP, here].astype(F32)
            weight = unbiased((value + shifts[s]) * norms[s], everyone)
            ref[k : k + STEP, :] = jnp.where(gaps[s].astype(F32) <= lims[s], weight, 0.0).astype(BF16)
    row, col = index_parts(base, rows, half)
    one, two = one_ref[...], two_ref[...]
    zero = jnp.zeros_like(two)
    upper, lower = jnp.where(row < col, two, zero), jnp.where(row > col, two, zero)
    f_left, f_right = flag_ref[:, :half], flag_ref[:, half : 2 * half]
    s_left, s_right = sub_ref[:, :rows], sub_ref[:, 128 : 128 + rows]
    out_ref[:, :half] = dot_n(s_left, upper) + placed_at(dot_t(f_right, one) + dot_t(f_left, upper), base, half)
    out_ref[:, half:] = dot_n(s_left, one) + dot_n(s_right, lower) + placed_at(dot_t(f_right, lower), base, half)


def cross_score_kernel(
    pos_ref, kept_ref, msg_ref, stats_ref, vec_ref, limit_ref, flag_ref, sub_ref, own_ref,
    out_ref, col_ref, three_ref, *, bit, many, samples,
):
    rows = three_ref.shape[0]
    half = kept_ref.shape[1]
    quarter = half // 2
    core = pos_ref[0]
    first = core == 0
    everyone = 2.0 * many * samples
    base = pos_ref[2]
    sums, exact = merged(pos_ref[bit], msg_ref, stats_ref, rows, many, 2)
    apart = deviations(sums, samples)
    squares = exact[:1] + jnp.sum(apart * apart, axis=0, keepdims=True)
    place = list_rows(2 * many)
    apart = jnp.concatenate([vec_ref[: 2 * many, :], apart], axis=1)
    a_apart, b_apart = cross_halves(apart, first, half)
    level = exact[1:2] + jnp.sum(a_apart * b_apart, axis=0, keepdims=True)
    scale = 1.0 / jnp.sqrt(squares * (1.0 / everyone) + VAR_EPS)
    scale = jnp.concatenate([vec_ref[place : place + 1, :], scale], axis=1)
    limit = limit_ref[:1, :]
    factors = cross_vectors(scale * (1.0 / everyone), first, half)
    column_table(factors + cross_vectors(limit, first, half)[:2], base, col_ref)
    scales = cross_cols(scale, first, half)
    there = apart[:, 2 * half :]
    a2_apart = pick(first, apart[:, half : 2 * half], there)
    b3_apart = pick(first, pltpu.roll(there, quarter, 1), apart[:, :half])
    late_a, late_b = pltpu.roll(a_apart, quarter, 1), pltpu.roll(b_apart, quarter, 1)
    shifts = (
        outer_sums(from_row(a_apart, base), b_apart),
        outer_sums(from_row(late_b, base), late_a),
        outer_sums(from_row(a2_apart, base), b3_apart),
    )
    _, late_lim, _ = cross_cols(limit, first, half)
    for k in range(0, rows, STEP):
        start = base + k
        row, col = index_parts(start, STEP, half)
        fold = col < quarter
        parts = table_rows(col_ref, k, range(5), half)
        a_lim, a2_lim = parts[3:]
        straight, late, apart = (x[k : k + STEP] for x in shifts)
        products = jnp.where(fold, jnp.where(row > col, straight, late), apart)
        norms = cross_products(parts[:3], scales, row, col)
        lims = jnp.where(fold, jnp.where(row > col, a_lim, late_lim), a2_lim)
        near = jnp.where(row == col, 8 * half, 2 * half - jnp.abs(row - col))
        gaps = jnp.where(fold, near, quarter + quarter * core + col - row)
        value = kept_ref[k : k + STEP, :].astype(F32) + msg_ref[k : k + STEP, :].astype(F32)
        weight = unbiased((value + products) * norms, everyone)
        three_ref[k : k + STEP, :] = jnp.where(gaps.astype(F32) <= lims, weight, 0.0).astype(BF16)
    a_scale, b_scale = cross_halves(scale, first, half)
    a_limit, _ = cross_halves(limit, first, half)
    lane = lax.broadcasted_iota(jnp.int32, (1, half), 1)
    level = unbiased(level * (1.0 / everyone) * a_scale * b_scale, everyone)
    mine = (lane >= base) & (lane < base + rows) & (a_limit >= 2.0 * half)
    level = jnp.where(mine, level, 0.0)
    row, col = index_parts(base, rows, half)
    three = three_ref[...]
    zero = jnp.zeros_like(three)
    fold = col < quarter
    straight = jnp.where(fold & (row > col), three, zero)
    folded = jnp.where(fold & (row < col), three, zero)
    apart = jnp.where(fold, zero, three)
    f_a, f_b = flag_ref[:, :half], flag_ref[:, half : 2 * half]
    f_late, f_b3 = flag_ref[:, 2 * half : 3 * half], flag_ref[:, 3 * half :]
    s_a, s_a2, s_late = sub_ref[:, 256 : 256 + rows], sub_ref[:, 384 : 384 + rows], sub_ref[:, 512 : 512 + rows]
    out_a = placed_at(dot_t(f_b, straight), base, half) + pltpu.roll(dot_n(s_late, folded), quarter, 1)
    out_b = dot_n(s_a, straight) + placed_at(dot_t(f_late, folded), lax.rem(base + quarter, half), half)
    out_a = out_a + f_b.astype(F32) * level
    out_b = out_b + f_a.astype(F32) * level
    out_a2 = placed_at(dot_t(f_b3, apart), base, half)
    out_b3 = dot_n(s_a2, apart)
    out_ref[:, :half] = own_ref[:, :half] + pick(first, out_a, out_b3)
    out_ref[:, half : 2 * half] = own_ref[:, half:] + pick(first, out_a2, out_b)
    out_ref[:, 2 * half :] = pick(first, out_b + pltpu.roll(out_b3, quarter, 1), out_a + out_a2)


def local_kernel(pos_ref, annot_ref, chrom_ref, reach_ref, ids_ref, flag_ref, cross_ref, sub_ref, limit_ref, hot_ref):
    half = annot_ref.shape[1] // 4
    first = pos_ref[0] == 0
    base = pos_ref[2]
    flags = annot_ref[...].astype(F32)

    def quarters(x):
        return [x[:, k * half : (k + 1) * half] for k in range(4)]

    def local(x):
        one, two, three, four = quarters(x)
        return pick(first, one, three), pick(first, two, four), pick(first, three, two)

    left, right, there = local(flags)
    for k, x in enumerate((left, right, there)):
        flag_ref[:, k * half : (k + 1) * half] = x.astype(BF16)
    a_cols, b_cols, a2_cols = pick(first, left, there), pick(first, there, right), pick(first, right, there)
    b3_cols = pick(first, pltpu.roll(there, half // 2, 1), left)
    for k, x in enumerate((a_cols, b_cols, pltpu.roll(a_cols, half // 2, 1), b3_cols)):
        cross_ref[:, k * half : (k + 1) * half] = x.astype(BF16)
    back = lax.rem(half - base, half)
    late = lax.rem(half + half // 2 - base, half)
    for k, (x, turn) in enumerate(((left, back), (right, back), (a_cols, back), (a2_cols, back), (b_cols, late))):
        sub_ref[:, k * 128 : (k + 1) * 128] = pltpu.roll(x, turn, 1)[:, :128].astype(BF16)

    def line(ref):
        return jnp.concatenate([ref[k : k + 1, :] for k in range(ref.shape[0])], axis=1).astype(F32)

    chrom, reach = line(chrom_ref), line(reach_ref)
    ends = [jnp.sum((chrom <= k).astype(F32), axis=1, keepdims=True) for k in (1, 2, 3)]
    last = jnp.where(chrom == 1, ends[0], jnp.where(chrom == 2, ends[1], ends[2]))
    place = lax.broadcasted_iota(jnp.int32, chrom.shape, 1).astype(F32)
    limit = jnp.concatenate(local(jnp.minimum(reach, last - 1.0 - place)), axis=1)
    limit_ref[...] = jnp.broadcast_to(limit, limit_ref.shape)
    block = jnp.concatenate(local(line(ids_ref)), axis=1)
    number = lax.broadcasted_iota(jnp.int32, hot_ref.shape, 0).astype(F32)
    hot_ref[...] = jnp.where(number == block, 1.0, 0.0).astype(BF16)


def block_kernel(pos_ref, score_ref, flag_ref, hot_ref, sum_ref):
    slab = flag_ref.shape[1] // 3 * 2
    hot = hot_ref[...]
    own = score_ref[:, :slab] + flag_ref[:, :slab].astype(F32)
    scores = jnp.concatenate([own, score_ref[:, slab:]], axis=1)
    high = scores.astype(BF16)
    left = (scores - high.astype(F32)).astype(BF16)
    gap = jnp.zeros((128 - scores.shape[0], scores.shape[1]), BF16)
    both = dot_t(hot, jnp.concatenate([high, gap, left, gap], axis=0))
    sum_ref[...] = (both[:, :128] + both[:, 128:])[:, : sum_ref.shape[1]]


def call(kernel, inputs, outputs, scratch, flops, moved):
    vmem = pl.BlockSpec(memory_space=pltpu.VMEM)
    smem = pl.BlockSpec(memory_space=pltpu.SMEM)
    return pl.pallas_call(
        kernel,
        out_shape=outputs,
        in_specs=[smem] + [vmem] * (len(inputs) - 1),
        out_specs=jax.tree.map(lambda _: vmem, outputs),
        scratch_shapes=scratch,
        compiler_params=pltpu.CompilerParams(vmem_limit_bytes=VMEM_LIMIT),
        cost_estimate=pl.CostEstimate(flops=flops, bytes_accessed=moved, transcendentals=0),
    )(*inputs)


def body(genotypes, chromosome, blocks, annotation, reach):
    count, slab = genotypes.shape
    half = slab // 2
    quarter = half // 2
    width = 3 * half
    snps = chromosome.shape[0]
    parts = lax.axis_size("samples")
    bits = parts.bit_length() - 1
    core = lax.axis_index("genome")
    place = lax.axis_index("samples")
    order = [first + list(range(3, bits)) for first in ORDERS]
    bit_at = [(place >> jnp.where(core == 0, order[0][t], order[1][t])) & 1 for t in range(bits)]

    def exchange(x, t, order=order):
        route = []
        for s in range(parts):
            for g in range(2):
                route.append((s * 2 + g, (s ^ (1 << order[g][t])) * 2 + g))
        return lax.ppermute(x, ("samples", "genome"), route)

    def across(x):
        return lax.ppermute(x, "genome", [(0, 1), (1, 0)])

    def shape(rows, cols, dtype):
        return jax.ShapeDtypeStruct((rows, cols), dtype)

    base = bit_at[0] * quarter + bit_at[1] * (quarter // 2)
    rows = quarter // 2

    where = jnp.stack([core, place, base] + bit_at).astype(jnp.int32)
    annot = annotation.shape[0]

    hot_rows = -(-NBLK // 8) * 8

    def tiles(x):
        return x.reshape(-1, 128)

    flags, flags_cross, subs, limit, hot = call(
        local_kernel,
        (where, annotation, tiles(chromosome), tiles(reach), tiles(blocks)),
        (
            shape(annot, width, BF16),
            shape(annot, 4 * half, BF16),
            shape(annot, 5 * 128, BF16),
            shape(8, width, F32),
            shape(hot_rows, width, BF16),
        ),
        [],
        annot * snps * 10,
        annot * snps * 8,
    )
    def table_of(vectors, count):
        return pltpu.VMEM((vectors, -(-count // 128) * 128, 128), F32)

    def outputs(kept, sent, cols, many, exact):
        kept_shape = (shape(kept, cols, F32),) if kept else ()
        coded_shape = shape(sent + coded_rows(many, exact), cols, BF16)
        return kept_shape + (coded_shape, shape(list_rows(many) + 8, cols, F32))

    keep_a, send_a, stats_a, turned, piece = call(
        own_gram_kernel,
        (where, genotypes),
        outputs(quarter, quarter, slab, 1, 1)
        + (shape(slab, count, BF16), shape(count, half, BF16)),
        [pltpu.VMEM((half, slab), F32), table_of(2, half)],
        2 * count * half * half * 3,
        count * slab * 2,
    )
    there = across(piece)
    msg_a = exchange(send_a, 0)
    keep_b, send_b, stats_b = call(
        cross_gram_kernel,
        (where, turned, there, stats_a),
        outputs(quarter, quarter, half, 1, 2),
        [pltpu.VMEM((half, slab), F32), table_of(3, half), pltpu.VMEM((half, count), BF16)],
        2 * count * half * half * 3,
        count * slab * 2,
    )
    msg_b = exchange(send_b, 0)

    def merge(keep, msg, stats, cols, t, exact, *after):
        split = t == 1
        *kept, send, stats = call(
            functools.partial(merge_kernel, rows_in=quarter if split else rows, bits=(2 + t, 3 + t), many=1 << (t - 1), exact=exact, split=split),
            (where, keep, msg, stats) + after,
            outputs(rows if split else 0, rows, cols, 1 << t, exact),
            [],
            rows * cols * 8,
            rows * cols * 20,
        )
        return (kept[0] if split else send), send, stats

    for t in range(1, bits):
        if t == 1:
            msg_a, send_b = lax.optimization_barrier((msg_a, send_b))
        keep_a, send_a, stats_a = merge(keep_a, msg_a, stats_a, slab, t, 1)
        msg_a = exchange(send_a, t)
        keep_b, send_b, stats_b = merge(keep_b, msg_b, stats_b, half, t, 2, stats_a)
        msg_b = exchange(send_b, t)
    last = {"bit": 2 + bits, "many": parts // 2, "samples": float(count)}
    scores_a, vectors = call(
        functools.partial(own_score_kernel, **last),
        (where, keep_a, msg_a, stats_a, limit, flags, subs),
        (shape(annot, slab, F32), shape(list_rows(parts) + 8, slab, F32)),
        [table_of(3, rows)] + [pltpu.VMEM((rows, half), BF16)] * 2,
        2 * annot * half * rows * 8,
        rows * slab * 20,
    )
    partial = call(
        functools.partial(cross_score_kernel, **last),
        (where, keep_b, msg_b, stats_b, vectors, limit, flags_cross, subs, scores_a),
        shape(annot, width, F32),
        [table_of(5, rows)] + [pltpu.VMEM((rows, half), BF16)],
        2 * annot * half * rows * 8,
        rows * slab * 20,
    )
    cut = -(-width // 256) * 128
    pieces = [partial[:, cut:], partial[:, :cut]]
    for t in range(2):
        rounded = [x.astype(jnp.float16) for x in pieces]
        pieces = [x.astype(F32) + exchange(x, t, ROUNDS).astype(F32) for x in rounded]
    partial = jnp.concatenate(pieces[::-1], axis=1)
    arrived = across(partial[:, slab:])
    sums = call(
        block_kernel,
        (where, partial, flags, hot),
        shape(hot_rows, annot, F32),
        [],
        2 * annot * width * hot_rows * 2,
        annot * width * 8,
    )
    nothing = jnp.zeros_like(arrived)
    ld_scores = (partial[:, :slab] + flags[:, :slab].astype(F32)) + jnp.where(
        core == 0,
        jnp.concatenate([nothing, arrived], axis=1),
        jnp.concatenate([arrived, nothing], axis=1),
    )
    sums = sums.astype(jnp.float16)
    sums, sums_there = sums.astype(F32), across(sums).astype(F32)
    sums, ld_scores = lax.optimization_barrier((sums, ld_scores))
    return (ld_scores, (sums + sums_there)[:NBLK].T)


def solution(mesh):
    placed = (
        P(("groups", "samples"), "genome"),
        P("groups"),
        P("groups"),
        P(None, "groups"),
        P("groups"),
    )
    return jax.shard_map(
        body,
        mesh=mesh,
        in_specs=placed,
        out_specs=(P(None, ("groups", "genome")), P(None, "groups")),
        check_vma=False,
    )
```
